32 devices in a mesh: groups: 2 (over x), tx: 16 (over z, y, core).
Axes of the slice: x: 2, y: 2, z: 4, core: 2. Of those that a mesh axis runs over, the one named last changes fastest.
Arguments:
- masters: float32 [128, 1024], P(('groups', 'tx')), parts along dimension 0, may hold values from 0 to 1
- velocity: float32 [128, 1024], P(('groups', 'tx')), parts along dimension 0, may hold values from -4 to 4
- place_owner: int32 [4096, 1], P(('groups', 'tx')), parts along dimension 0, may hold values from 0 to 15; in each aligned block of 128 rows (0 to 127, 128 to 255, ...) at most 16 rows name the same one
- place_local: int32 [4096], P(('groups', 'tx')), parts along dimension 0, may hold values from 0 to 3
- place_row: int32 [4096], P(('groups', 'tx')), parts along dimension 0, may hold values from 0 to 32
- place_col: int32 [4096], P(('groups', 'tx')), parts along dimension 0, may hold values from 0 to 224
- row_taps: bfloat16 [12, 4, 2, 63], replicated, may hold values from -0.75 to 0.75
- col_taps: bfloat16 [12, 4, 2, 63], replicated, may hold values from -0.25 to 0.25
- mode_weights: float32 [12], replicated, may hold values from 0.02 to 0.2
- target: bfloat16 [2048, 256], P(('groups', 'tx')), parts along dimension 0, may hold values from 0 to 1
Outputs:
- resist_residual: float32 [2048, 256], P(('groups', 'tx')), parts along dimension 0
- velocity_new: float32 [128, 1024], P(('groups', 'tx')), parts along dimension 0
- masters_new: float32 [128, 1024], P(('groups', 'tx')), parts along dimension 0
The draws below stay inside these ranges and needn't reach their ends.
There are 2 independent parts, one for each index of `groups`. The reference program is written for one: setup_inputs(seed, part) draws one part's arguments, and reference() takes and returns one part's arrays. A program takes and returns all parts, laid end to end along the dimension named above; an argument that names none is the same for every part. Nothing has to cross between parts.
Inputs may be any that keep to these rules, and one draw needn't show every extreme that they name: `place_owner`: among the placements of one device (aligned blocks of 128), at most 16 name any one owner, a bound that some block reaches.
All inputs are finite; a program needn't handle non-finite values.
Results may differ from the reference program's by a relative error of at most 0.0012.
Values may be sent and summed in bfloat16 or wider, within the bound.
No kernel may reach another device: no remote copies, remote signals or barrier semaphores. Data moves between devices by JAX's collectives and lax.ppermute only.
A program may use at most 192 MiB of HBM per device.

```python
import math
import jax
import jax.numpy as jnp
import numpy as np
from jax import lax

W = 256
ROW_DEV = 64
MS = 32
TAPS = 63
HALF = 31
TERMS = 4
MODES = 12
M_DEV = 4
PLC = 128
CAP = 16
NM = 64
ROWS = 1024
PLACES = 2048
N_TX = 16


def with_ends(values, stream_key, least, high):
    shape = values.shape
    index_at = [jax.random.randint(jax.random.fold_in(stream_key, axis), (), 0, shape[axis]) for axis in range(len(shape))]
    values = values.at[tuple(index_at)].set(least)
    longest = shape.index(max(shape))
    index_at[longest] = (index_at[longest] + 1) % shape[longest]
    return values.at[tuple(index_at)].set(high)


def shard_levels(own_key, extent, cuts, smallest, largest):
    def one(axis_at, parts):
        draws = jax.random.uniform(jax.random.fold_in(jax.random.fold_in(own_key, 6), axis_at), (parts,), jnp.float32, smallest / len(cuts), largest / len(cuts))
        return jnp.repeat(jnp.exp(draws), extent[axis_at] // parts).reshape((-1,) + (1,) * (len(extent) - axis_at - 1))

    level = one(*cuts[0])
    for cut in cuts[1:]:
        level = level * one(*cut)
    return level


def routed_block(key, own, number, rows, amount, top, most, lean):
    sequence = jax.random.permutation(key, amount)
    packed, common = load_shares(amount, rows * top, most, lean, True), load_shares(amount, rows * top, most, lean, False)
    places = jnp.arange(amount)

    def named(lengths, rotation):
        used = int((lengths > 0).sum())
        fixed = max(1, used // 4)
        shifted = fixed + (places - fixed + rotation * (used - fixed)) % max(1, amount - fixed)
        return jnp.zeros((amount,), jnp.int32).at[sequence[jnp.where(places < fixed, places, shifted)]].set(jnp.asarray(lengths, jnp.int32))

    lengths = jnp.where(number % 4 == 0, named(packed, number // 4), named(common, number - number // 4 - 1))
    mixed = jax.random.permutation(jax.random.fold_in(own, 3), amount)
    giver, taker = mixed[0:amount // 2 * 2:2], mixed[1:amount // 2 * 2:2]
    margin = jnp.minimum(lengths[giver] - 1, most - lengths[taker]) // 2
    margin = jnp.where((giver == sequence[0]) | (taker == sequence[0]) | (lengths[taker] == 0), 0, jnp.maximum(margin, 0))
    shifted = jax.random.randint(jax.random.fold_in(own, 4), (amount // 2,), 0, 1 << 20) % (margin + 1)
    lengths = lengths.at[giver].add(-shifted).at[taker].add(shifted)
    items = jnp.searchsorted(jnp.cumsum(lengths), jnp.arange(rows * top), side="right").astype(jnp.int32)
    table = items.reshape(top, rows).T
    table = table[jax.random.permutation(jax.random.fold_in(own, 1), rows)]
    rotation = jax.random.randint(jax.random.fold_in(own, 2), (rows, 1), 0, top)
    return jnp.take_along_axis(table, (jnp.arange(top)[None, :] + rotation) % top, axis=1)


def load_shares(count, total, limit, skew, full):
    portions = [(1 << 20) // math.isqrt(rank ** skew) + 1 for rank in range(1, count + 1)]
    largest = limit if full else min(limit, max(-(-total // count), total * portions[0] // sum(portions)))
    least = 1 if total - largest >= count - 1 else 0
    counts, spare = [largest] + [least] * (count - 1), total - largest - least * (count - 1)
    while spare > 0:
        free = [i for i in range(1, count) if counts[i] < largest] or [i for i in range(1, count) if counts[i] < limit]
        mass, budget = sum([portions[i] for i in free]), spare
        for i in free:
            more = min(limit - counts[i], max(1, budget * portions[i] // mass), spare)
            counts[i] = counts[i] + more
            spare = spare - more
    return np.array(counts)


def gaussian(key, shape, spread, limit, split=(), kind=jnp.bfloat16):
    gain = shard_levels(key, shape, split, -0.22, 0.18) if split else 1.0
    result = jax.random.normal(key, shape, jnp.float32) * spread * gain
    return jnp.minimum(jnp.maximum(result, -limit), limit).astype(kind)


def setup_inputs(seed: int = 0, part: int = 0) -> dict:
    splits = jax.random.split(jax.random.key(seed), 11)
    part_splits = jax.random.split(jax.random.fold_in(splits[10], part), 11)
    masters = jnp.clip(1.0 * jax.random.uniform(part_splits[0], (NM, MS * MS), jnp.float32) ** shard_levels(part_splits[0], (NM, MS * MS), ((0, 16),), -0.2, 0.2), 0.0, 1.0)
    velocity = gaussian(part_splits[1], (NM, MS * MS), 0.5, 4.0, ((0, 16),), jnp.float32)
    place_owner_keys = jax.random.split(jax.random.fold_in(part_splits[2], 1), PLACES // PLC)
    place_owner_turns = jax.random.permutation(jax.random.fold_in(part_splits[2], 3), PLACES // PLC)
    place_owner = jax.vmap(lambda own, number: routed_block(jax.random.fold_in(part_splits[2], 2), own, number, PLC, N_TX, 1, CAP, 2))(place_owner_keys, place_owner_turns).reshape((PLACES, 1))
    place_local = with_ends(jax.random.randint(part_splits[3], (PLACES,), 0, M_DEV), jax.random.fold_in(part_splits[3], 1), 0, M_DEV - 1).astype(jnp.int32)
    place_row = with_ends(jax.random.randint(part_splits[4], (PLACES,), 0, ROW_DEV - MS + 1), jax.random.fold_in(part_splits[4], 1), 0, ROW_DEV - MS).astype(jnp.int32)
    place_col = with_ends(jax.random.randint(part_splits[5], (PLACES,), 0, W - MS + 1), jax.random.fold_in(part_splits[5], 1), 0, W - MS).astype(jnp.int32)
    row_taps = gaussian(splits[6], (MODES, TERMS, 2, TAPS), TAPS ** -0.5, 0.75)
    col_taps = gaussian(splits[7], (MODES, TERMS, 2, TAPS), (2 * TERMS * TAPS) ** -0.5, 0.25)
    mode_weights = jnp.clip(jnp.exp(jax.random.uniform(splits[8], (MODES,), jnp.float32, math.log(0.02), math.log(0.2))), 0.02, 0.2)
    target = jnp.clip(1.0 * jax.random.uniform(part_splits[9], (ROWS, W), jnp.float32) ** shard_levels(part_splits[9], (ROWS, W), ((0, 16),), -0.2, 0.2), 0.0, 1.0).astype(jnp.bfloat16)
    return dict(masters=masters, velocity=velocity, place_owner=place_owner, place_local=place_local, place_row=place_row, place_col=place_col, row_taps=row_taps, col_taps=col_taps, mode_weights=mode_weights, target=target)


steepness = 0.5
threshold = 8.0
momentum = 0.9
step_size = 0.05


def correlate(inputs, kernel, pad_rows, pad_cols):
    return lax.conv_general_dilated(inputs, kernel, (1, 1), ((pad_rows, pad_rows), (pad_cols, pad_cols)), precision=lax.Precision.HIGHEST)


def column_kernel(col_mode):
    real_part = col_mode[:, 0].astype(jnp.float32)
    imag_part = col_mode[:, 1].astype(jnp.float32)
    to_real = jnp.stack([real_part, -imag_part], 1).reshape(2 * TERMS, TAPS)
    to_imag = jnp.stack([imag_part, real_part], 1).reshape(2 * TERMS, TAPS)
    return jnp.stack([to_real, to_imag])[:, :, None, :]


def reference(masters, velocity, place_owner, place_local, place_row, place_col, row_taps, col_taps, mode_weights, target):
    total = place_local.shape[0]
    master_id = (place_owner[:, 0] * M_DEV + place_local).astype(jnp.int32)
    master_half = masters.astype(jnp.bfloat16)
    block_index = jnp.arange(total, dtype=jnp.int32) // PLC
    first_row = (block_index * ROW_DEV + place_row).astype(jnp.int32)
    offsets = jnp.arange(MS, dtype=jnp.int32)
    flat_index = ((first_row[:, None, None] + offsets[None, :, None]) * W + place_col[:, None, None] + offsets[None, None, :]).reshape(total, MS * MS).astype(jnp.int32)
    values = master_half[master_id].astype(jnp.float32)
    canvas = jnp.zeros((ROWS * W,), jnp.float32).at[flat_index.reshape(-1)].add(values.reshape(-1))
    mask_half = lax.optimization_barrier(canvas.reshape(ROWS, W).astype(jnp.bfloat16))
    mask = mask_half.astype(jnp.float32)

    def forward_mode(pair):
        row_mode, col_mode = pair
        row_kernel = row_mode.astype(jnp.float32).reshape(2 * TERMS, 1, TAPS, 1)
        field_y = correlate(mask[None, None], row_kernel, HALF, 0)
        field_y = lax.optimization_barrier(field_y.astype(jnp.bfloat16)).astype(jnp.float32)
        return correlate(field_y, column_kernel(col_mode), 0, HALF)[0]

    fields = lax.map(forward_mode, (row_taps, col_taps))
    intensity = jnp.sum(mode_weights[:, None, None] * (fields[:, 0] ** 2 + fields[:, 1] ** 2), 0)
    resist = jax.nn.sigmoid(steepness * (intensity - threshold))
    resist_residual = resist - target.astype(jnp.float32)
    grad_intensity = resist_residual * steepness * resist * (1.0 - resist)

    def adjoint_mode(running, inputs):
        row_mode, col_mode, field, weight = inputs
        grad_field = (2.0 * weight * grad_intensity[None] * field).astype(jnp.bfloat16)
        grad_field = lax.optimization_barrier(grad_field).astype(jnp.float32)
        col_adjoint = jnp.flip(jnp.transpose(column_kernel(col_mode), (1, 0, 2, 3)), axis=3)
        grad_y = correlate(grad_field[None], col_adjoint, 0, HALF)
        grad_y = lax.optimization_barrier(grad_y.astype(jnp.bfloat16)).astype(jnp.float32)
        row_kernel = row_mode.astype(jnp.float32).reshape(2 * TERMS, 1, TAPS, 1)
        row_adjoint = jnp.flip(jnp.transpose(row_kernel, (1, 0, 2, 3)), axis=2)
        return running + correlate(grad_y, row_adjoint, HALF, 0)[0, 0], None

    grad_mask, _ = lax.scan(adjoint_mode, jnp.zeros((ROWS, W), jnp.float32), (row_taps, col_taps, fields, mode_weights))
    grad_patch = grad_mask.reshape(-1)[flat_index]
    master_grad = jax.ops.segment_sum(grad_patch, master_id, num_segments=M_DEV * N_TX)
    velocity_new = momentum * velocity + master_grad
    masters_new = masters - step_size * velocity_new
    return resist_residual, velocity_new, masters_new
```

```python
import jax
import jax.numpy as jnp
from jax import lax
from jax.experimental import pallas as pl
from jax.experimental.pallas import tpu as pltpu
from jax.sharding import PartitionSpec as P

W = 256
MS = 32
TAPS = 63
HALF = 31
TERMS = 4
MODES = 12
CH = 2 * TERMS
LANES = 128
BLK = 64
NBLK = W // BLK
EXT = 128
PAD = 40
CROWS = 72

steepness = 0.5
threshold = 8.0
momentum = 0.9
step_size = 0.05


def lane_iota(shape):
    return lax.broadcasted_iota(jnp.int32, shape, len(shape) - 1)


def skew(row, shift, rows):
    return pltpu.roll(
        jnp.broadcast_to(row, (rows, LANES)), shift, 1, stride=1, stride_axis=0
    )


def bands_kernel(taps_ref, r_ref, rt_ref, cf_ref, ca_ref):
    low = lane_iota((EXT, LANES)) < BLK

    def step(n, carry):
        k = n // 2
        half = n % 2
        first = k * CH + half * 4
        for f in range(4):
            r_ref[pl.ds((first + f) * BLK, BLK), :] = skew(
                taps_ref[0, pl.ds(first + f, 1), :], 0, BLK
            ).astype(jnp.bfloat16)
        for par in range(2):
            lo = skew(taps_ref[1, pl.ds(first + par, 1), :], 0, EXT)
            hi = skew(taps_ref[1, pl.ds(first + 2 + par, 1), :], BLK, EXT)
            rt_ref[n, par * EXT : (par + 1) * EXT, :] = jnp.where(low, lo, hi).astype(
                jnp.bfloat16
            )
        for t in range(2):
            c0 = taps_ref[2, pl.ds(first + 2 * t, 1), :]
            c1 = taps_ref[2, pl.ds(first + 2 * t + 1, 1), :]
            a0, a1 = skew(c0, 0, EXT), skew(c1, 0, EXT)
            b0, b1 = skew(c0, BLK, EXT), skew(c1, BLK, EXT)
            at = (half * 2 + t) * 2 * EXT
            cf_ref[k, pl.ds(at, EXT), :] = jnp.where(low, a0, b1).astype(jnp.bfloat16)
            cf_ref[k, pl.ds(at + EXT, EXT), :] = jnp.where(low, -a1, b0).astype(jnp.bfloat16)
            c0 = taps_ref[3, pl.ds(first + 2 * t, 1), :]
            c1 = taps_ref[3, pl.ds(first + 2 * t + 1, 1), :]
            a0, a1 = skew(c0, 0, EXT), skew(c1, 0, EXT)
            b0, b1 = skew(c0, BLK, EXT), skew(c1, BLK, EXT)
            ca_ref[n * 2 + t, :EXT, :] = jnp.where(low, a0, -b1).astype(jnp.bfloat16)
            ca_ref[n * 2 + t, EXT:, :] = jnp.where(low, a1, b0).astype(jnp.bfloat16)
        return carry

    lax.fori_loop(0, 2 * MODES, step, 0)


def build_bands(row_taps, col_taps):
    row = row_taps.reshape(MODES * CH, TAPS).astype(jnp.float32)
    col = col_taps.reshape(MODES * CH, TAPS).astype(jnp.float32)
    gap = LANES - TAPS

    def reversed_taps(v):
        return jnp.concatenate(
            [v[:, :1], jnp.zeros((v.shape[0], gap), jnp.float32), v[:, :0:-1]], axis=1
        )

    from_last = jnp.concatenate(
        [col[:, TAPS - 1 :], jnp.zeros((col.shape[0], gap), jnp.float32), col[:, : TAPS - 1]],
        axis=1,
    )
    taps = jnp.stack(
        [jnp.pad(row, ((0, 0), (0, gap))), reversed_taps(row), reversed_taps(col), from_last]
    )
    return pl.pallas_call(
        bands_kernel,
        out_shape=(
            jax.ShapeDtypeStruct((MODES * CH * BLK, LANES), jnp.bfloat16),
            jax.ShapeDtypeStruct((2 * MODES, 2 * EXT, LANES), jnp.bfloat16),
            jax.ShapeDtypeStruct((MODES, CH * EXT, LANES), jnp.bfloat16),
            jax.ShapeDtypeStruct((4 * MODES, 2 * EXT, LANES), jnp.bfloat16),
        ),
        in_specs=[pl.BlockSpec(memory_space=pltpu.VMEM)],
        out_specs=[pl.BlockSpec(memory_space=pltpu.VMEM)] * 4,
        name="bands",
    )(taps)


def main_kernel(
    own_ref,
    above_ref,
    below_ref,
    weight_ref,
    masters_ref,
    target_ref,
    r_ref,
    rt_ref,
    cf_ref,
    ca_ref,
    resid_ref,
    grads_ref,
    canvas_own,
    canvas_above,
    canvas_below,
    window,
    fields,
    gys,
    grad,
    acc_above,
    acc_below,
):
    places = own_ref.shape[1]
    rows = BLK
    canvases = ((own_ref, canvas_own), (above_ref, canvas_above), (below_ref, canvas_below))
    for _, canvas in canvases:
        canvas[...] = jnp.zeros_like(canvas)
    lanes8 = lane_iota((8, LANES))

    def place(q, carry):
        for ids, canvas in canvases:
            master = masters_ref[ids[0, q]].astype(jnp.float32)
            top = ids[1, q] + 7
            col = ids[2, q] + HALF
            side = col // LANES
            shift = col % LANES
            for k in range(4):
                moved = pltpu.roll(master, (shift + LANES - 32 * k) % LANES, 1)
                here = (lanes8 >= shift) & (lanes8 < shift + MS)
                after = lanes8 < shift + MS - LANES
                at = pl.ds(top + k, 8, stride=4)
                canvas[side, at, :] += jnp.where(here, moved, 0.0)
                canvas[side + 1, at, :] += jnp.where(after, moved, 0.0)
        return carry

    lax.fori_loop(0, places, place, 0)

    sides = []
    for h in range(3):
        a, o, b = canvas_above[h], canvas_own[h], canvas_below[h]
        sides.append(
            jnp.concatenate(
                [a[40:64], a[64:72] + o[0:8], o[8:64], o[64:72] + b[0:8], b[8:40]], axis=0
            )
        )
    low = lane_iota((EXT, LANES)) < BLK
    turned = [pltpu.roll(s, BLK, 1) for s in sides]
    window[:, 0:128] = sides[0].astype(jnp.bfloat16)
    window[:, 128:256] = jnp.where(low, turned[0], turned[1]).astype(jnp.bfloat16)
    window[:, 256:384] = sides[1].astype(jnp.bfloat16)
    window[:, 384:512] = jnp.where(low, turned[1], turned[2]).astype(jnp.bfloat16)

    intensity = jnp.zeros((NBLK * rows, LANES), jnp.float32)
    for k in range(MODES):
        field_y = jnp.dot(
            r_ref[k * CH * rows : (k + 1) * CH * rows, :],
            window[...],
            preferred_element_type=jnp.float32,
        ).astype(jnp.bfloat16)
        lhs = jnp.concatenate(
            [
                jnp.concatenate(
                    [
                        field_y[c * rows : (c + 1) * rows, b * LANES : (b + 1) * LANES]
                        for c in range(CH)
                    ],
                    axis=1,
                )
                for b in range(NBLK)
            ],
            axis=0,
        )
        e = jnp.dot(lhs, cf_ref[k], preferred_element_type=jnp.float32)
        fields[k] = e
        intensity = intensity + weight_ref[k] * (e * e)
    intensity = intensity + pltpu.roll(intensity, BLK, 1)
    low_rows = lane_iota((rows, LANES)) < BLK
    goal = []
    for h in range(2):
        t = target_ref[:, h * LANES : (h + 1) * LANES].astype(jnp.float32)
        other = pltpu.roll(t, BLK, 1)
        goal += [jnp.where(low_rows, t, other), jnp.where(low_rows, other, t)]
    resist = jax.nn.sigmoid(steepness * (intensity - threshold))
    resid = resist - jnp.concatenate(goal, axis=0)
    for h in range(2):
        first = resid[2 * h * rows : (2 * h + 1) * rows]
        second = resid[(2 * h + 1) * rows : (2 * h + 2) * rows]
        resid_ref[:, h * LANES : (h + 1) * LANES] = jnp.where(low_rows, first, second)
    grad_intensity = resid * steepness * resist * (1.0 - resist)

    lanes = lane_iota((rows, LANES))
    middle = (lanes >= HALF) & (lanes < HALF + BLK)
    left = lanes < HALF
    nothing = jnp.zeros((rows, LANES), jnp.float32)
    for k in range(MODES):
        g = 2.0 * weight_ref[k] * grad_intensity * fields[k]
        r31 = pltpu.roll(g, HALF, 1)
        r95 = pltpu.roll(g, HALF + BLK, 1)

        def part(v, b):
            return v[b * rows : (b + 1) * rows] if 0 <= b < NBLK else nothing

        parts = []
        for b in range(NBLK):
            re = jnp.where(
                middle, part(r31, b), jnp.where(left, part(r95, b - 1), part(r95, b + 1))
            )
            im = jnp.where(
                middle, part(r95, b), jnp.where(left, part(r31, b - 1), part(r31, b + 1))
            )
            parts.append(jnp.concatenate([re, im], axis=1))
        gw = jnp.concatenate(parts, axis=0).astype(jnp.bfloat16)
        for t in range(TERMS):
            gy = jnp.dot(
                gw, ca_ref[k * TERMS + t], preferred_element_type=jnp.float32
            ).astype(jnp.bfloat16)
            at = (k * TERMS + t) * rows
            for b in range(NBLK):
                gys[at : at + rows, b * LANES : (b + 1) * LANES] = gy[b * rows : (b + 1) * rows]

    total = jnp.zeros((2 * EXT, NBLK * LANES), jnp.float32)
    for n in range(2 * MODES):
        total = total + jnp.dot(
            rt_ref[n], gys[n * LANES : (n + 1) * LANES, :], preferred_element_type=jnp.float32
        )
    zeros = jnp.zeros((PAD, LANES), jnp.float32)
    for h in range(2):
        v0 = total[:EXT, 2 * h * LANES : (2 * h + 1) * LANES]
        v1 = total[:EXT, (2 * h + 1) * LANES : (2 * h + 2) * LANES]
        u0 = total[EXT:, 2 * h * LANES : (2 * h + 1) * LANES]
        u1 = total[EXT:, (2 * h + 1) * LANES : (2 * h + 2) * LANES]
        grad[h, PAD : PAD + EXT, :] = jnp.where(
            low, v0 + pltpu.roll(u0, BLK, 1), pltpu.roll(v1, BLK, 1) + u1
        )
        grad[h, :PAD, :] = zeros
        grad[h, PAD + EXT :, :] = zeros

    sums = (
        (own_ref, grads_ref, PAD + HALF),
        (above_ref, acc_above, PAD + HALF - rows),
        (below_ref, acc_below, PAD + HALF + rows),
    )
    for _, acc, _ in sums:
        acc[...] = jnp.zeros_like(acc)

    def gather(q, carry):
        for ids, acc, base in sums:
            m = ids[0, q]
            top = ids[1, q] + base
            col = ids[2, q]
            side = col // LANES
            after = jnp.minimum(side + 1, 1)
            shift = col % LANES
            patch = jnp.zeros((8, LANES), jnp.float32)
            for k in range(4):
                at = pl.ds(top + k, 8, stride=4)
                both = jnp.where(lanes8 >= shift, grad[side, at, :], grad[after, at, :])
                moved = pltpu.roll(both, (LANES + 32 * k - shift) % LANES, 1)
                patch = jnp.where((lanes8 >= 32 * k) & (lanes8 < 32 * k + MS), moved, patch)
            acc[m] += patch
        return carry

    lax.fori_loop(0, places, gather, 0)
    grads_ref[...] += acc_above[...] + acc_below[...]


def main_step(own, above, below, weights, masters, target, bands):
    count = masters.shape[0]
    smem = pl.BlockSpec(memory_space=pltpu.SMEM)
    vmem = pl.BlockSpec(memory_space=pltpu.VMEM)
    return pl.pallas_call(
        main_kernel,
        out_shape=(
            jax.ShapeDtypeStruct(target.shape, jnp.float32),
            jax.ShapeDtypeStruct((count, 8, LANES), jnp.float32),
        ),
        in_specs=[smem] * 4 + [vmem] * 6,
        out_specs=[vmem] * 2,
        scratch_shapes=[
            pltpu.VMEM((3, CROWS, LANES), jnp.float32),
            pltpu.VMEM((3, CROWS, LANES), jnp.float32),
            pltpu.VMEM((3, CROWS, LANES), jnp.float32),
            pltpu.VMEM((EXT, NBLK * LANES), jnp.bfloat16),
            pltpu.VMEM((MODES, NBLK * BLK, LANES), jnp.float32),
            pltpu.VMEM((MODES * TERMS * BLK, NBLK * LANES), jnp.bfloat16),
            pltpu.VMEM((2, 2 * PAD + EXT, LANES), jnp.float32),
            pltpu.VMEM((count, 8, LANES), jnp.float32),
            pltpu.VMEM((count, 8, LANES), jnp.float32),
        ],
        name="imaging",
    )(own, above, below, weights, masters, target, *bands)


def update_kernel(sent_ref, velocity_ref, masters_ref, velocity_out, masters_out, sums):
    count = velocity_ref.shape[0]
    total = sent_ref[0]
    for d in range(1, sent_ref.shape[0]):
        total = total + sent_ref[d]
    sums[...] = total.reshape(count * 8, LANES)
    for s in range(8):
        at = slice(s * LANES, (s + 1) * LANES)
        gradient = sums[pl.ds(s, count, stride=8), :]
        velocity = momentum * velocity_ref[:, at] + gradient
        velocity_out[:, at] = velocity
        masters_out[:, at] = masters_ref[:, at] - step_size * velocity


def update(sent, velocity, masters):
    vmem = pl.BlockSpec(memory_space=pltpu.VMEM)
    return pl.pallas_call(
        update_kernel,
        out_shape=(jax.ShapeDtypeStruct(velocity.shape, jnp.float32),) * 2,
        in_specs=[vmem] * 3,
        out_specs=[vmem] * 2,
        scratch_shapes=[pltpu.VMEM((8 * velocity.shape[0], LANES), jnp.float32)],
        name="update",
    )(sent, velocity, masters)


def on_device(
    masters,
    velocity,
    place_owner,
    place_local,
    place_row,
    place_col,
    row_taps,
    col_taps,
    mode_weights,
    target,
):
    devices = lax.axis_size("tx")
    count = masters.shape[0]
    master_id = place_owner[:, 0] * count + place_local
    own = jnp.stack([master_id, place_row, place_col])
    flipped = jnp.stack([master_id, (BLK - MS) - place_row, place_col])
    forward = [(i, i + 1) for i in range(devices - 1)]
    backward = [(i + 1, i) for i in range(devices - 1)]
    above = lax.ppermute(own, "tx", forward)
    below = lax.ppermute(flipped, "tx", backward)
    below = below * jnp.array([1, -1, 1], jnp.int32)[:, None] + jnp.array(
        [0, BLK - MS, 0], jnp.int32
    )[:, None]
    half = masters.astype(jnp.bfloat16).reshape(count, 8, LANES)
    everywhere = jnp.broadcast_to(half[None], (devices, count, 8, LANES))
    gathered = lax.all_to_all(everywhere, "tx", split_axis=0, concat_axis=0, tiled=True)
    gathered = gathered.reshape(devices * count, 8, LANES)
    bands = build_bands(row_taps, col_taps)
    resid, grads = main_step(own, above, below, mode_weights, gathered, target, bands)
    sent = lax.all_to_all(
        grads.reshape(devices, count, 8, LANES), "tx", split_axis=0, concat_axis=0, tiled=True
    )
    velocity_new, masters_new = update(sent, velocity, masters)
    return resid, velocity_new, masters_new


def solution(mesh):
    return jax.shard_map(
        on_device,
        mesh=mesh,
        in_specs=(
            P(("groups", "tx"), None),
            P(("groups", "tx"), None),
            P(("groups", "tx"), None),
            P(("groups", "tx")),
            P(("groups", "tx")),
            P(("groups", "tx")),
            P(),
            P(),
            P(),
            P(("groups", "tx"), None),
        ),
        out_specs=(P(("groups", "tx"), None), P(("groups", "tx"), None), P(("groups", "tx"), None)),
        check_vma=False,
    )
```

```python
import jax
import jax.numpy as jnp
from jax import lax
from jax.experimental import pallas as pl
from jax.experimental.pallas import tpu as pltpu
from jax.sharding import PartitionSpec as P

W = 256
MS = 32
TAPS = 63
HALF = 31
TERMS = 4
MODES = 12
CH = 2 * TERMS
LANES = 128
BLK = 64
NBLK = W // BLK
EXT = 128
PAD = 40
CROWS = 72

steepness = 0.5
threshold = 8.0
momentum = 0.9
step_size = 0.05


def in_vmem(x):
    return pltpu.with_memory_space_constraint(x, pltpu.VMEM)


def lane_iota(shape):
    return lax.broadcasted_iota(jnp.int32, shape, len(shape) - 1)


def skew(row, shift):
    return pltpu.roll(
        jnp.broadcast_to(row, (BLK, LANES)), shift, 1, stride=1, stride_axis=0
    )


def pair(first, second):
    return (skew(first, 0), skew(first, BLK), skew(second, 0), skew(second, BLK))


def half_band(x):
    return x.astype(jnp.bfloat16)


def low_lanes():
    return lane_iota((BLK, LANES)) < BLK


def row_bands_kernel(row_ref, col_ref, r_ref, taps):
    count = MODES * CH
    taps[...] = jnp.zeros_like(taps)
    for k in range(MODES):
        for t in range(TERMS):
            at = k * CH + 2 * t
            taps[at : at + 2, :TAPS] = row_ref[k, t].astype(jnp.float32)
            taps[count + at : count + at + 2, :TAPS] = col_ref[k, t].astype(jnp.float32)
    source = lax.broadcasted_iota(jnp.int32, (LANES, LANES), 0)
    mirror = (source + lane_iota((LANES, LANES))) % LANES == 0
    taps[2 * count :, :] = jnp.dot(
        taps[: 2 * count, :].astype(jnp.bfloat16),
        mirror.astype(jnp.bfloat16),
        preferred_element_type=jnp.float32,
    )
    taps[count : 2 * count, :] = pltpu.roll(taps[count : 2 * count, :], LANES - (TAPS - 1), 1)

    def step(n, carry):
        for f in range(4):
            at = n * 4 + f
            r_ref[pl.ds(at * BLK, BLK), :] = half_band(skew(taps[pl.ds(at, 1), :], 0))
        return carry

    lax.fori_loop(0, 2 * MODES, step, 0)


def row_adjoint_kernel(taps, rt_ref):
    count = MODES * CH
    low = low_lanes()

    def step(n, carry):
        first = 2 * count + 4 * n
        for par in range(2):
            a, a_far, b, b_far = pair(
                taps[pl.ds(first + par, 1), :], taps[pl.ds(first + 2 + par, 1), :]
            )
            rt_ref[n, par * EXT : par * EXT + BLK, :] = half_band(jnp.where(low, a, b_far))
            rt_ref[n, par * EXT + BLK : (par + 1) * EXT, :] = half_band(jnp.where(low, a_far, b))
        return carry

    lax.fori_loop(0, 2 * MODES, step, 0)


def column_bands_kernel(taps, cf_ref):
    count = MODES * CH
    low = low_lanes()

    def step(n, carry):
        first = 3 * count + 4 * n
        for t in range(2):
            at = t * 2 * EXT
            a, a_far, b, b_far = pair(
                taps[pl.ds(first + 2 * t, 1), :], taps[pl.ds(first + 2 * t + 1, 1), :]
            )
            cf_ref[n, at : at + BLK, :] = half_band(jnp.where(low, a, b_far))
            cf_ref[n, at + BLK : at + EXT, :] = half_band(jnp.where(low, a_far, b))
            cf_ref[n, at + EXT : at + EXT + BLK, :] = half_band(jnp.where(low, -b, a_far))
            cf_ref[n, at + EXT + BLK : at + 2 * EXT, :] = half_band(jnp.where(low, -b_far, a))
        return carry

    lax.fori_loop(0, 2 * MODES, step, 0)


def column_adjoint_kernel(taps, ca_ref):
    count = MODES * CH
    low = low_lanes()

    def step(n, carry):
        first = count + 4 * n
        for t in range(2):
            a, a_far, b, b_far = pair(
                taps[pl.ds(first + 2 * t, 1), :], taps[pl.ds(first + 2 * t + 1, 1), :]
            )
            ca_ref[n * 2 + t, :BLK, :] = half_band(jnp.where(low, a, -b_far))
            ca_ref[n * 2 + t, BLK:EXT, :] = half_band(jnp.where(low, a_far, -b))
            ca_ref[n * 2 + t, EXT : EXT + BLK, :] = half_band(jnp.where(low, b, a_far))
            ca_ref[n * 2 + t, EXT + BLK :, :] = half_band(jnp.where(low, b_far, a))
        return carry

    lax.fori_loop(0, 2 * MODES, step, 0)


def build_bands(row_taps, col_taps):
    vmem = pl.BlockSpec(memory_space=pltpu.VMEM)
    small = pltpu.CompilerParams(vmem_limit_bytes=4 << 20)
    r, taps = pl.pallas_call(
        row_bands_kernel,
        out_shape=(
            pltpu.VMEM((MODES * CH * BLK, LANES), jnp.bfloat16),
            pltpu.VMEM((4 * MODES * CH, LANES), jnp.float32),
        ),
        in_specs=[vmem] * 2,
        out_specs=[vmem] * 2,
        compiler_params=small,
        name="row_bands",
    )(row_taps, col_taps)
    taps = in_vmem(taps)
    built = [
        pl.pallas_call(
            kernel,
            out_shape=pltpu.VMEM(shape, jnp.bfloat16),
            in_specs=[vmem],
            out_specs=vmem,
            compiler_params=small,
            name=name,
        )(taps)
        for kernel, shape, name in (
            (row_adjoint_kernel, (2 * MODES, 2 * EXT, LANES), "row_adjoint"),
            (column_bands_kernel, (2 * MODES, CH * EXT // 2, LANES), "column_bands"),
            (column_adjoint_kernel, (4 * MODES, 2 * EXT, LANES), "column_adjoint"),
        )
    ]
    return [r, *built]


def main_kernel(
    weight_ref,
    gathered_ref,
    target_ref,
    r_ref,
    rt_ref,
    cf_ref,
    ca_ref,
    resid_ref,
    grads_ref,
    canvas_own,
    canvas_above,
    canvas_below,
    window,
    fields,
    gys,
    grad,
    acc_own,
    acc_above,
    acc_below,
    table,
    ids,
    sem,
):
    devices, slabs = gathered_ref.shape[:2]
    count = slabs - 1
    places = LANES
    rows = BLK
    me = lax.axis_index("tx")
    bits = devices.bit_length() - 1
    for n, (other, missing) in enumerate(
        ((me, 0), (jnp.maximum(me - 1, 0), 0), (jnp.minimum(me + 1, devices - 1), BLK - MS))
    ):
        slab = gathered_ref[other ^ me, count].astype(jnp.float32).astype(jnp.int32)
        owner, local = slab[0:1] ^ me, slab[1:2]
        turned = sum(((owner >> b) & 1) << (bits - 1 - b) for b in range(bits))
        table[n, 0:1, :] = owner * slabs + local
        table[n, 1:2, :] = turned * count + local
        row = slab[2:3]
        table[n, 2:3, :] = row if n == 0 else jnp.where(other == me, missing, row)
        table[n, 3:4, :] = slab[3:4]
    to_scalar = pltpu.make_async_copy(table, ids, sem)
    to_scalar.start()
    canvases = ((0, canvas_own), (1, canvas_above), (2, canvas_below))
    for _, canvas in canvases:
        canvas[...] = jnp.zeros_like(canvas)
    lanes8 = lane_iota((8, LANES))
    to_scalar.wait()

    def place(q, carry):
        for n, canvas in canvases:
            at = ids[n, 0, q]
            master = gathered_ref[at // slabs, at % slabs].astype(jnp.float32)
            top = ids[n, 2, q] + 7
            col = ids[n, 3, q] + HALF
            side = col >> 7
            shift = col & 127
            for k in range(4):
                moved = pltpu.roll(master, (shift + LANES - 32 * k) & 127, 1)
                here = (lanes8 >= shift) & (lanes8 < shift + MS)
                after = lanes8 < shift + MS - LANES
                at = pl.ds(top + k, 8, stride=4)
                canvas[side, at, :] += jnp.where(here, moved, 0.0)
                canvas[side + 1, at, :] += jnp.where(after, moved, 0.0)
        return carry

    lax.fori_loop(0, places, place, 0, unroll=8)

    sides = []
    for h in range(3):
        a, o, b = canvas_above[h], canvas_own[h], canvas_below[h]
        sides.append(
            jnp.concatenate(
                [a[40:64], a[64:72] + o[0:8], o[8:64], o[64:72] + b[0:8], b[8:40]], axis=0
            )
        )
    low = lane_iota((EXT, LANES)) < BLK
    turned = [pltpu.roll(s, BLK, 1) for s in sides]
    window[:, 0:128] = sides[0].astype(jnp.bfloat16)
    window[:, 128:256] = jnp.where(low, turned[0], turned[1]).astype(jnp.bfloat16)
    window[:, 256:384] = sides[1].astype(jnp.bfloat16)
    window[:, 384:512] = jnp.where(low, turned[1], turned[2]).astype(jnp.bfloat16)

    intensity = jnp.zeros((NBLK * rows, LANES), jnp.float32)
    for k in range(MODES):
        field_y = jnp.dot(
            r_ref[k * CH * rows : (k + 1) * CH * rows, :],
            window[...],
            preferred_element_type=jnp.float32,
        ).astype(jnp.bfloat16)
        lhs = jnp.concatenate(
            [
                jnp.concatenate(
                    [
                        field_y[c * rows : (c + 1) * rows, b * LANES : (b + 1) * LANES]
                        for c in range(CH)
                    ],
                    axis=1,
                )
                for b in range(NBLK)
            ],
            axis=0,
        )
        e = jnp.dot(
            lhs,
            jnp.concatenate([cf_ref[2 * k], cf_ref[2 * k + 1]], axis=0),
            preferred_element_type=jnp.float32,
        )
        fields[k] = e
        intensity = intensity + weight_ref[k] * (e * e)
    intensity = intensity + pltpu.roll(intensity, BLK, 1)
    low_rows = lane_iota((rows, LANES)) < BLK
    goal = []
    for h in range(2):
        t = target_ref[:, h * LANES : (h + 1) * LANES].astype(jnp.float32)
        other = pltpu.roll(t, BLK, 1)
        goal += [jnp.where(low_rows, t, other), jnp.where(low_rows, other, t)]
    resist = jax.nn.sigmoid(steepness * (intensity - threshold))
    resid = resist - jnp.concatenate(goal, axis=0)
    for h in range(2):
        first = resid[2 * h * rows : (2 * h + 1) * rows]
        second = resid[(2 * h + 1) * rows : (2 * h + 2) * rows]
        resid_ref[:, h * LANES : (h + 1) * LANES] = jnp.where(low_rows, first, second)
    grad_intensity = resid * steepness * resist * (1.0 - resist)

    lanes = lane_iota((rows, LANES))
    middle = (lanes >= HALF) & (lanes < HALF + BLK)
    left = lanes < HALF
    nothing = jnp.zeros((rows, LANES), jnp.float32)
    for k in range(MODES):
        g = 2.0 * weight_ref[k] * grad_intensity * fields[k]
        r31 = pltpu.roll(g, HALF, 1)
        r95 = pltpu.roll(g, HALF + BLK, 1)

        def part(v, b):
            return v[b * rows : (b + 1) * rows] if 0 <= b < NBLK else nothing

        parts = []
        for b in range(NBLK):
            re = jnp.where(
                middle, part(r31, b), jnp.where(left, part(r95, b - 1), part(r95, b + 1))
            )
            im = jnp.where(
                middle, part(r95, b), jnp.where(left, part(r31, b - 1), part(r31, b + 1))
            )
            parts.append(jnp.concatenate([re, im], axis=1))
        gw = jnp.concatenate(parts, axis=0).astype(jnp.bfloat16)
        for t in range(TERMS):
            gy = jnp.dot(
                gw, ca_ref[k * TERMS + t], preferred_element_type=jnp.float32
            ).astype(jnp.bfloat16)
            at = (k * TERMS + t) * rows
            for b in range(NBLK):
                gys[at : at + rows, b * LANES : (b + 1) * LANES] = gy[b * rows : (b + 1) * rows]

    total = jnp.zeros((2 * EXT, NBLK * LANES), jnp.float32)
    for n in range(2 * MODES):
        total = total + jnp.dot(
            rt_ref[n], gys[n * LANES : (n + 1) * LANES, :], preferred_element_type=jnp.float32
        )
    zeros = jnp.zeros((PAD, LANES), jnp.float32)
    for h in range(2):
        v0 = total[:EXT, 2 * h * LANES : (2 * h + 1) * LANES]
        v1 = total[:EXT, (2 * h + 1) * LANES : (2 * h + 2) * LANES]
        u0 = total[EXT:, 2 * h * LANES : (2 * h + 1) * LANES]
        u1 = total[EXT:, (2 * h + 1) * LANES : (2 * h + 2) * LANES]
        grad[h, PAD : PAD + EXT, :] = jnp.where(
            low, v0 + pltpu.roll(u0, BLK, 1), pltpu.roll(v1, BLK, 1) + u1
        )
        grad[h, :PAD, :] = zeros
        grad[h, PAD + EXT :, :] = zeros

    sums = (
        (0, acc_own, PAD + HALF),
        (1, acc_above, PAD + HALF - rows),
        (2, acc_below, PAD + HALF + rows),
    )
    for _, acc, _ in sums:
        acc[...] = jnp.zeros_like(acc)

    def gather(q, carry):
        for n, acc, base in sums:
            m = ids[n, 1, q]
            top = ids[n, 2, q] + base
            col = ids[n, 3, q]
            side = col >> 7
            after = jnp.minimum(side + 1, 1)
            shift = col & 127
            patch = jnp.zeros((8, LANES), jnp.float32)
            for k in range(4):
                at = pl.ds(top + k, 8, stride=4)
                both = jnp.where(lanes8 >= shift, grad[side, at, :], grad[after, at, :])
                moved = pltpu.roll(both, (LANES + 32 * k - shift) & 127, 1)
                patch = jnp.where((lanes8 >= 32 * k) & (lanes8 < 32 * k + MS), moved, patch)
            acc[m] += patch
        return carry

    lax.fori_loop(0, places, gather, 0, unroll=8)
    grads_ref[...] = (acc_own[...] + acc_above[...] + acc_below[...]).reshape(grads_ref.shape)


def main_step(weights, gathered, target, bands):
    devices, slabs = gathered.shape[:2]
    count = slabs - 1
    vmem = pl.BlockSpec(memory_space=pltpu.VMEM)
    accumulator = pltpu.VMEM((devices * count, 8, LANES), jnp.float32)
    return pl.pallas_call(
        main_kernel,
        out_shape=(
            jax.ShapeDtypeStruct(target.shape, jnp.float32),
            pltpu.VMEM((devices, count, 8, LANES), jnp.float32),
        ),
        in_specs=[pl.BlockSpec(memory_space=pltpu.SMEM)] + [vmem] * 6,
        out_specs=[vmem] * 2,
        scratch_shapes=[
            pltpu.VMEM((3, CROWS, LANES), jnp.float32),
            pltpu.VMEM((3, CROWS, LANES), jnp.float32),
            pltpu.VMEM((3, CROWS, LANES), jnp.float32),
            pltpu.VMEM((EXT, NBLK * LANES), jnp.bfloat16),
            pltpu.VMEM((MODES, NBLK * BLK, LANES), jnp.float32),
            pltpu.VMEM((MODES * TERMS * BLK, NBLK * LANES), jnp.bfloat16),
            pltpu.VMEM((2, 2 * PAD + EXT, LANES), jnp.float32),
            accumulator,
            accumulator,
            accumulator,
            pltpu.VMEM((3, 8, LANES), jnp.int32),
            pltpu.SMEM((3, 8, LANES), jnp.int32),
            pltpu.SemaphoreType.DMA,
        ],
        compiler_params=pltpu.CompilerParams(vmem_limit_bytes=24 << 20),
        name="imaging",
    )(weights, in_vmem(gathered), target, *[in_vmem(b) for b in bands])


def pack_kernel(masters_ref, owner_ref, local_ref, row_ref, col_ref, out_ref, spread):
    count = masters_ref.shape[0]
    for s in range(8):
        spread[pl.ds(s, count, stride=8), :] = masters_ref[:, s * LANES : (s + 1) * LANES]
    spread[8 * count :, :] = jnp.zeros((8, LANES), jnp.float32)
    for n, ref in enumerate((owner_ref, local_ref, row_ref, col_ref)):
        spread[8 * count + n : 8 * count + n + 1, :] = ref[...].astype(jnp.float32)
    out_ref[...] = spread[...].reshape(out_ref.shape).astype(jnp.bfloat16)


def pack(masters, *places):
    count = masters.shape[0]
    vmem = pl.BlockSpec(memory_space=pltpu.VMEM)
    return pl.pallas_call(
        pack_kernel,
        out_shape=pltpu.VMEM((1, count + 1, 8, LANES), jnp.bfloat16),
        in_specs=[vmem] * 5,
        out_specs=vmem,
        scratch_shapes=[pltpu.VMEM((8 * count + 8, LANES), jnp.float32)],
        compiler_params=pltpu.CompilerParams(vmem_limit_bytes=4 << 20),
        name="pack",
    )(masters, *[p.reshape(1, LANES) for p in places])


def update_kernel(kept_ref, sent_ref, velocity_ref, masters_ref, velocity_out, masters_out, sums):
    count = velocity_ref.shape[0]
    sums[...] = (kept_ref[0] + sent_ref[0]).reshape(count * 8, LANES)
    for s in range(8):
        at = slice(s * LANES, (s + 1) * LANES)
        gradient = sums[pl.ds(s, count, stride=8), :]
        velocity = momentum * velocity_ref[:, at] + gradient
        velocity_out[:, at] = velocity
        masters_out[:, at] = masters_ref[:, at] - step_size * velocity


def update(kept, sent, velocity, masters):
    vmem = pl.BlockSpec(memory_space=pltpu.VMEM)
    return pl.pallas_call(
        update_kernel,
        out_shape=(jax.ShapeDtypeStruct(velocity.shape, jnp.float32),) * 2,
        in_specs=[vmem] * 4,
        out_specs=[vmem] * 2,
        scratch_shapes=[pltpu.VMEM((8 * velocity.shape[0], LANES), jnp.float32)],
        compiler_params=pltpu.CompilerParams(vmem_limit_bytes=4 << 20),
        name="update",
    )(kept, sent, velocity, masters)


def swap(value, bit, devices):
    return lax.ppermute(value, "tx", [(i, i ^ bit) for i in range(devices)])


def on_device(
    masters,
    velocity,
    place_owner,
    place_local,
    place_row,
    place_col,
    row_taps,
    col_taps,
    mode_weights,
    target,
):
    devices = lax.axis_size("tx")
    bits = devices.bit_length() - 1
    held = pack(masters, place_owner, place_local, place_row, place_col)
    for b in range(bits):
        held = jnp.concatenate([held, swap(held, 1 << b, devices)], axis=0)
    bands = build_bands(row_taps, col_taps)
    resid, grads = main_step(mode_weights, held, target, bands)
    for b in range(bits):
        half = grads.shape[0] // 2
        sent = swap(grads[half:], 1 << b, devices)
        if b < bits - 1:
            grads = grads[:half] + sent
    velocity_new, masters_new = update(grads, sent, velocity, masters)
    return resid, velocity_new, masters_new


def solution(mesh):
    return jax.shard_map(
        on_device,
        mesh=mesh,
        in_specs=(
            P(("groups", "tx"), None),
            P(("groups", "tx"), None),
            P(("groups", "tx"), None),
            P(("groups", "tx")),
            P(("groups", "tx")),
            P(("groups", "tx")),
            P(),
            P(),
            P(),
            P(("groups", "tx"), None),
        ),
        out_specs=(P(("groups", "tx"), None), P(("groups", "tx"), None), P(("groups", "tx"), None)),
        check_vma=False,
    )
```

```python
import functools
import jax
import jax.numpy as jnp
from jax import lax
from jax.experimental import pallas as pl
from jax.experimental.pallas import tpu as pltpu
from jax.sharding import PartitionSpec as P

W = 256
MS = 32
TAPS = 63
HALF = 31
TERMS = 4
MODES = 12
CH = 2 * TERMS
LANES = 128
BLK = 64
NBLK = W // BLK
EXT = 128
PAD = 40
CROWS = 72

steepness = 0.5
threshold = 8.0
momentum = 0.9
step_size = 0.05


def in_vmem(x):
    return pltpu.with_memory_space_constraint(x, pltpu.VMEM)


def in_hbm(x):
    return pltpu.with_memory_space_constraint(x, pltpu.HBM)


def lane_iota(shape):
    return lax.broadcasted_iota(jnp.int32, shape, len(shape) - 1)


def skew(row, shift):
    return pltpu.roll(
        jnp.broadcast_to(row, (BLK, LANES)), shift, 1, stride=1, stride_axis=0
    )


def pair(first, second):
    return (skew(first, 0), skew(first, BLK), skew(second, 0), skew(second, BLK))


def half_band(x):
    return x.astype(jnp.bfloat16)


def low_lanes():
    return lane_iota((BLK, LANES)) < BLK


def row_bands_kernel(row_ref, col_ref, r_ref, taps):
    count = MODES * CH
    taps[...] = jnp.zeros_like(taps)
    for k in range(MODES):
        for t in range(TERMS):
            at = k * CH + 2 * t
            taps[at : at + 2, :TAPS] = row_ref[k, t].astype(jnp.float32)
            taps[count + at : count + at + 2, :TAPS] = col_ref[k, t].astype(jnp.float32)
    source = lax.broadcasted_iota(jnp.int32, (LANES, LANES), 0)
    mirror = (source + lane_iota((LANES, LANES))) % LANES == 0
    taps[2 * count :, :] = jnp.dot(
        taps[: 2 * count, :].astype(jnp.bfloat16),
        mirror.astype(jnp.bfloat16),
        preferred_element_type=jnp.float32,
    )
    taps[count : 2 * count, :] = pltpu.roll(taps[count : 2 * count, :], LANES - (TAPS - 1), 1)

    def step(n, carry):
        for f in range(4):
            at = n * 4 + f
            r_ref[pl.ds(at * BLK, BLK), :] = half_band(skew(taps[pl.ds(at, 1), :], 0))
        return carry

    lax.fori_loop(0, 2 * MODES, step, 0, unroll=3)


def row_adjoint_kernel(taps, _, rt_ref):
    count = MODES * CH
    low = low_lanes()

    def step(n, carry):
        first = 2 * count + 4 * n
        for par in range(2):
            a, a_far, b, b_far = pair(
                taps[pl.ds(first + par, 1), :], taps[pl.ds(first + 2 + par, 1), :]
            )
            rt_ref[n, par * EXT : par * EXT + BLK, :] = half_band(jnp.where(low, a, b_far))
            rt_ref[n, par * EXT + BLK : (par + 1) * EXT, :] = half_band(jnp.where(low, a_far, b))
        return carry

    lax.fori_loop(0, 2 * MODES, step, 0, unroll=3)


def column_bands_kernel(taps, _, cf_ref):
    count = MODES * CH
    low = low_lanes()

    def step(n, carry):
        first = 3 * count + 4 * n
        for t in range(2):
            at = t * 2 * EXT
            a, a_far, b, b_far = pair(
                taps[pl.ds(first + 2 * t, 1), :], taps[pl.ds(first + 2 * t + 1, 1), :]
            )
            cf_ref[n, at : at + BLK, :] = half_band(jnp.where(low, a, b_far))
            cf_ref[n, at + BLK : at + EXT, :] = half_band(jnp.where(low, a_far, b))
            cf_ref[n, at + EXT : at + EXT + BLK, :] = half_band(jnp.where(low, -b, a_far))
            cf_ref[n, at + EXT + BLK : at + 2 * EXT, :] = half_band(jnp.where(low, -b_far, a))
        return carry

    lax.fori_loop(0, 2 * MODES, step, 0, unroll=3)


def column_adjoint_kernel(taps, _, ca_ref):
    count = MODES * CH
    low = low_lanes()

    def step(n, carry):
        first = count + 4 * n
        for t in range(2):
            a, a_far, b, b_far = pair(
                taps[pl.ds(first + 2 * t, 1), :], taps[pl.ds(first + 2 * t + 1, 1), :]
            )
            ca_ref[n * 2 + t, :BLK, :] = half_band(jnp.where(low, a, -b_far))
            ca_ref[n * 2 + t, BLK:EXT, :] = half_band(jnp.where(low, a_far, -b))
            ca_ref[n * 2 + t, EXT : EXT + BLK, :] = half_band(jnp.where(low, b, a_far))
            ca_ref[n * 2 + t, EXT + BLK :, :] = half_band(jnp.where(low, b_far, a))
        return carry

    lax.fori_loop(0, 2 * MODES, step, 0, unroll=3)


def build_bands(row_taps, col_taps, stages):
    vmem = pl.BlockSpec(memory_space=pltpu.VMEM)
    small = pltpu.CompilerParams(vmem_limit_bytes=4 << 20)
    r, taps = pl.pallas_call(
        row_bands_kernel,
        out_shape=(
            pltpu.VMEM((MODES * CH * BLK, LANES), jnp.bfloat16),
            pltpu.VMEM((4 * MODES * CH, LANES), jnp.float32),
        ),
        in_specs=[vmem] * 2,
        out_specs=[vmem] * 2,
        compiler_params=small,
        name="row_bands",
    )(in_hbm(row_taps), in_hbm(col_taps))
    taps = in_vmem(taps)
    built = [
        pl.pallas_call(
            kernel,
            out_shape=pltpu.VMEM(shape, jnp.bfloat16),
            in_specs=[vmem, pl.BlockSpec(memory_space=pl.ANY)],
            out_specs=vmem,
            compiler_params=small,
            name=name,
        )(taps, stage)
        for stage, (kernel, shape, name) in zip(
            stages,
            (
                (column_bands_kernel, (2 * MODES, CH * EXT // 2, LANES), "column_bands"),
                (row_adjoint_kernel, (2 * MODES, 2 * EXT, LANES), "row_adjoint"),
                (column_adjoint_kernel, (4 * MODES, 2 * EXT, LANES), "column_adjoint"),
            ),
        )
    ]
    return [r, built[1], built[0], built[2]]


def main_kernel(
    devices,
    weight_ref,
    gathered_ref,
    target_ref,
    r_ref,
    rt_ref,
    cf_ref,
    ca_ref,
    resid_ref,
    grads_ref,
    canvas_own,
    canvas_above,
    canvas_below,
    window,
    fields,
    gys,
    grad,
    acc_own,
    acc_above,
    acc_below,
    table,
    ids,
    sem,
):
    slabs = gathered_ref.shape[0] // devices
    count = slabs - 1
    places = LANES
    rows = BLK
    me = lax.axis_index("tx")
    bits = devices.bit_length() - 1
    for n, (other, missing) in enumerate(
        ((me, 0), (jnp.maximum(me - 1, 0), 0), (jnp.minimum(me + 1, devices - 1), BLK - MS))
    ):
        slab = gathered_ref[(other ^ me) * slabs + count].astype(jnp.float32).astype(jnp.int32)
        owner, local = slab[0:1] ^ me, slab[1:2]
        turned = sum(((owner >> b) & 1) << (bits - 1 - b) for b in range(bits))
        table[n, 0:1, :] = owner * slabs + local
        table[n, 1:2, :] = turned * count + local
        row = slab[2:3]
        table[n, 2:3, :] = row if n == 0 else jnp.where(other == me, missing, row)
        table[n, 3:4, :] = slab[3:4]
    to_scalar = pltpu.make_async_copy(table, ids, sem)
    to_scalar.start()
    canvases = ((0, canvas_own), (1, canvas_above), (2, canvas_below))
    for _, canvas in canvases:
        canvas[...] = jnp.zeros_like(canvas)
    lanes8 = lane_iota((8, LANES))
    to_scalar.wait()

    def place(q, carry):
        for n, canvas in canvases:
            master = gathered_ref[ids[n, 0, q]].astype(jnp.float32)
            top = ids[n, 2, q] + 7
            col = ids[n, 3, q] + HALF
            side = col >> 7
            shift = col & 127
            for k in range(4):
                moved = pltpu.roll(master, (shift + LANES - 32 * k) & 127, 1)
                here = (lanes8 >= shift) & (lanes8 < shift + MS)
                after = lanes8 < shift + MS - LANES
                at = pl.ds(top + k, 8, stride=4)
                canvas[side, at, :] += jnp.where(here, moved, 0.0)
                canvas[side + 1, at, :] += jnp.where(after, moved, 0.0)
        return carry

    lax.fori_loop(0, places, place, 0, unroll=8)

    sides = []
    for h in range(3):
        a, o, b = canvas_above[h], canvas_own[h], canvas_below[h]
        sides.append(
            jnp.concatenate(
                [a[40:64], a[64:72] + o[0:8], o[8:64], o[64:72] + b[0:8], b[8:40]], axis=0
            )
        )
    low = lane_iota((EXT, LANES)) < BLK
    turned = [pltpu.roll(s, BLK, 1) for s in sides]
    window[:, 0:128] = sides[0].astype(jnp.bfloat16)
    window[:, 128:256] = jnp.where(low, turned[0], turned[1]).astype(jnp.bfloat16)
    window[:, 256:384] = sides[1].astype(jnp.bfloat16)
    window[:, 384:512] = jnp.where(low, turned[1], turned[2]).astype(jnp.bfloat16)

    intensity = jnp.zeros((NBLK * rows, LANES), jnp.float32)
    for k in range(MODES):
        field_y = jnp.dot(
            r_ref[k * CH * rows : (k + 1) * CH * rows, :],
            window[...],
            preferred_element_type=jnp.float32,
        ).astype(jnp.bfloat16)
        lhs = jnp.concatenate(
            [
                jnp.concatenate(
                    [
                        field_y[c * rows : (c + 1) * rows, b * LANES : (b + 1) * LANES]
                        for c in range(CH)
                    ],
                    axis=1,
                )
                for b in range(NBLK)
            ],
            axis=0,
        )
        e = jnp.dot(
            lhs,
            jnp.concatenate([cf_ref[2 * k], cf_ref[2 * k + 1]], axis=0),
            preferred_element_type=jnp.float32,
        )
        fields[k] = e
        intensity = intensity + weight_ref[k] * (e * e)
    intensity = intensity + pltpu.roll(intensity, BLK, 1)
    low_rows = lane_iota((rows, LANES)) < BLK
    goal = []
    for h in range(2):
        t = target_ref[:, h * LANES : (h + 1) * LANES].astype(jnp.float32)
        other = pltpu.roll(t, BLK, 1)
        goal += [jnp.where(low_rows, t, other), jnp.where(low_rows, other, t)]
    resist = jax.nn.sigmoid(steepness * (intensity - threshold))
    resid = resist - jnp.concatenate(goal, axis=0)
    for h in range(2):
        first = resid[2 * h * rows : (2 * h + 1) * rows]
        second = resid[(2 * h + 1) * rows : (2 * h + 2) * rows]
        resid_ref[:, h * LANES : (h + 1) * LANES] = jnp.where(low_rows, first, second)
    grad_intensity = resid * steepness * resist * (1.0 - resist)

    lanes = lane_iota((rows, LANES))
    middle = (lanes >= HALF) & (lanes < HALF + BLK)
    left = lanes < HALF
    nothing = jnp.zeros((rows, LANES), jnp.float32)
    for k in range(MODES):
        g = 2.0 * weight_ref[k] * grad_intensity * fields[k]
        r31 = pltpu.roll(g, HALF, 1)
        r95 = pltpu.roll(g, HALF + BLK, 1)

        def part(v, b):
            return v[b * rows : (b + 1) * rows] if 0 <= b < NBLK else nothing

        parts = []
        for b in range(NBLK):
            re = jnp.where(
                middle, part(r31, b), jnp.where(left, part(r95, b - 1), part(r95, b + 1))
            )
            im = jnp.where(
                middle, part(r95, b), jnp.where(left, part(r31, b - 1), part(r31, b + 1))
            )
            parts.append(jnp.concatenate([re, im], axis=1))
        gw = jnp.concatenate(parts, axis=0).astype(jnp.bfloat16)
        for t in range(TERMS):
            gy = jnp.dot(
                gw, ca_ref[k * TERMS + t], preferred_element_type=jnp.float32
            ).astype(jnp.bfloat16)
            at = (k * TERMS + t) * rows
            for b in range(NBLK):
                gys[at : at + rows, b * LANES : (b + 1) * LANES] = gy[b * rows : (b + 1) * rows]

    total = jnp.zeros((2 * EXT, NBLK * LANES), jnp.float32)
    for n in range(2 * MODES):
        total = total + jnp.dot(
            rt_ref[n], gys[n * LANES : (n + 1) * LANES, :], preferred_element_type=jnp.float32
        )
    zeros = jnp.zeros((PAD, LANES), jnp.float32)
    for h in range(2):
        v0 = total[:EXT, 2 * h * LANES : (2 * h + 1) * LANES]
        v1 = total[:EXT, (2 * h + 1) * LANES : (2 * h + 2) * LANES]
        u0 = total[EXT:, 2 * h * LANES : (2 * h + 1) * LANES]
        u1 = total[EXT:, (2 * h + 1) * LANES : (2 * h + 2) * LANES]
        grad[h, PAD : PAD + EXT, :] = jnp.where(
            low, v0 + pltpu.roll(u0, BLK, 1), pltpu.roll(v1, BLK, 1) + u1
        )
        grad[h, :PAD, :] = zeros
        grad[h, PAD + EXT :, :] = zeros

    sums = (
        (0, acc_own, PAD + HALF),
        (1, acc_above, PAD + HALF - rows),
        (2, acc_below, PAD + HALF + rows),
    )
    for _, acc, _ in sums:
        acc[...] = jnp.zeros_like(acc)

    def gather(q, carry):
        for n, acc, base in sums:
            m = ids[n, 1, q]
            top = ids[n, 2, q] + base
            col = ids[n, 3, q]
            side = col >> 7
            after = jnp.minimum(side + 1, 1)
            shift = col & 127
            patch = jnp.zeros((8, LANES), jnp.float32)
            for k in range(4):
                at = pl.ds(top + k, 8, stride=4)
                both = jnp.where(lanes8 >= shift, grad[side, at, :], grad[after, at, :])
                moved = pltpu.roll(both, (LANES + 32 * k - shift) & 127, 1)
                patch = jnp.where((lanes8 >= 32 * k) & (lanes8 < 32 * k + MS), moved, patch)
            acc[m] += patch
        return carry

    lax.fori_loop(0, places, gather, 0, unroll=8)
    grads_ref[...] = (acc_own[...] + acc_above[...] + acc_below[...]).reshape(grads_ref.shape)


def main_step(weights, gathered, target, bands):
    devices, slabs = gathered.shape[:2]
    count = slabs - 1
    vmem = pl.BlockSpec(memory_space=pltpu.VMEM)
    accumulator = pltpu.VMEM((devices * count, 8, LANES), jnp.float32)
    return pl.pallas_call(
        functools.partial(main_kernel, devices),
        out_shape=(
            jax.ShapeDtypeStruct(target.shape, jnp.float32),
            pltpu.VMEM((devices, count, 8, LANES), jnp.float32),
        ),
        in_specs=[pl.BlockSpec(memory_space=pltpu.SMEM)] + [vmem] * 6,
        out_specs=[vmem] * 2,
        scratch_shapes=[
            pltpu.VMEM((3, CROWS, LANES), jnp.float32),
            pltpu.VMEM((3, CROWS, LANES), jnp.float32),
            pltpu.VMEM((3, CROWS, LANES), jnp.float32),
            pltpu.VMEM((EXT, NBLK * LANES), jnp.bfloat16),
            pltpu.VMEM((MODES, NBLK * BLK, LANES), jnp.float32),
            pltpu.VMEM((MODES * TERMS * BLK, NBLK * LANES), jnp.bfloat16),
            pltpu.VMEM((2, 2 * PAD + EXT, LANES), jnp.float32),
            accumulator,
            accumulator,
            accumulator,
            pltpu.VMEM((3, 8, LANES), jnp.int32),
            pltpu.SMEM((3, 8, LANES), jnp.int32),
            pltpu.SemaphoreType.DMA,
        ],
        compiler_params=pltpu.CompilerParams(vmem_limit_bytes=24 << 20),
        name="imaging",
    )(weights, in_vmem(gathered.reshape(devices * slabs, 8, LANES)), target, *[in_vmem(b) for b in bands])


def pack_kernel(masters_ref, owner_ref, local_ref, row_ref, col_ref, out_ref, spread):
    count = masters_ref.shape[0]
    for s in range(8):
        spread[pl.ds(s, count, stride=8), :] = masters_ref[:, s * LANES : (s + 1) * LANES]
    spread[8 * count :, :] = jnp.zeros((8, LANES), jnp.float32)
    for n, ref in enumerate((owner_ref, local_ref, row_ref, col_ref)):
        spread[8 * count + n : 8 * count + n + 1, :] = ref[...].astype(jnp.float32)
    out_ref[...] = spread[...].reshape(out_ref.shape).astype(jnp.bfloat16)


def pack(masters, *places):
    count = masters.shape[0]
    vmem = pl.BlockSpec(memory_space=pltpu.VMEM)
    return pl.pallas_call(
        pack_kernel,
        out_shape=pltpu.VMEM((1, count + 1, 8, LANES), jnp.bfloat16),
        in_specs=[vmem] * 5,
        out_specs=vmem,
        scratch_shapes=[pltpu.VMEM((8 * count + 8, LANES), jnp.float32)],
        compiler_params=pltpu.CompilerParams(vmem_limit_bytes=4 << 20),
        name="pack",
    )(in_hbm(masters), *[in_hbm(p.reshape(1, LANES)) for p in places])


def update_kernel(kept_ref, sent_ref, velocity_ref, masters_ref, velocity_out, masters_out, sums):
    count = velocity_ref.shape[0]
    sums[...] = (kept_ref[0] + sent_ref[0]).reshape(count * 8, LANES)
    for s in range(8):
        at = slice(s * LANES, (s + 1) * LANES)
        gradient = sums[pl.ds(s, count, stride=8), :]
        velocity = momentum * velocity_ref[:, at] + gradient
        velocity_out[:, at] = velocity
        masters_out[:, at] = masters_ref[:, at] - step_size * velocity


def update(kept, sent, velocity, masters):
    vmem = pl.BlockSpec(memory_space=pltpu.VMEM)
    return pl.pallas_call(
        update_kernel,
        out_shape=(jax.ShapeDtypeStruct(velocity.shape, jnp.float32),) * 2,
        in_specs=[vmem] * 4,
        out_specs=[vmem] * 2,
        scratch_shapes=[pltpu.VMEM((8 * velocity.shape[0], LANES), jnp.float32)],
        compiler_params=pltpu.CompilerParams(vmem_limit_bytes=4 << 20),
        name="update",
    )(kept, sent, velocity, masters)


def swap(value, bit, devices):
    return lax.ppermute(value, "tx", [(i, i ^ bit) for i in range(devices)])


def on_device(
    masters,
    velocity,
    place_owner,
    place_local,
    place_row,
    place_col,
    row_taps,
    col_taps,
    mode_weights,
    target,
):
    devices = lax.axis_size("tx")
    bits = devices.bit_length() - 1
    held = pack(masters, place_owner, place_local, place_row, place_col)
    stages = []
    for b in range(bits):
        held = jnp.concatenate([held, swap(held, 1 << b, devices)], axis=0)
        stages.append(held)
    bands = build_bands(row_taps, col_taps, stages[-4:-1])
    resid, grads = main_step(mode_weights, held, target, bands)
    for b in range(bits):
        half = grads.shape[0] // 2
        sent = swap(grads[half:], 1 << b, devices)
        if b < bits - 1:
            grads = grads[:half] + sent
    velocity_new, masters_new = update(grads, sent, velocity, masters)
    return resid, velocity_new, masters_new


def solution(mesh):
    return jax.shard_map(
        on_device,
        mesh=mesh,
        in_specs=(
            P(("groups", "tx"), None),
            P(("groups", "tx"), None),
            P(("groups", "tx"), None),
            P(("groups", "tx")),
            P(("groups", "tx")),
            P(("groups", "tx")),
            P(),
            P(),
            P(),
            P(("groups", "tx"), None),
        ),
        out_specs=(P(("groups", "tx"), None), P(("groups", "tx"), None), P(("groups", "tx"), None)),
        check_vma=False,
    )
```

```python
import functools
import jax
import jax.numpy as jnp
from jax import lax
from jax.experimental import pallas as pl
from jax.experimental.pallas import tpu as pltpu
from jax.sharding import PartitionSpec as P

W = 256
MS = 32
TAPS = 63
HALF = 31
TERMS = 4
MODES = 12
CH = 2 * TERMS
LANES = 128
BLK = 64
STEP = 32
NBLK = W // BLK
EXT = 128
PAD = 40
CROWS = 72
GROWS = 2 * PAD + EXT

steepness = 0.5
threshold = 8.0
momentum = 0.9
step_size = 0.05


def in_vmem(x):
    return pltpu.with_memory_space_constraint(x, pltpu.VMEM)


def in_hbm(x):
    return pltpu.with_memory_space_constraint(x, pltpu.HBM)


def lane_iota(shape):
    return lax.broadcasted_iota(jnp.int32, shape, len(shape) - 1)


def skew(row, shift):
    return pltpu.roll(
        jnp.broadcast_to(row, (BLK, LANES)), shift, 1, stride=1, stride_axis=0
    )


def pair(first, second):
    return (skew(first, 0), skew(first, BLK), skew(second, 0), skew(second, BLK))


def half_band(x):
    return x.astype(jnp.bfloat16)


def low_lanes():
    return lane_iota((BLK, LANES)) < BLK


def row_bands_kernel(row_ref, col_ref, r_ref, taps):
    count = MODES * CH
    taps[...] = jnp.zeros_like(taps)
    for k in range(MODES):
        for t in range(TERMS):
            at = k * CH + 2 * t
            taps[at : at + 2, :TAPS] = row_ref[k, t].astype(jnp.float32)
            taps[count + at : count + at + 2, :TAPS] = col_ref[k, t].astype(jnp.float32)
    source = lax.broadcasted_iota(jnp.int32, (LANES, LANES), 0)
    mirror = (source + lane_iota((LANES, LANES))) % LANES == 0
    taps[2 * count :, :] = jnp.dot(
        taps[: 2 * count, :].astype(jnp.bfloat16),
        mirror.astype(jnp.bfloat16),
        preferred_element_type=jnp.float32,
    )
    taps[count : 2 * count, :] = pltpu.roll(taps[count : 2 * count, :], LANES - (TAPS - 1), 1)

    def step(n, carry):
        for f in range(4):
            at = n * 4 + f
            r_ref[pl.ds(at * BLK, BLK), :] = half_band(skew(taps[pl.ds(at, 1), :], 0))
        return carry

    lax.fori_loop(0, 2 * MODES, step, 0, unroll=3)


def row_adjoint_kernel(taps, _, rt_ref):
    count = MODES * CH
    low = low_lanes()

    def step(n, carry):
        first = 2 * count + 4 * n
        for par in range(2):
            a, a_far, b, b_far = pair(
                taps[pl.ds(first + par, 1), :], taps[pl.ds(first + 2 + par, 1), :]
            )
            rt_ref[n, par * EXT : par * EXT + BLK, :] = half_band(jnp.where(low, a, b_far))
            rt_ref[n, par * EXT + BLK : (par + 1) * EXT, :] = half_band(jnp.where(low, a_far, b))
        return carry

    lax.fori_loop(0, 2 * MODES, step, 0, unroll=3)


def column_bands_kernel(taps, _, cf_ref):
    count = MODES * CH
    low = low_lanes()

    def step(n, carry):
        first = 3 * count + 4 * n
        for t in range(2):
            at = t * 2 * EXT
            a, a_far, b, b_far = pair(
                taps[pl.ds(first + 2 * t, 1), :], taps[pl.ds(first + 2 * t + 1, 1), :]
            )
            cf_ref[n, at : at + BLK, :] = half_band(jnp.where(low, a, b_far))
            cf_ref[n, at + BLK : at + EXT, :] = half_band(jnp.where(low, a_far, b))
            cf_ref[n, at + EXT : at + EXT + BLK, :] = half_band(jnp.where(low, -b, a_far))
            cf_ref[n, at + EXT + BLK : at + 2 * EXT, :] = half_band(jnp.where(low, -b_far, a))
        return carry

    lax.fori_loop(0, 2 * MODES, step, 0, unroll=3)


def column_adjoint_kernel(taps, _, ca_ref):
    count = MODES * CH
    low = low_lanes()

    def step(n, carry):
        first = count + 4 * n
        for t in range(2):
            a, a_far, b, b_far = pair(
                taps[pl.ds(first + 2 * t, 1), :], taps[pl.ds(first + 2 * t + 1, 1), :]
            )
            ca_ref[n * 2 + t, :BLK, :] = half_band(jnp.where(low, a, -b_far))
            ca_ref[n * 2 + t, BLK:EXT, :] = half_band(jnp.where(low, a_far, -b))
            ca_ref[n * 2 + t, EXT : EXT + BLK, :] = half_band(jnp.where(low, b, a_far))
            ca_ref[n * 2 + t, EXT + BLK :, :] = half_band(jnp.where(low, b_far, a))
        return carry

    lax.fori_loop(0, 2 * MODES, step, 0, unroll=3)


def build_bands(row_taps, col_taps, stages):
    vmem = pl.BlockSpec(memory_space=pltpu.VMEM)
    small = pltpu.CompilerParams(vmem_limit_bytes=4 << 20)
    r, taps = pl.pallas_call(
        row_bands_kernel,
        out_shape=(
            pltpu.VMEM((MODES * CH * BLK, LANES), jnp.bfloat16),
            pltpu.VMEM((4 * MODES * CH, LANES), jnp.float32),
        ),
        in_specs=[vmem] * 2,
        out_specs=[vmem] * 2,
        compiler_params=small,
        name="row_bands",
    )(in_hbm(row_taps), in_hbm(col_taps))
    taps = in_vmem(taps)
    built = [
        pl.pallas_call(
            kernel,
            out_shape=pltpu.VMEM(shape, jnp.bfloat16),
            in_specs=[vmem, pl.BlockSpec(memory_space=pl.ANY)],
            out_specs=vmem,
            compiler_params=small,
            name=name,
        )(taps, stage)
        for stage, (kernel, shape, name) in zip(
            stages,
            (
                (column_bands_kernel, (2 * MODES, CH * EXT // 2, LANES), "column_bands"),
                (row_adjoint_kernel, (2 * MODES, 2 * EXT, LANES), "row_adjoint"),
                (column_adjoint_kernel, (4 * MODES, 2 * EXT, LANES), "column_adjoint"),
            ),
        )
    ]
    return [r, built[1], built[0], built[2]]


def reversed_bits(value, bits):
    return sum(((value >> b) & 1) << (bits - 1 - b) for b in range(bits))


def main_kernel(
    devices,
    weight_ref,
    gathered_ref,
    target_ref,
    r_ref,
    rt_ref,
    cf_ref,
    ca_ref,
    resid_ref,
    grads_ref,
    *scratch,
):
    canvases = (scratch[0:4], scratch[4:8], scratch[8:12])
    grads = scratch[12:16]
    sums = scratch[16:19]
    window, lhs, fields, slope, gw, gys, table, ids, sem = scratch[19:]
    slabs = gathered_ref.shape[0] // devices
    count = slabs - 1
    places = LANES
    rows = BLK
    me = lax.axis_index("tx")
    bits = devices.bit_length() - 1
    bases = (PAD + HALF, PAD + HALF - rows, PAD + HALF + rows)
    for n, (other, missing) in enumerate(
        ((me, 0), (jnp.maximum(me - 1, 0), 0), (jnp.minimum(me + 1, devices - 1), BLK - MS))
    ):
        slab = gathered_ref[(other ^ me) * slabs + count].astype(jnp.float32).astype(jnp.int32)
        owner, local, row, col = slab[0:1] ^ me, slab[1:2], slab[2:3], slab[3:4]
        if n:
            row = jnp.where(other == me, missing, row)
        lines = jnp.concatenate(
            [
                owner * slabs + local,
                reversed_bits(owner, bits) * count + local,
                ((col + HALF) >> 7) * CROWS + row + 7,
                (col + HALF) & 127,
                (col >> 7) * GROWS + row + bases[n],
                col & 127,
                (LANES - (col & 127)) & 127,
                row,
            ],
            axis=0,
        )
        for j in range(places // STEP):
            table[j, 8 * n : 8 * n + 8, :] = (
                pltpu.roll(lines, LANES - STEP * j, 1) if j else lines
            )[:, :STEP]
    to_scalar = pltpu.make_async_copy(table, ids, sem)
    to_scalar.start()
    for group in canvases:
        for canvas in group:
            canvas[...] = jnp.zeros_like(canvas)
    for acc in sums:
        acc[...] = jnp.zeros_like(acc)
    lanes8 = lane_iota((8, LANES))
    to_scalar.wait()

    def place(j, u):
        for n, group in enumerate(canvases):
            at, shift = ids[j, 8 * n + 2, u], ids[j, 8 * n + 3, u]
            moved = pltpu.roll(gathered_ref[ids[j, 8 * n, u]].astype(jnp.float32), shift, 1)
            ahead = lanes8 - shift
            here = ahead >= 0
            nth = (ahead & 127) >> 5
            near, far = jnp.where(here, moved, 0.0), jnp.where(here, 0.0, moved)
            for k, canvas in enumerate(group):
                spot = pl.ds(at + k, 8, stride=4)
                spot_far = pl.ds(at + k + CROWS, 8, stride=4)
                mine = nth == k
                old, old_far = canvas[spot, :], canvas[spot_far, :]
                canvas[spot, :] = old + jnp.where(mine, near, 0.0)
                canvas[spot_far, :] = old_far + jnp.where(mine, far, 0.0)

    @pl.loop(0, places // STEP)
    def _(j):
        for u in range(STEP):
            place(j, u)


    lanes_ext = lane_iota((EXT, LANES))
    parts = [
        [
            jnp.concatenate(
                [
                    above[h * CROWS + 40 : h * CROWS + 64],
                    above[h * CROWS + 64 : (h + 1) * CROWS] + own[h * CROWS : h * CROWS + 8],
                    own[h * CROWS + 8 : h * CROWS + 64],
                    own[h * CROWS + 64 : (h + 1) * CROWS] + below[h * CROWS : h * CROWS + 8],
                    below[h * CROWS + 8 : h * CROWS + 40],
                ],
                axis=0,
            )
            for h in range(3)
        ]
        for own, above, below in zip(*canvases)
    ]
    sides = [parts[0][h] for h in range(3)]
    for k in range(1, 4):
        back = [pltpu.roll(part, LANES - MS * k, 1) for part in parts[k]]
        for h in range(3):
            after = back[h + 1] if h < 2 else 0.0
            sides[h] = sides[h] + jnp.where(lanes_ext < LANES - MS * k, back[h], after)
    low = lanes_ext < BLK
    turned = [pltpu.roll(side, BLK, 1) for side in sides]
    window[:, 0:128] = sides[0].astype(jnp.bfloat16)
    window[:, 128:256] = jnp.where(low, turned[0], turned[1]).astype(jnp.bfloat16)
    window[:, 256:384] = sides[1].astype(jnp.bfloat16)
    window[:, 384:512] = jnp.where(low, turned[1], turned[2]).astype(jnp.bfloat16)

    lanes16 = lane_iota((16, LANES))
    before = lanes16 < HALF
    until = lanes16 < HALF + BLK
    intensity = jnp.zeros((NBLK * rows, LANES), jnp.float32)
    for k in range(MODES):
        field_y = jnp.dot(
            r_ref[k * CH * rows : (k + 1) * CH * rows, :],
            window[...],
            preferred_element_type=jnp.float32,
        ).astype(jnp.bfloat16)
        for c in range(CH):
            for b in range(NBLK):
                lhs[k % 2, b * rows : (b + 1) * rows, c * LANES : (c + 1) * LANES] = field_y[
                    c * rows : (c + 1) * rows, b * LANES : (b + 1) * LANES
                ]
        e = jnp.dot(
            lhs[k % 2],
            jnp.concatenate([cf_ref[2 * k], cf_ref[2 * k + 1]], axis=0),
            preferred_element_type=jnp.float32,
        )
        fields[k] = e
        intensity = intensity + weight_ref[k] * (e * e)
    low_rows = lane_iota((rows, LANES)) < BLK
    resids = []
    for b in range(NBLK):
        inten = intensity[b * rows : (b + 1) * rows]
        inten = inten + pltpu.roll(inten, BLK, 1)
        t = target_ref[:, (b // 2) * LANES : (b // 2 + 1) * LANES].astype(jnp.float32)
        other = pltpu.roll(t, BLK, 1)
        goal = jnp.where(low_rows, t, other) if b % 2 == 0 else jnp.where(low_rows, other, t)
        resist = jax.nn.sigmoid(steepness * (inten - threshold))
        resid = resist - goal
        slope[b * rows : (b + 1) * rows, :] = 2.0 * (resid * steepness * resist * (1.0 - resist))
        if b % 2 == 0:
            resid_ref[:, (b // 2) * LANES : (b // 2 + 1) * LANES] = resid
        else:
            resid_ref[:, (b // 2) * LANES + BLK : (b // 2 + 1) * LANES] = resid[:, BLK:]

    nothing = jnp.zeros((16, LANES), jnp.float32)
    for k in range(MODES):
        weight = weight_ref[k]
        for i in range(0, rows, 16):
            r31, r95 = [nothing], [nothing]
            for b in range(NBLK):
                at = slice(b * rows + i, b * rows + i + 16)
                g = weight * slope[at, :] * fields[k, at, :]
                r31.append(pltpu.roll(g, HALF, 1))
                r95.append(pltpu.roll(g, HALF + BLK, 1))
            r31.append(nothing)
            r95.append(nothing)
            for b in range(NBLK):
                at = slice(b * rows + i, b * rows + i + 16)
                re = jnp.where(before, r95[b], jnp.where(until, r31[b + 1], r95[b + 2]))
                im = jnp.where(before, r31[b], jnp.where(until, r95[b + 1], r31[b + 2]))
                gw[k % 2, at, :LANES] = re.astype(jnp.bfloat16)
                gw[k % 2, at, LANES:] = im.astype(jnp.bfloat16)
        for t in range(TERMS):
            gy = jnp.dot(
                gw[k % 2], ca_ref[k * TERMS + t], preferred_element_type=jnp.float32
            ).astype(jnp.bfloat16)
            at = (k * TERMS + t) * rows
            for b in range(NBLK):
                gys[at : at + rows, b * LANES : (b + 1) * LANES] = gy[b * rows : (b + 1) * rows]

    total = jnp.zeros((2 * EXT, NBLK * LANES), jnp.float32)
    for k in range(MODES):
        total = total + jnp.dot(
            jnp.concatenate([rt_ref[2 * k], rt_ref[2 * k + 1]], axis=1),
            gys[2 * k * LANES : 2 * (k + 1) * LANES, :],
            preferred_element_type=jnp.float32,
        )
    whole = []
    for h in range(2):
        v0 = total[:EXT, 2 * h * LANES : (2 * h + 1) * LANES]
        v1 = total[:EXT, (2 * h + 1) * LANES : (2 * h + 2) * LANES]
        u0 = total[EXT:, 2 * h * LANES : (2 * h + 1) * LANES]
        u1 = total[EXT:, (2 * h + 1) * LANES : (2 * h + 2) * LANES]
        whole.append(
            jnp.where(low, v0 + pltpu.roll(u0, BLK, 1), pltpu.roll(v1, BLK, 1) + u1)
        )
    zeros = jnp.zeros((PAD, LANES), jnp.float32)
    for k, grad in enumerate(grads):
        ahead = [pltpu.roll(side, MS * k, 1) if k else side for side in whole]
        for h in range(3):
            here = ahead[h] if h < 2 else 0.0
            behind = ahead[h - 1] if h else 0.0
            base = h * GROWS
            grad[base : base + PAD, :] = zeros
            grad[base + PAD : base + PAD + EXT, :] = jnp.where(lanes_ext >= MS * k, here, behind)
            grad[base + PAD + EXT : base + GROWS, :] = zeros

    def gather(j, u):
        for n, acc in enumerate(sums):
            m, at, shift, back = [ids[j, 8 * n + line, u] for line in (1, 4, 5, 6)]
            ahead = lanes8 - shift
            here = ahead >= 0
            nth = ahead & 127
            patch = None
            for k, grad in enumerate(grads):
                both = jnp.where(
                    here,
                    grad[pl.ds(at + k, 8, stride=4), :],
                    grad[pl.ds(at + k + GROWS, 8, stride=4), :],
                )
                patch = jnp.where(nth >= MS * k, both, patch) if k else both
            acc[m] += pltpu.roll(patch, back, 1)

    @pl.loop(0, places // STEP)
    def _(j):
        for u in range(STEP):
            gather(j, u)

    grads_ref[...] = (sums[0][...] + sums[1][...] + sums[2][...]).reshape(grads_ref.shape)


def main_step(weights, gathered, target, bands):
    devices, slabs = gathered.shape[:2]
    count = slabs - 1
    vmem = pl.BlockSpec(memory_space=pltpu.VMEM)
    return pl.pallas_call(
        functools.partial(main_kernel, devices),
        out_shape=(
            jax.ShapeDtypeStruct(target.shape, jnp.float32),
            pltpu.VMEM((devices, count, 8, LANES), jnp.float32),
        ),
        in_specs=[pl.BlockSpec(memory_space=pltpu.SMEM)] + [vmem] * 6,
        out_specs=[vmem] * 2,
        scratch_shapes=[
            *[pltpu.VMEM((3 * CROWS, LANES), jnp.float32)] * 12,
            *[pltpu.VMEM((3 * GROWS, LANES), jnp.float32)] * 4,
            *[pltpu.VMEM((devices * count, 8, LANES), jnp.float32)] * 3,
            pltpu.VMEM((EXT, NBLK * LANES), jnp.bfloat16),
            pltpu.VMEM((2, NBLK * BLK, CH * LANES), jnp.bfloat16),
            pltpu.VMEM((MODES, NBLK * BLK, LANES), jnp.float32),
            pltpu.VMEM((NBLK * BLK, LANES), jnp.float32),
            pltpu.VMEM((2, NBLK * BLK, 2 * LANES), jnp.bfloat16),
            pltpu.VMEM((MODES * TERMS * BLK, NBLK * LANES), jnp.bfloat16),
            pltpu.VMEM((LANES // STEP, 24, STEP), jnp.int32),
            pltpu.SMEM((LANES // STEP, 24, STEP), jnp.int32),
            pltpu.SemaphoreType.DMA,
        ],
        compiler_params=pltpu.CompilerParams(vmem_limit_bytes=24 << 20),
        name="imaging",
    )(weights, in_vmem(gathered.reshape(devices * slabs, 8, LANES)), target, *[in_vmem(b) for b in bands])


def pack_kernel(masters_ref, owner_ref, local_ref, row_ref, col_ref, out_ref, spread):
    count = masters_ref.shape[0]
    for s in range(8):
        spread[pl.ds(s, count, stride=8), :] = masters_ref[:, s * LANES : (s + 1) * LANES]
    spread[8 * count :, :] = jnp.zeros((8, LANES), jnp.float32)
    for n, ref in enumerate((owner_ref, local_ref, row_ref, col_ref)):
        spread[8 * count + n : 8 * count + n + 1, :] = ref[...].astype(jnp.float32)
    out_ref[...] = spread[...].reshape(out_ref.shape).astype(jnp.bfloat16)


def pack(masters, *places):
    count = masters.shape[0]
    vmem = pl.BlockSpec(memory_space=pltpu.VMEM)
    return pl.pallas_call(
        pack_kernel,
        out_shape=pltpu.VMEM((1, count + 1, 8, LANES), jnp.bfloat16),
        in_specs=[vmem] * 5,
        out_specs=vmem,
        scratch_shapes=[pltpu.VMEM((8 * count + 8, LANES), jnp.float32)],
        compiler_params=pltpu.CompilerParams(vmem_limit_bytes=4 << 20),
        name="pack",
    )(in_hbm(masters), *[in_hbm(p.reshape(1, LANES)) for p in places])


def update_kernel(kept_ref, sent_ref, velocity_ref, masters_ref, velocity_out, masters_out, sums):
    count = velocity_ref.shape[0]
    sums[...] = (kept_ref[0] + sent_ref[0]).reshape(count * 8, LANES)
    for s in range(8):
        at = slice(s * LANES, (s + 1) * LANES)
        gradient = sums[pl.ds(s, count, stride=8), :]
        velocity = momentum * velocity_ref[:, at] + gradient
        velocity_out[:, at] = velocity
        masters_out[:, at] = masters_ref[:, at] - step_size * velocity


def update(kept, sent, velocity, masters):
    vmem = pl.BlockSpec(memory_space=pltpu.VMEM)
    return pl.pallas_call(
        update_kernel,
        out_shape=(jax.ShapeDtypeStruct(velocity.shape, jnp.float32),) * 2,
        in_specs=[vmem] * 4,
        out_specs=[vmem] * 2,
        scratch_shapes=[pltpu.VMEM((8 * velocity.shape[0], LANES), jnp.float32)],
        compiler_params=pltpu.CompilerParams(vmem_limit_bytes=4 << 20),
        name="update",
    )(kept, sent, velocity, masters)


def swap(value, bit, devices):
    return lax.ppermute(value, "tx", [(i, i ^ bit) for i in range(devices)])


def on_device(
    masters,
    velocity,
    place_owner,
    place_local,
    place_row,
    place_col,
    row_taps,
    col_taps,
    mode_weights,
    target,
):
    devices = lax.axis_size("tx")
    bits = devices.bit_length() - 1
    held = pack(masters, place_owner, place_local, place_row, place_col)
    stages = []
    for b in range(bits):
        held = jnp.concatenate([held, swap(held, 1 << b, devices)], axis=0)
        stages.append(held)
    bands = build_bands(row_taps, col_taps, stages[-4:-1])
    resid, grads = main_step(mode_weights, held, target, bands)
    for b in range(bits):
        half = grads.shape[0] // 2
        sent = swap(grads[half:], 1 << b, devices)
        if b < bits - 1:
            grads = grads[:half] + sent
    velocity_new, masters_new = update(grads, sent, velocity, masters)
    return resid, velocity_new, masters_new


def solution(mesh):
    return jax.shard_map(
        on_device,
        mesh=mesh,
        in_specs=(
            P(("groups", "tx"), None),
            P(("groups", "tx"), None),
            P(("groups", "tx"), None),
            P(("groups", "tx")),
            P(("groups", "tx")),
            P(("groups", "tx")),
            P(),
            P(),
            P(),
            P(("groups", "tx"), None),
        ),
        out_specs=(P(("groups", "tx"), None), P(("groups", "tx"), None), P(("groups", "tx"), None)),
        check_vma=False,
    )
```

```python
import functools
import jax
import jax.numpy as jnp
from jax import lax
from jax.experimental import pallas as pl
from jax.experimental.pallas import tpu as pltpu
from jax.sharding import PartitionSpec as P

W = 256
MS = 32
TAPS = 63
HALF = 31
TERMS = 4
MODES = 12
CH = 2 * TERMS
LANES = 128
BLK = 64
EXT = 128
STEP = 32
GROUP = 4
BANDS = (
    (MODES * CH * BLK, LANES),
    (2 * MODES, 2 * EXT, LANES),
    (2 * MODES, CH * EXT // 2, LANES),
    (4 * MODES, 2 * EXT, LANES),
)
NBLK = W // BLK
PAD = 40
CROWS = 72
GROWS = 2 * PAD + EXT

steepness = 0.5
threshold = 8.0
momentum = 0.9
step_size = 0.05


def in_vmem(x):
    return pltpu.with_memory_space_constraint(x, pltpu.VMEM)


def in_hbm(x):
    return pltpu.with_memory_space_constraint(x, pltpu.HBM)


def lane_iota(shape):
    return lax.broadcasted_iota(jnp.int32, shape, len(shape) - 1)


def skew(row, shift):
    return pltpu.roll(
        jnp.broadcast_to(row, (BLK, LANES)), shift, 1, stride=1, stride_axis=0
    )


def pair(first, second):
    return (skew(first, 0), skew(first, BLK), skew(second, 0), skew(second, BLK))


def half_band(x):
    return x.astype(jnp.bfloat16)


def low_lanes():
    return lane_iota((BLK, LANES)) < BLK


def fill_taps(row_ref, col_ref, taps):
    count = MODES * CH
    taps[...] = jnp.zeros_like(taps)
    for k in range(MODES):
        for t in range(TERMS):
            at = k * CH + 2 * t
            taps[at : at + 2, :TAPS] = row_ref[k, t].astype(jnp.float32)
            taps[count + at : count + at + 2, :TAPS] = col_ref[k, t].astype(jnp.float32)
    source = lax.broadcasted_iota(jnp.int32, (LANES, LANES), 0)
    mirror = (source + lane_iota((LANES, LANES))) % LANES == 0
    taps[2 * count :, :] = jnp.dot(
        taps[: 2 * count, :].astype(jnp.bfloat16),
        mirror.astype(jnp.bfloat16),
        preferred_element_type=jnp.float32,
    )
    taps[count : 2 * count, :] = pltpu.roll(taps[count : 2 * count, :], LANES - (TAPS - 1), 1)


def bands_kernel(row_ref, col_ref, r_ref, rt_ref, cf_ref, ca_ref, taps):
    count = MODES * CH

    @pl.when(pl.program_id(0) == 0)
    def _():
        fill_taps(row_ref, col_ref, taps)

    low = low_lanes()

    def step(n, carry):
        first = (pl.program_id(0) * GROUP + n) * 4
        for f in range(4):
            r_ref[pl.ds((4 * n + f) * BLK, BLK), :] = half_band(
                skew(taps[pl.ds(first + f, 1), :], 0)
            )
        for par in range(2):
            a, a_far, b, b_far = pair(
                taps[pl.ds(2 * count + first + par, 1), :],
                taps[pl.ds(2 * count + first + 2 + par, 1), :],
            )
            rt_ref[n, par * EXT : par * EXT + BLK, :] = half_band(jnp.where(low, a, b_far))
            rt_ref[n, par * EXT + BLK : (par + 1) * EXT, :] = half_band(jnp.where(low, a_far, b))
        for t in range(2):
            at = t * 2 * EXT
            a, a_far, b, b_far = pair(
                taps[pl.ds(3 * count + first + 2 * t, 1), :],
                taps[pl.ds(3 * count + first + 2 * t + 1, 1), :],
            )
            cf_ref[n, at : at + BLK, :] = half_band(jnp.where(low, a, b_far))
            cf_ref[n, at + BLK : at + EXT, :] = half_band(jnp.where(low, a_far, b))
            cf_ref[n, at + EXT : at + EXT + BLK, :] = half_band(jnp.where(low, -b, a_far))
            cf_ref[n, at + EXT + BLK : at + 2 * EXT, :] = half_band(jnp.where(low, -b_far, a))
            a, a_far, b, b_far = pair(
                taps[pl.ds(count + first + 2 * t, 1), :],
                taps[pl.ds(count + first + 2 * t + 1, 1), :],
            )
            ca_ref[n * 2 + t, :BLK, :] = half_band(jnp.where(low, a, -b_far))
            ca_ref[n * 2 + t, BLK:EXT, :] = half_band(jnp.where(low, a_far, -b))
            ca_ref[n * 2 + t, EXT : EXT + BLK, :] = half_band(jnp.where(low, b, a_far))
            ca_ref[n * 2 + t, EXT + BLK :, :] = half_band(jnp.where(low, b_far, a))
        return carry

    lax.fori_loop(0, GROUP, step, 0)


def build_bands(row_taps, col_taps):
    vmem = pl.BlockSpec(memory_space=pltpu.VMEM)
    return pl.pallas_call(
        bands_kernel,
        grid=(2 * MODES // GROUP,),
        out_shape=[pltpu.HBM(shape, jnp.bfloat16) for shape in BANDS],
        in_specs=[vmem] * 2,
        out_specs=[
            pl.BlockSpec((4 * GROUP * BLK, LANES), lambda n: (n, 0)),
            pl.BlockSpec((GROUP, 2 * EXT, LANES), lambda n: (n, 0, 0)),
            pl.BlockSpec((GROUP, CH * EXT // 2, LANES), lambda n: (n, 0, 0)),
            pl.BlockSpec((2 * GROUP, 2 * EXT, LANES), lambda n: (n, 0, 0)),
        ],
        scratch_shapes=[pltpu.VMEM((4 * MODES * CH, LANES), jnp.float32)],
        compiler_params=pltpu.CompilerParams(vmem_limit_bytes=8 << 20),
        name="bands",
    )(in_hbm(row_taps), in_hbm(col_taps))


def reversed_bits(value, bits):
    return sum(((value >> b) & 1) << (bits - 1 - b) for b in range(bits))


def main_kernel(
    devices,
    weight_ref,
    gathered_ref,
    target_ref,
    r_hbm,
    rt_hbm,
    cf_hbm,
    ca_hbm,
    resid_ref,
    grads_ref,
    *scratch,
):
    canvases = (scratch[0:4], scratch[4:8], scratch[8:12])
    grads = scratch[12:16]
    sums = scratch[16:19]
    window, lhs, fields, slope, gw, gys, table, ids, sem = scratch[19:28]
    r_ref, rt_ref, cf_ref, ca_ref, band_sems = scratch[28:]
    loads = [
        pltpu.make_async_copy(source, target, band_sems.at[n])
        for n, (source, target) in enumerate(
            ((r_hbm, r_ref), (cf_hbm, cf_ref), (ca_hbm, ca_ref), (rt_hbm, rt_ref))
        )
    ]
    slabs = gathered_ref.shape[0] // devices
    count = slabs - 1
    places = LANES
    rows = BLK
    me = lax.axis_index("tx")
    bits = devices.bit_length() - 1
    bases = (PAD + HALF, PAD + HALF - rows, PAD + HALF + rows)
    for n, (other, missing) in enumerate(
        ((me, 0), (jnp.maximum(me - 1, 0), 0), (jnp.minimum(me + 1, devices - 1), BLK - MS))
    ):
        slab = gathered_ref[other * slabs + count].astype(jnp.float32).astype(jnp.int32)
        owner, local, row, col = slab[0:1], slab[1:2], slab[2:3], slab[3:4]
        if n:
            row = jnp.where(other == me, missing, row)
        lines = jnp.concatenate(
            [
                owner * slabs + local,
                reversed_bits(owner ^ me, bits) * count + local,
                ((col + HALF) >> 7) * CROWS + row + 7,
                (col + HALF) & 127,
                (col >> 7) * GROWS + row + bases[n],
                col & 127,
                (LANES - (col & 127)) & 127,
                row,
            ],
            axis=0,
        )
        for j in range(places // STEP):
            table[j, 8 * n : 8 * n + 8, :] = (
                pltpu.roll(lines, LANES - STEP * j, 1) if j else lines
            )[:, :STEP]
    to_scalar = pltpu.make_async_copy(table, ids, sem)
    to_scalar.start()
    for load in loads:
        load.start()
    for group in canvases:
        for canvas in group:
            canvas[...] = jnp.zeros_like(canvas)
    for acc in sums:
        acc[...] = jnp.zeros_like(acc)
    lanes8 = lane_iota((8, LANES))
    to_scalar.wait()

    def place(j, u):
        for n, group in enumerate(canvases):
            at, shift = ids[j, 8 * n + 2, u], ids[j, 8 * n + 3, u]
            moved = pltpu.roll(gathered_ref[ids[j, 8 * n, u]].astype(jnp.float32), shift, 1)
            ahead = lanes8 - shift
            here = ahead >= 0
            nth = (ahead & 127) >> 5
            near, far = jnp.where(here, moved, 0.0), jnp.where(here, 0.0, moved)
            for k, canvas in enumerate(group):
                spot = pl.ds(at + k, 8, stride=4)
                spot_far = pl.ds(at + k + CROWS, 8, stride=4)
                mine = nth == k
                old, old_far = canvas[spot, :], canvas[spot_far, :]
                canvas[spot, :] = old + jnp.where(mine, near, 0.0)
                canvas[spot_far, :] = old_far + jnp.where(mine, far, 0.0)

    @pl.loop(0, places // STEP)
    def _(j):
        for u in range(STEP):
            place(j, u)


    lanes_ext = lane_iota((EXT, LANES))
    parts = [
        [
            jnp.concatenate(
                [
                    above[h * CROWS + 40 : h * CROWS + 64],
                    above[h * CROWS + 64 : (h + 1) * CROWS] + own[h * CROWS : h * CROWS + 8],
                    own[h * CROWS + 8 : h * CROWS + 64],
                    own[h * CROWS + 64 : (h + 1) * CROWS] + below[h * CROWS : h * CROWS + 8],
                    below[h * CROWS + 8 : h * CROWS + 40],
                ],
                axis=0,
            )
            for h in range(3)
        ]
        for own, above, below in zip(*canvases)
    ]
    sides = [parts[0][h] for h in range(3)]
    for k in range(1, 4):
        back = [pltpu.roll(part, LANES - MS * k, 1) for part in parts[k]]
        for h in range(3):
            after = back[h + 1] if h < 2 else 0.0
            sides[h] = sides[h] + jnp.where(lanes_ext < LANES - MS * k, back[h], after)
    low = lanes_ext < BLK
    turned = [pltpu.roll(side, BLK, 1) for side in sides]
    window[:, 0:128] = sides[0].astype(jnp.bfloat16)
    window[:, 128:256] = jnp.where(low, turned[0], turned[1]).astype(jnp.bfloat16)
    window[:, 256:384] = sides[1].astype(jnp.bfloat16)
    window[:, 384:512] = jnp.where(low, turned[1], turned[2]).astype(jnp.bfloat16)

    lanes16 = lane_iota((16, LANES))
    before = lanes16 < HALF
    until = lanes16 < HALF + BLK
    loads[0].wait()
    loads[1].wait()
    intensity = jnp.zeros((NBLK * rows, LANES), jnp.float32)
    for k in range(MODES):
        field_y = jnp.dot(
            r_ref[k * CH * rows : (k + 1) * CH * rows, :],
            window[...],
            preferred_element_type=jnp.float32,
        ).astype(jnp.bfloat16)
        for c in range(CH):
            for b in range(NBLK):
                lhs[k % 2, b * rows : (b + 1) * rows, c * LANES : (c + 1) * LANES] = field_y[
                    c * rows : (c + 1) * rows, b * LANES : (b + 1) * LANES
                ]
        e = jnp.dot(
            lhs[k % 2],
            jnp.concatenate([cf_ref[2 * k], cf_ref[2 * k + 1]], axis=0),
            preferred_element_type=jnp.float32,
        )
        fields[k] = e
        intensity = intensity + weight_ref[k] * (e * e)
    low_rows = lane_iota((rows, LANES)) < BLK
    resids = []
    for b in range(NBLK):
        inten = intensity[b * rows : (b + 1) * rows]
        inten = inten + pltpu.roll(inten, BLK, 1)
        t = target_ref[:, (b // 2) * LANES : (b // 2 + 1) * LANES].astype(jnp.float32)
        other = pltpu.roll(t, BLK, 1)
        goal = jnp.where(low_rows, t, other) if b % 2 == 0 else jnp.where(low_rows, other, t)
        resist = jax.nn.sigmoid(steepness * (inten - threshold))
        resid = resist - goal
        slope[b * rows : (b + 1) * rows, :] = 2.0 * (resid * steepness * resist * (1.0 - resist))
        if b % 2 == 0:
            resid_ref[:, (b // 2) * LANES : (b // 2 + 1) * LANES] = resid
        else:
            resid_ref[:, (b // 2) * LANES + BLK : (b // 2 + 1) * LANES] = resid[:, BLK:]

    loads[2].wait()
    nothing = jnp.zeros((16, LANES), jnp.float32)
    for k in range(MODES):
        weight = weight_ref[k]
        for i in range(0, rows, 16):
            r31, r95 = [nothing], [nothing]
            for b in range(NBLK):
                at = slice(b * rows + i, b * rows + i + 16)
                g = weight * slope[at, :] * fields[k, at, :]
                r31.append(pltpu.roll(g, HALF, 1))
                r95.append(pltpu.roll(g, HALF + BLK, 1))
            r31.append(nothing)
            r95.append(nothing)
            for b in range(NBLK):
                at = slice(b * rows + i, b * rows + i + 16)
                re = jnp.where(before, r95[b], jnp.where(until, r31[b + 1], r95[b + 2]))
                im = jnp.where(before, r31[b], jnp.where(until, r95[b + 1], r31[b + 2]))
                gw[k % 2, at, :LANES] = re.astype(jnp.bfloat16)
                gw[k % 2, at, LANES:] = im.astype(jnp.bfloat16)
        for t in range(TERMS):
            gy = jnp.dot(
                gw[k % 2], ca_ref[k * TERMS + t], preferred_element_type=jnp.float32
            ).astype(jnp.bfloat16)
            at = (k * TERMS + t) * rows
            for b in range(NBLK):
                gys[at : at + rows, b * LANES : (b + 1) * LANES] = gy[b * rows : (b + 1) * rows]

    loads[3].wait()
    total = jnp.zeros((2 * EXT, NBLK * LANES), jnp.float32)
    for k in range(MODES):
        total = total + jnp.dot(
            jnp.concatenate([rt_ref[2 * k], rt_ref[2 * k + 1]], axis=1),
            gys[2 * k * LANES : 2 * (k + 1) * LANES, :],
            preferred_element_type=jnp.float32,
        )
    whole = []
    for h in range(2):
        v0 = total[:EXT, 2 * h * LANES : (2 * h + 1) * LANES]
        v1 = total[:EXT, (2 * h + 1) * LANES : (2 * h + 2) * LANES]
        u0 = total[EXT:, 2 * h * LANES : (2 * h + 1) * LANES]
        u1 = total[EXT:, (2 * h + 1) * LANES : (2 * h + 2) * LANES]
        whole.append(
            jnp.where(low, v0 + pltpu.roll(u0, BLK, 1), pltpu.roll(v1, BLK, 1) + u1)
        )
    zeros = jnp.zeros((PAD, LANES), jnp.float32)
    for k, grad in enumerate(grads):
        ahead = [pltpu.roll(side, MS * k, 1) if k else side for side in whole]
        for h in range(3):
            here = ahead[h] if h < 2 else 0.0
            behind = ahead[h - 1] if h else 0.0
            base = h * GROWS
            grad[base : base + PAD, :] = zeros
            grad[base + PAD : base + PAD + EXT, :] = jnp.where(lanes_ext >= MS * k, here, behind)
            grad[base + PAD + EXT : base + GROWS, :] = zeros

    def gather(j, u):
        for n, acc in enumerate(sums):
            m, at, shift, back = [ids[j, 8 * n + line, u] for line in (1, 4, 5, 6)]
            ahead = lanes8 - shift
            here = ahead >= 0
            nth = ahead & 127
            patch = None
            for k, grad in enumerate(grads):
                both = jnp.where(
                    here,
                    grad[pl.ds(at + k, 8, stride=4), :],
                    grad[pl.ds(at + k + GROWS, 8, stride=4), :],
                )
                patch = jnp.where(nth >= MS * k, both, patch) if k else both
            acc[m] += pltpu.roll(patch, back, 1)

    @pl.loop(0, places // STEP)
    def _(j):
        for u in range(STEP):
            gather(j, u)

    grads_ref[...] = (sums[0][...] + sums[1][...] + sums[2][...]).reshape(grads_ref.shape)


def main_step(weights, gathered, target, bands):
    devices, slabs = gathered.shape[:2]
    count = slabs - 1
    vmem = pl.BlockSpec(memory_space=pltpu.VMEM)
    return pl.pallas_call(
        functools.partial(main_kernel, devices),
        out_shape=(
            jax.ShapeDtypeStruct(target.shape, jnp.float32),
            pltpu.VMEM((devices, count, 8, LANES), jnp.float32),
        ),
        in_specs=[pl.BlockSpec(memory_space=pltpu.SMEM)]
        + [vmem] * 2
        + [pl.BlockSpec(memory_space=pl.ANY)] * 4,
        out_specs=[vmem] * 2,
        scratch_shapes=[
            *[pltpu.VMEM((3 * CROWS, LANES), jnp.float32)] * 12,
            *[pltpu.VMEM((3 * GROWS, LANES), jnp.float32)] * 4,
            *[pltpu.VMEM((devices * count, 8, LANES), jnp.float32)] * 3,
            pltpu.VMEM((EXT, NBLK * LANES), jnp.bfloat16),
            pltpu.VMEM((2, NBLK * BLK, CH * LANES), jnp.bfloat16),
            pltpu.VMEM((MODES, NBLK * BLK, LANES), jnp.float32),
            pltpu.VMEM((NBLK * BLK, LANES), jnp.float32),
            pltpu.VMEM((2, NBLK * BLK, 2 * LANES), jnp.bfloat16),
            pltpu.VMEM((MODES * TERMS * BLK, NBLK * LANES), jnp.bfloat16),
            pltpu.VMEM((LANES // STEP, 24, STEP), jnp.int32),
            pltpu.SMEM((LANES // STEP, 24, STEP), jnp.int32),
            pltpu.SemaphoreType.DMA,
            *[pltpu.VMEM(shape, jnp.bfloat16) for shape in BANDS],
            pltpu.SemaphoreType.DMA((4,)),
        ],
        compiler_params=pltpu.CompilerParams(vmem_limit_bytes=36 << 20),
        name="imaging",
    )(weights, in_vmem(gathered.reshape(devices * slabs, 8, LANES)), target, *[in_hbm(b) for b in bands])


def pack_kernel(masters_ref, owner_ref, local_ref, row_ref, col_ref, out_ref, spread):
    count = masters_ref.shape[0]
    for s in range(8):
        spread[pl.ds(s, count, stride=8), :] = masters_ref[:, s * LANES : (s + 1) * LANES]
    spread[8 * count :, :] = jnp.zeros((8, LANES), jnp.float32)
    for n, ref in enumerate((owner_ref, local_ref, row_ref, col_ref)):
        spread[8 * count + n : 8 * count + n + 1, :] = ref[...].astype(jnp.float32)
    packed = spread[...].reshape(out_ref.shape[1:]).astype(jnp.bfloat16)
    for d in range(out_ref.shape[0]):
        out_ref[d] = packed


def pack(devices, masters, *places):
    count = masters.shape[0]
    vmem = pl.BlockSpec(memory_space=pltpu.VMEM)
    return pl.pallas_call(
        pack_kernel,
        out_shape=pltpu.VMEM((devices, count + 1, 8, LANES), jnp.bfloat16),
        in_specs=[vmem] * 5,
        out_specs=vmem,
        scratch_shapes=[pltpu.VMEM((8 * count + 8, LANES), jnp.float32)],
        compiler_params=pltpu.CompilerParams(vmem_limit_bytes=4 << 20),
        name="pack",
    )(in_hbm(masters), *[in_hbm(p.reshape(1, LANES)) for p in places])


def update_kernel(kept_ref, sent_ref, velocity_ref, masters_ref, velocity_out, masters_out, sums):
    count = velocity_ref.shape[0]
    sums[...] = (kept_ref[0] + sent_ref[0]).reshape(count * 8, LANES)
    for s in range(8):
        at = slice(s * LANES, (s + 1) * LANES)
        gradient = sums[pl.ds(s, count, stride=8), :]
        velocity = momentum * velocity_ref[:, at] + gradient
        velocity_out[:, at] = velocity
        masters_out[:, at] = masters_ref[:, at] - step_size * velocity


def update(kept, sent, velocity, masters):
    vmem = pl.BlockSpec(memory_space=pltpu.VMEM)
    return pl.pallas_call(
        update_kernel,
        out_shape=(jax.ShapeDtypeStruct(velocity.shape, jnp.float32),) * 2,
        in_specs=[vmem] * 4,
        out_specs=[vmem] * 2,
        scratch_shapes=[pltpu.VMEM((8 * velocity.shape[0], LANES), jnp.float32)],
        compiler_params=pltpu.CompilerParams(vmem_limit_bytes=4 << 20),
        name="update",
    )(kept, sent, velocity, masters)


def swap(value, bit, devices):
    return lax.ppermute(value, "tx", [(i, i ^ bit) for i in range(devices)])


def on_device(
    masters,
    velocity,
    place_owner,
    place_local,
    place_row,
    place_col,
    row_taps,
    col_taps,
    mode_weights,
    target,
):
    devices = lax.axis_size("tx")
    bits = devices.bit_length() - 1
    packed = pack(devices, masters, place_owner, place_local, place_row, place_col)
    held = lax.all_to_all(packed, "tx", split_axis=0, concat_axis=0, tiled=True)
    bands = build_bands(row_taps, col_taps)
    resid, grads = main_step(mode_weights, held, target, bands)
    for b in range(bits):
        half = grads.shape[0] // 2
        sent = swap(grads[half:], 1 << b, devices)
        if b < bits - 1:
            grads = grads[:half] + sent
    velocity_new, masters_new = update(grads, sent, velocity, masters)
    return resid, velocity_new, masters_new


def solution(mesh):
    return jax.shard_map(
        on_device,
        mesh=mesh,
        in_specs=(
            P(("groups", "tx"), None),
            P(("groups", "tx"), None),
            P(("groups", "tx"), None),
            P(("groups", "tx")),
            P(("groups", "tx")),
            P(("groups", "tx")),
            P(),
            P(),
            P(),
            P(("groups", "tx"), None),
        ),
        out_specs=(P(("groups", "tx"), None), P(("groups", "tx"), None), P(("groups", "tx"), None)),
        check_vma=False,
    )
```

```python
import functools
import jax
import jax.numpy as jnp
from jax import lax
from jax.experimental import pallas as pl
from jax.experimental.pallas import tpu as pltpu
from jax.sharding import PartitionSpec as P

W = 256
MS = 32
TAPS = 63
HALF = 31
TERMS = 4
MODES = 12
CH = 2 * TERMS
LANES = 128
BLK = 64
EXT = 128
STEP = 32
GROUP = 4
NBLK = W // BLK
PAD = 40
CROWS = 72
GROWS = 2 * PAD + EXT

steepness = 0.5
threshold = 8.0
momentum = 0.9
step_size = 0.05


def in_vmem(x):
    return pltpu.with_memory_space_constraint(x, pltpu.VMEM)


def in_hbm(x):
    return pltpu.with_memory_space_constraint(x, pltpu.HBM)


def lane_iota(shape):
    return lax.broadcasted_iota(jnp.int32, shape, len(shape) - 1)


def skew(row, shift):
    return pltpu.roll(
        jnp.broadcast_to(row, (BLK, LANES)), shift, 1, stride=1, stride_axis=0
    )


def pair(first, second):
    return (skew(first, 0), skew(first, BLK), skew(second, 0), skew(second, BLK))


def half_band(x):
    return x.astype(jnp.bfloat16)


def low_lanes():
    return lane_iota((BLK, LANES)) < BLK


def fill_taps(row_ref, col_ref, taps):
    count = MODES * CH
    taps[...] = jnp.zeros_like(taps)
    for k in range(MODES):
        for t in range(TERMS):
            at = k * CH + 2 * t
            taps[at : at + 2, :TAPS] = row_ref[k, t].astype(jnp.float32)
            taps[count + at : count + at + 2, :TAPS] = col_ref[k, t].astype(jnp.float32)
    source = lax.broadcasted_iota(jnp.int32, (LANES, LANES), 0)
    mirror = (source + lane_iota((LANES, LANES))) % LANES == 0
    taps[2 * count :, :] = jnp.dot(
        taps[: 2 * count, :].astype(jnp.bfloat16),
        mirror.astype(jnp.bfloat16),
        preferred_element_type=jnp.float32,
    )
    taps[count : 2 * count, :] = pltpu.roll(taps[count : 2 * count, :], LANES - (TAPS - 1), 1)


def bands_kernel(row_ref, col_ref, taps, cf_ref, ca_ref):
    count = MODES * CH

    @pl.when(pl.program_id(0) == 0)
    def _():
        fill_taps(row_ref, col_ref, taps)

    low = low_lanes()

    def step(n, carry):
        first = (pl.program_id(0) * GROUP + n) * 4
        for t in range(2):
            at = t * 2 * EXT
            a, a_far, b, b_far = pair(
                taps[pl.ds(3 * count + first + 2 * t, 1), :],
                taps[pl.ds(3 * count + first + 2 * t + 1, 1), :],
            )
            cf_ref[n, at : at + BLK, :] = half_band(jnp.where(low, a, b_far))
            cf_ref[n, at + BLK : at + EXT, :] = half_band(jnp.where(low, a_far, b))
            cf_ref[n, at + EXT : at + EXT + BLK, :] = half_band(jnp.where(low, -b, a_far))
            cf_ref[n, at + EXT + BLK : at + 2 * EXT, :] = half_band(jnp.where(low, -b_far, a))
            a, a_far, b, b_far = pair(
                taps[pl.ds(count + first + 2 * t, 1), :],
                taps[pl.ds(count + first + 2 * t + 1, 1), :],
            )
            ca_ref[n * 2 + t, :BLK, :] = half_band(jnp.where(low, a, -b_far))
            ca_ref[n * 2 + t, BLK:EXT, :] = half_band(jnp.where(low, a_far, -b))
            ca_ref[n * 2 + t, EXT : EXT + BLK, :] = half_band(jnp.where(low, b, a_far))
            ca_ref[n * 2 + t, EXT + BLK :, :] = half_band(jnp.where(low, b_far, a))
        return carry

    lax.fori_loop(0, GROUP, step, 0, unroll=2)


def build_bands(row_taps, col_taps):
    vmem = pl.BlockSpec(memory_space=pltpu.VMEM)
    return pl.pallas_call(
        bands_kernel,
        grid=(2 * MODES // GROUP,),
        out_shape=(
            pltpu.HBM((4 * MODES * CH, LANES), jnp.float32),
            pltpu.HBM((2 * MODES, CH * EXT // 2, LANES), jnp.bfloat16),
            pltpu.HBM((4 * MODES, 2 * EXT, LANES), jnp.bfloat16),
        ),
        in_specs=[vmem] * 2,
        out_specs=[
            pl.BlockSpec((4 * MODES * CH, LANES), lambda n: (0, 0)),
            pl.BlockSpec((GROUP, CH * EXT // 2, LANES), lambda n: (n, 0, 0)),
            pl.BlockSpec((2 * GROUP, 2 * EXT, LANES), lambda n: (n, 0, 0)),
        ],
        compiler_params=pltpu.CompilerParams(vmem_limit_bytes=8 << 20),
        name="bands",
    )(in_hbm(row_taps), in_hbm(col_taps))


def reversed_bits(value, bits):
    return sum(((value >> b) & 1) << (bits - 1 - b) for b in range(bits))


def main_kernel(
    devices,
    gathered_ref,
    weight_hbm,
    target_hbm,
    taps_hbm,
    cf_hbm,
    ca_hbm,
    resid_ref,
    grads_ref,
    *scratch,
):
    canvases = (scratch[0:4], scratch[4:8], scratch[8:12])
    grads = scratch[12:16]
    sums = scratch[16:19]
    window, lhs, fields, slope, gw, gys, table, ids, sem = scratch[19:28]
    weight_ref, target_ref, taps, cf_ref, ca_ref, r_ref, rt_ref, load_sems = scratch[28:]
    loads = [
        pltpu.make_async_copy(source, target, load_sems.at[n])
        for n, (source, target) in enumerate(
            (
                (taps_hbm, taps),
                (weight_hbm, weight_ref),
                (cf_hbm, cf_ref),
                (target_hbm, target_ref),
                (ca_hbm, ca_ref),
            )
        )
    ]
    slabs = gathered_ref.shape[0] // devices
    count = slabs - 1
    places = LANES
    rows = BLK
    me = lax.axis_index("tx")
    bits = devices.bit_length() - 1
    bases = (PAD + HALF, PAD + HALF - rows, PAD + HALF + rows)
    for n, (other, missing) in enumerate(
        ((me, 0), (jnp.maximum(me - 1, 0), 0), (jnp.minimum(me + 1, devices - 1), BLK - MS))
    ):
        slab = gathered_ref[other * slabs + count].astype(jnp.float32).astype(jnp.int32)
        owner, local, row, col = slab[0:1], slab[1:2], slab[2:3], slab[3:4]
        if n:
            row = jnp.where(other == me, missing, row)
        lines = jnp.concatenate(
            [
                owner * slabs + local,
                reversed_bits(owner ^ me, bits) * count + local,
                ((col + HALF) >> 7) * CROWS + row + 7,
                (col + HALF) & 127,
                (col >> 7) * GROWS + row + bases[n],
                col & 127,
                (LANES - (col & 127)) & 127,
                row,
            ],
            axis=0,
        )
        for j in range(places // STEP):
            table[j, 8 * n : 8 * n + 8, :] = (
                pltpu.roll(lines, LANES - STEP * j, 1) if j else lines
            )[:, :STEP]
    to_scalar = pltpu.make_async_copy(table, ids, sem)
    to_scalar.start()
    for load in loads:
        load.start()
    for group in canvases:
        for canvas in group:
            canvas[...] = jnp.zeros_like(canvas)
    for acc in sums:
        acc[...] = jnp.zeros_like(acc)
    lanes8 = lane_iota((8, LANES))
    to_scalar.wait()

    def place(j, u):
        for n, group in enumerate(canvases):
            at, shift = ids[j, 8 * n + 2, u], ids[j, 8 * n + 3, u]
            moved = pltpu.roll(gathered_ref[ids[j, 8 * n, u]].astype(jnp.float32), shift, 1)
            ahead = lanes8 - shift
            here = ahead >= 0
            nth = (ahead & 127) >> 5
            near, far = jnp.where(here, moved, 0.0), jnp.where(here, 0.0, moved)
            for k, canvas in enumerate(group):
                spot = pl.ds(at + k, 8, stride=4)
                spot_far = pl.ds(at + k + CROWS, 8, stride=4)
                mine = nth == k
                old, old_far = canvas[spot, :], canvas[spot_far, :]
                canvas[spot, :] = old + jnp.where(mine, near, 0.0)
                canvas[spot_far, :] = old_far + jnp.where(mine, far, 0.0)

    @pl.loop(0, places // STEP)
    def _(j):
        for u in range(STEP):
            place(j, u)


    lanes_ext = lane_iota((EXT, LANES))
    parts = [
        [
            jnp.concatenate(
                [
                    above[h * CROWS + 40 : h * CROWS + 64],
                    above[h * CROWS + 64 : (h + 1) * CROWS] + own[h * CROWS : h * CROWS + 8],
                    own[h * CROWS + 8 : h * CROWS + 64],
                    own[h * CROWS + 64 : (h + 1) * CROWS] + below[h * CROWS : h * CROWS + 8],
                    below[h * CROWS + 8 : h * CROWS + 40],
                ],
                axis=0,
            )
            for h in range(3)
        ]
        for own, above, below in zip(*canvases)
    ]
    sides = [parts[0][h] for h in range(3)]
    for k in range(1, 4):
        back = [pltpu.roll(part, LANES - MS * k, 1) for part in parts[k]]
        for h in range(3):
            after = back[h + 1] if h < 2 else 0.0
            sides[h] = sides[h] + jnp.where(lanes_ext < LANES - MS * k, back[h], after)
    low = lanes_ext < BLK
    turned = [pltpu.roll(side, BLK, 1) for side in sides]
    window[:, 0:128] = sides[0].astype(jnp.bfloat16)
    window[:, 128:256] = jnp.where(low, turned[0], turned[1]).astype(jnp.bfloat16)
    window[:, 256:384] = sides[1].astype(jnp.bfloat16)
    window[:, 384:512] = jnp.where(low, turned[1], turned[2]).astype(jnp.bfloat16)

    lanes16 = lane_iota((16, LANES))
    before = lanes16 < HALF
    until = lanes16 < HALF + BLK
    low64 = low_lanes()

    def row_bands(k):
        for c in range(CH):
            at = k * CH + c
            r_ref[at * BLK : (at + 1) * BLK, :] = half_band(skew(taps[at : at + 1, :], 0))

    def row_adjoint_bands(k):
        for n in (2 * k, 2 * k + 1):
            tap = 2 * MODES * CH + 4 * n
            for par in range(2):
                one, two = tap + par, tap + 2 + par
                a, a_far, b, b_far = pair(taps[one : one + 1, :], taps[two : two + 1, :])
                at = par * EXT
                rt_ref[n, at : at + BLK, :] = half_band(jnp.where(low64, a, b_far))
                rt_ref[n, at + BLK : at + EXT, :] = half_band(jnp.where(low64, a_far, b))

    for load in loads[:3]:
        load.wait()
    row_bands(0)
    intensity = jnp.zeros((NBLK * rows, LANES), jnp.float32)
    for k in range(MODES):
        if k + 1 < MODES:
            row_bands(k + 1)
        row_adjoint_bands(k)
        field_y = jnp.dot(
            r_ref[k * CH * rows : (k + 1) * CH * rows, :],
            window[...],
            preferred_element_type=jnp.float32,
        ).astype(jnp.bfloat16)
        for c in range(CH):
            for b in range(NBLK):
                lhs[k % 2, b * rows : (b + 1) * rows, c * LANES : (c + 1) * LANES] = field_y[
                    c * rows : (c + 1) * rows, b * LANES : (b + 1) * LANES
                ]
        e = jnp.dot(
            lhs[k % 2],
            jnp.concatenate([cf_ref[2 * k], cf_ref[2 * k + 1]], axis=0),
            preferred_element_type=jnp.float32,
        )
        fields[k] = e
        intensity = intensity + weight_ref[k] * (e * e)
    loads[3].wait()
    low_rows = lane_iota((rows, LANES)) < BLK
    for b in range(NBLK):
        inten = intensity[b * rows : (b + 1) * rows]
        inten = inten + pltpu.roll(inten, BLK, 1)
        t = target_ref[:, (b // 2) * LANES : (b // 2 + 1) * LANES].astype(jnp.float32)
        other = pltpu.roll(t, BLK, 1)
        goal = jnp.where(low_rows, t, other) if b % 2 == 0 else jnp.where(low_rows, other, t)
        resist = jax.nn.sigmoid(steepness * (inten - threshold))
        resid = resist - goal
        slope[b * rows : (b + 1) * rows, :] = 2.0 * (resid * steepness * resist * (1.0 - resist))
        if b % 2 == 0:
            resid_ref[:, (b // 2) * LANES : (b // 2 + 1) * LANES] = resid
        else:
            resid_ref[:, (b // 2) * LANES + BLK : (b // 2 + 1) * LANES] = resid[:, BLK:]

    loads[4].wait()
    nothing = jnp.zeros((16, LANES), jnp.float32)
    for k in range(MODES):
        weight = weight_ref[k]
        for i in range(0, rows, 16):
            r31, r95 = [nothing], [nothing]
            for b in range(NBLK):
                at = slice(b * rows + i, b * rows + i + 16)
                g = weight * slope[at, :] * fields[k, at, :]
                r31.append(pltpu.roll(g, HALF, 1))
                r95.append(pltpu.roll(g, HALF + BLK, 1))
            r31.append(nothing)
            r95.append(nothing)
            for b in range(NBLK):
                at = slice(b * rows + i, b * rows + i + 16)
                re = jnp.where(before, r95[b], jnp.where(until, r31[b + 1], r95[b + 2]))
                im = jnp.where(before, r31[b], jnp.where(until, r95[b + 1], r31[b + 2]))
                gw[k % 2, at, :LANES] = re.astype(jnp.bfloat16)
                gw[k % 2, at, LANES:] = im.astype(jnp.bfloat16)
        for t in range(TERMS):
            gy = jnp.dot(
                gw[k % 2], ca_ref[k * TERMS + t], preferred_element_type=jnp.float32
            ).astype(jnp.bfloat16)
            at = (k * TERMS + t) * rows
            for b in range(NBLK):
                gys[at : at + rows, b * LANES : (b + 1) * LANES] = gy[b * rows : (b + 1) * rows]

    total = jnp.zeros((2 * EXT, NBLK * LANES), jnp.float32)
    for k in range(MODES):
        total = total + jnp.dot(
            jnp.concatenate([rt_ref[2 * k], rt_ref[2 * k + 1]], axis=1),
            gys[2 * k * LANES : 2 * (k + 1) * LANES, :],
            preferred_element_type=jnp.float32,
        )
    whole = []
    for h in range(2):
        v0 = total[:EXT, 2 * h * LANES : (2 * h + 1) * LANES]
        v1 = total[:EXT, (2 * h + 1) * LANES : (2 * h + 2) * LANES]
        u0 = total[EXT:, 2 * h * LANES : (2 * h + 1) * LANES]
        u1 = total[EXT:, (2 * h + 1) * LANES : (2 * h + 2) * LANES]
        whole.append(
            jnp.where(low, v0 + pltpu.roll(u0, BLK, 1), pltpu.roll(v1, BLK, 1) + u1)
        )
    zeros = jnp.zeros((PAD, LANES), jnp.float32)
    for k, grad in enumerate(grads):
        ahead = [pltpu.roll(side, MS * k, 1) if k else side for side in whole]
        for h in range(3):
            here = ahead[h] if h < 2 else 0.0
            behind = ahead[h - 1] if h else 0.0
            base = h * GROWS
            grad[base : base + PAD, :] = zeros
            grad[base + PAD : base + PAD + EXT, :] = jnp.where(lanes_ext >= MS * k, here, behind)
            grad[base + PAD + EXT : base + GROWS, :] = zeros

    def gather(j, u):
        for n, acc in enumerate(sums):
            m, at, shift, back = [ids[j, 8 * n + line, u] for line in (1, 4, 5, 6)]
            ahead = lanes8 - shift
            here = ahead >= 0
            nth = ahead & 127
            patch = None
            for k, grad in enumerate(grads):
                both = jnp.where(
                    here,
                    grad[pl.ds(at + k, 8, stride=4), :],
                    grad[pl.ds(at + k + GROWS, 8, stride=4), :],
                )
                patch = jnp.where(nth >= MS * k, both, patch) if k else both
            acc[m] += pltpu.roll(patch, back, 1)

    @pl.loop(0, places // STEP)
    def _(j):
        for u in range(STEP):
            gather(j, u)

    grads_ref[...] = (sums[0][...] + sums[1][...] + sums[2][...]).reshape(grads_ref.shape)


def main_step(weights, gathered, target, bands):
    devices, slabs = gathered.shape[:2]
    count = slabs - 1
    vmem = pl.BlockSpec(memory_space=pltpu.VMEM)
    return pl.pallas_call(
        functools.partial(main_kernel, devices),
        out_shape=(
            jax.ShapeDtypeStruct(target.shape, jnp.float32),
            pltpu.VMEM((devices, count, 8, LANES), jnp.float32),
        ),
        in_specs=[vmem] + [pl.BlockSpec(memory_space=pl.ANY)] * 5,
        out_specs=[vmem] * 2,
        scratch_shapes=[
            *[pltpu.VMEM((3 * CROWS, LANES), jnp.float32)] * 12,
            *[pltpu.VMEM((3 * GROWS, LANES), jnp.float32)] * 4,
            *[pltpu.VMEM((devices * count, 8, LANES), jnp.float32)] * 3,
            pltpu.VMEM((EXT, NBLK * LANES), jnp.bfloat16),
            pltpu.VMEM((2, NBLK * BLK, CH * LANES), jnp.bfloat16),
            pltpu.VMEM((MODES, NBLK * BLK, LANES), jnp.float32),
            pltpu.VMEM((NBLK * BLK, LANES), jnp.float32),
            pltpu.VMEM((2, NBLK * BLK, 2 * LANES), jnp.bfloat16),
            pltpu.VMEM((MODES * TERMS * BLK, NBLK * LANES), jnp.bfloat16),
            pltpu.VMEM((LANES // STEP, 24, STEP), jnp.int32),
            pltpu.SMEM((LANES // STEP, 24, STEP), jnp.int32),
            pltpu.SemaphoreType.DMA,
            pltpu.SMEM(weights.shape, jnp.float32),
            pltpu.VMEM(target.shape, jnp.bfloat16),
            pltpu.VMEM(bands[0].shape, jnp.float32),
            pltpu.VMEM(bands[1].shape, jnp.bfloat16),
            pltpu.VMEM(bands[2].shape, jnp.bfloat16),
            pltpu.VMEM((MODES * CH * BLK, LANES), jnp.bfloat16),
            pltpu.VMEM((2 * MODES, 2 * EXT, LANES), jnp.bfloat16),
            pltpu.SemaphoreType.DMA((5,)),
        ],
        compiler_params=pltpu.CompilerParams(vmem_limit_bytes=36 << 20),
        name="imaging",
    )(
        in_vmem(gathered.reshape(devices * slabs, 8, LANES)),
        *[in_hbm(x) for x in (weights, target, *bands)],
    )


def pack_kernel(masters_ref, owner_ref, local_ref, row_ref, col_ref, out_ref, spread):
    count = masters_ref.shape[0]
    for s in range(8):
        spread[pl.ds(s, count, stride=8), :] = masters_ref[:, s * LANES : (s + 1) * LANES]
    spread[8 * count :, :] = jnp.zeros((8, LANES), jnp.float32)
    for n, ref in enumerate((owner_ref, local_ref, row_ref, col_ref)):
        spread[8 * count + n : 8 * count + n + 1, :] = ref[...].astype(jnp.float32)
    packed = spread[...].reshape(out_ref.shape[1:]).astype(jnp.bfloat16)
    for d in range(out_ref.shape[0]):
        out_ref[d] = packed


def pack(devices, masters, *places):
    count = masters.shape[0]
    vmem = pl.BlockSpec(memory_space=pltpu.VMEM)
    return pl.pallas_call(
        pack_kernel,
        out_shape=pltpu.VMEM((devices, count + 1, 8, LANES), jnp.bfloat16),
        in_specs=[vmem] * 5,
        out_specs=vmem,
        scratch_shapes=[pltpu.VMEM((8 * count + 8, LANES), jnp.float32)],
        compiler_params=pltpu.CompilerParams(vmem_limit_bytes=4 << 20),
        name="pack",
    )(in_hbm(masters), *[in_hbm(p.reshape(1, LANES)) for p in places])


def update_kernel(kept_ref, sent_ref, velocity_ref, masters_ref, velocity_out, masters_out, sums):
    count = velocity_ref.shape[0]
    sums[...] = (kept_ref[0] + sent_ref[0]).reshape(count * 8, LANES)
    for s in range(8):
        at = slice(s * LANES, (s + 1) * LANES)
        gradient = sums[pl.ds(s, count, stride=8), :]
        velocity = momentum * velocity_ref[:, at] + gradient
        velocity_out[:, at] = velocity
        masters_out[:, at] = masters_ref[:, at] - step_size * velocity


def update(kept, sent, velocity, masters):
    vmem = pl.BlockSpec(memory_space=pltpu.VMEM)
    return pl.pallas_call(
        update_kernel,
        out_shape=(jax.ShapeDtypeStruct(velocity.shape, jnp.float32),) * 2,
        in_specs=[vmem] * 4,
        out_specs=[vmem] * 2,
        scratch_shapes=[pltpu.VMEM((8 * velocity.shape[0], LANES), jnp.float32)],
        compiler_params=pltpu.CompilerParams(vmem_limit_bytes=4 << 20),
        name="update",
    )(kept, sent, velocity, masters)


def swap(value, bit, devices):
    return lax.ppermute(value, "tx", [(i, i ^ bit) for i in range(devices)])


def on_device(
    masters,
    velocity,
    place_owner,
    place_local,
    place_row,
    place_col,
    row_taps,
    col_taps,
    mode_weights,
    target,
):
    devices = lax.axis_size("tx")
    bits = devices.bit_length() - 1
    packed = pack(devices, masters, place_owner, place_local, place_row, place_col)
    held = lax.all_to_all(packed, "tx", split_axis=0, concat_axis=0, tiled=True)
    bands = build_bands(row_taps, col_taps)
    resid, grads = main_step(mode_weights, held, target, bands)
    for b in range(bits):
        half = grads.shape[0] // 2
        sent = swap(grads[half:], 1 << b, devices)
        if b < bits - 1:
            grads = grads[:half] + sent
    velocity_new, masters_new = update(grads, sent, velocity, masters)
    return resid, velocity_new, masters_new


def solution(mesh):
    return jax.shard_map(
        on_device,
        mesh=mesh,
        in_specs=(
            P(("groups", "tx"), None),
            P(("groups", "tx"), None),
            P(("groups", "tx"), None),
            P(("groups", "tx")),
            P(("groups", "tx")),
            P(("groups", "tx")),
            P(),
            P(),
            P(),
            P(("groups", "tx"), None),
        ),
        out_specs=(P(("groups", "tx"), None), P(("groups", "tx"), None), P(("groups", "tx"), None)),
        check_vma=False,
    )
```

```python
import functools
import jax
import jax.numpy as jnp
from jax import lax
from jax.experimental import pallas as pl
from jax.experimental.pallas import tpu as pltpu
from jax.sharding import PartitionSpec as P

W = 256
MS = 32
TAPS = 63
HALF = 31
TERMS = 4
MODES = 12
CH = 2 * TERMS
LANES = 128
BLK = 64
EXT = 128
STEP = 32
NBLK = W // BLK
PAD = 40
CROWS = 72
GROWS = 2 * PAD + EXT

steepness = 0.5
threshold = 8.0
momentum = 0.9
step_size = 0.05


def in_vmem(x):
    return pltpu.with_memory_space_constraint(x, pltpu.VMEM)


def in_hbm(x):
    return pltpu.with_memory_space_constraint(x, pltpu.HBM)


def lane_iota(shape):
    return lax.broadcasted_iota(jnp.int32, shape, len(shape) - 1)


def skew(row, shift):
    return pltpu.roll(
        jnp.broadcast_to(row, (BLK, LANES)), shift, 1, stride=1, stride_axis=0
    )


def pair(first, second):
    return (skew(first, 0), skew(first, BLK), skew(second, 0), skew(second, BLK))


def half_band(x):
    return x.astype(jnp.bfloat16)


def low_lanes():
    return lane_iota((BLK, LANES)) < BLK


def taps_kernel(row_ref, col_ref, taps):
    count = MODES * CH
    taps[...] = jnp.zeros_like(taps)
    for k in range(MODES):
        for t in range(TERMS):
            at = k * CH + 2 * t
            taps[at : at + 2, :TAPS] = row_ref[k, t].astype(jnp.float32)
            taps[count + at : count + at + 2, :TAPS] = col_ref[k, t].astype(jnp.float32)
    source = lax.broadcasted_iota(jnp.int32, (LANES, LANES), 0)
    mirror = (source + lane_iota((LANES, LANES))) % LANES == 0
    taps[2 * count :, :] = jnp.dot(
        taps[: 2 * count, :].astype(jnp.bfloat16),
        mirror.astype(jnp.bfloat16),
        preferred_element_type=jnp.float32,
    )
    taps[count : 2 * count, :] = pltpu.roll(taps[count : 2 * count, :], LANES - (TAPS - 1), 1)


def column_bands_kernel(taps, _, cf_ref):
    count = MODES * CH
    low = low_lanes()

    def step(n, carry):
        first = 3 * count + 4 * n
        for t in range(2):
            at = t * 2 * EXT
            a, a_far, b, b_far = pair(
                taps[pl.ds(first + 2 * t, 1), :], taps[pl.ds(first + 2 * t + 1, 1), :]
            )
            cf_ref[n, at : at + BLK, :] = half_band(jnp.where(low, a, b_far))
            cf_ref[n, at + BLK : at + EXT, :] = half_band(jnp.where(low, a_far, b))
            cf_ref[n, at + EXT : at + EXT + BLK, :] = half_band(jnp.where(low, -b, a_far))
            cf_ref[n, at + EXT + BLK : at + 2 * EXT, :] = half_band(jnp.where(low, -b_far, a))
        return carry

    lax.fori_loop(0, 2 * MODES, step, 0, unroll=3)


def column_adjoint_kernel(taps, _, ca_ref):
    count = MODES * CH
    low = low_lanes()

    def step(n, carry):
        first = count + 4 * n
        for t in range(2):
            a, a_far, b, b_far = pair(
                taps[pl.ds(first + 2 * t, 1), :], taps[pl.ds(first + 2 * t + 1, 1), :]
            )
            ca_ref[n * 2 + t, :BLK, :] = half_band(jnp.where(low, a, -b_far))
            ca_ref[n * 2 + t, BLK:EXT, :] = half_band(jnp.where(low, a_far, -b))
            ca_ref[n * 2 + t, EXT : EXT + BLK, :] = half_band(jnp.where(low, b, a_far))
            ca_ref[n * 2 + t, EXT + BLK :, :] = half_band(jnp.where(low, b_far, a))
        return carry

    lax.fori_loop(0, 2 * MODES, step, 0, unroll=3)


def build_bands(row_taps, col_taps, stages):
    vmem = pl.BlockSpec(memory_space=pltpu.VMEM)
    small = pltpu.CompilerParams(vmem_limit_bytes=4 << 20)
    taps = in_vmem(
        pl.pallas_call(
            taps_kernel,
            out_shape=pltpu.VMEM((4 * MODES * CH, LANES), jnp.float32),
            in_specs=[vmem] * 2,
            out_specs=vmem,
            compiler_params=small,
            name="taps",
        )(in_hbm(row_taps), in_hbm(col_taps))
    )
    built = [
        pl.pallas_call(
            kernel,
            out_shape=pltpu.VMEM(shape, jnp.bfloat16),
            in_specs=[vmem, pl.BlockSpec(memory_space=pl.ANY)],
            out_specs=vmem,
            compiler_params=small,
            name=name,
        )(taps, stage)
        for stage, (kernel, shape, name) in zip(
            stages,
            (
                (column_bands_kernel, (2 * MODES, CH * EXT // 2, LANES), "column_bands"),
                (column_adjoint_kernel, (4 * MODES, 2 * EXT, LANES), "column_adjoint"),
            ),
        )
    ]
    return [taps, *built]


def reversed_bits(value, bits):
    return sum(((value >> b) & 1) << (bits - 1 - b) for b in range(bits))


def main_kernel(
    devices,
    gathered_ref,
    taps,
    cf_ref,
    ca_ref,
    weight_hbm,
    target_hbm,
    resid_ref,
    grads_ref,
    *scratch,
):
    canvases = (scratch[0:4], scratch[4:8], scratch[8:12])
    grads = scratch[12:16]
    sums = scratch[16:19]
    window, lhs, fields, slope, gw, gys, table, ids, sem = scratch[19:28]
    weight_ref, target_ref, r_ref, rt_ref, load_sems = scratch[28:]
    loads = [
        pltpu.make_async_copy(source, target, load_sems.at[n])
        for n, (source, target) in enumerate(
            (
                (weight_hbm, weight_ref),
                (target_hbm, target_ref),
            )
        )
    ]
    slabs = gathered_ref.shape[0] // devices
    count = slabs - 1
    places = LANES
    rows = BLK
    me = lax.axis_index("tx")
    bits = devices.bit_length() - 1
    bases = (PAD + HALF, PAD + HALF - rows, PAD + HALF + rows)
    for n, (other, missing) in enumerate(
        ((me, 0), (jnp.maximum(me - 1, 0), 0), (jnp.minimum(me + 1, devices - 1), BLK - MS))
    ):
        slab = gathered_ref[(other ^ me) * slabs + count].astype(jnp.float32).astype(jnp.int32)
        owner, local, row, col = slab[0:1] ^ me, slab[1:2], slab[2:3], slab[3:4]
        if n:
            row = jnp.where(other == me, missing, row)
        lines = jnp.concatenate(
            [
                owner * slabs + local,
                reversed_bits(owner, bits) * count + local,
                ((col + HALF) >> 7) * CROWS + row + 7,
                (col + HALF) & 127,
                (col >> 7) * GROWS + row + bases[n],
                col & 127,
                (LANES - (col & 127)) & 127,
                row,
            ],
            axis=0,
        )
        for j in range(places // STEP):
            table[j, 8 * n : 8 * n + 8, :] = (
                pltpu.roll(lines, LANES - STEP * j, 1) if j else lines
            )[:, :STEP]
    to_scalar = pltpu.make_async_copy(table, ids, sem)
    to_scalar.start()
    for load in loads:
        load.start()
    for group in canvases:
        for canvas in group:
            canvas[...] = jnp.zeros_like(canvas)
    for acc in sums:
        acc[...] = jnp.zeros_like(acc)
    lanes8 = lane_iota((8, LANES))
    to_scalar.wait()

    def place(j, u):
        for n, group in enumerate(canvases):
            at, shift = ids[j, 8 * n + 2, u], ids[j, 8 * n + 3, u]
            moved = pltpu.roll(gathered_ref[ids[j, 8 * n, u]].astype(jnp.float32), shift, 1)
            ahead = lanes8 - shift
            here = ahead >= 0
            nth = (ahead & 127) >> 5
            near, far = jnp.where(here, moved, 0.0), jnp.where(here, 0.0, moved)
            for k, canvas in enumerate(group):
                spot = pl.ds(at + k, 8, stride=4)
                spot_far = pl.ds(at + k + CROWS, 8, stride=4)
                mine = nth == k
                old, old_far = canvas[spot, :], canvas[spot_far, :]
                canvas[spot, :] = old + jnp.where(mine, near, 0.0)
                canvas[spot_far, :] = old_far + jnp.where(mine, far, 0.0)

    @pl.loop(0, places // STEP)
    def _(j):
        for u in range(STEP):
            place(j, u)


    lanes_ext = lane_iota((EXT, LANES))
    parts = [
        [
            jnp.concatenate(
                [
                    above[h * CROWS + 40 : h * CROWS + 64],
                    above[h * CROWS + 64 : (h + 1) * CROWS] + own[h * CROWS : h * CROWS + 8],
                    own[h * CROWS + 8 : h * CROWS + 64],
                    own[h * CROWS + 64 : (h + 1) * CROWS] + below[h * CROWS : h * CROWS + 8],
                    below[h * CROWS + 8 : h * CROWS + 40],
                ],
                axis=0,
            )
            for h in range(3)
        ]
        for own, above, below in zip(*canvases)
    ]
    sides = [parts[0][h] for h in range(3)]
    for k in range(1, 4):
        back = [pltpu.roll(part, LANES - MS * k, 1) for part in parts[k]]
        for h in range(3):
            after = back[h + 1] if h < 2 else 0.0
            sides[h] = sides[h] + jnp.where(lanes_ext < LANES - MS * k, back[h], after)
    low = lanes_ext < BLK
    turned = [pltpu.roll(side, BLK, 1) for side in sides]
    window[:, 0:128] = sides[0].astype(jnp.bfloat16)
    window[:, 128:256] = jnp.where(low, turned[0], turned[1]).astype(jnp.bfloat16)
    window[:, 256:384] = sides[1].astype(jnp.bfloat16)
    window[:, 384:512] = jnp.where(low, turned[1], turned[2]).astype(jnp.bfloat16)

    lanes16 = lane_iota((16, LANES))
    before = lanes16 < HALF
    until = lanes16 < HALF + BLK
    low64 = low_lanes()

    def row_bands(k):
        for c in range(CH):
            at = k * CH + c
            r_ref[at * BLK : (at + 1) * BLK, :] = half_band(skew(taps[at : at + 1, :], 0))

    def row_adjoint_bands(k):
        for n in (2 * k, 2 * k + 1):
            tap = 2 * MODES * CH + 4 * n
            for par in range(2):
                one, two = tap + par, tap + 2 + par
                a, a_far, b, b_far = pair(taps[one : one + 1, :], taps[two : two + 1, :])
                at = par * EXT
                rt_ref[n, at : at + BLK, :] = half_band(jnp.where(low64, a, b_far))
                rt_ref[n, at + BLK : at + EXT, :] = half_band(jnp.where(low64, a_far, b))

    loads[0].wait()
    row_bands(0)
    intensity = jnp.zeros((NBLK * rows, LANES), jnp.float32)
    for k in range(MODES):
        if k + 1 < MODES:
            row_bands(k + 1)
        row_adjoint_bands(k)
        field_y = jnp.dot(
            r_ref[k * CH * rows : (k + 1) * CH * rows, :],
            window[...],
            preferred_element_type=jnp.float32,
        ).astype(jnp.bfloat16)
        for c in range(CH):
            for b in range(NBLK):
                lhs[k % 2, b * rows : (b + 1) * rows, c * LANES : (c + 1) * LANES] = field_y[
                    c * rows : (c + 1) * rows, b * LANES : (b + 1) * LANES
                ]
        e = jnp.dot(
            lhs[k % 2],
            jnp.concatenate([cf_ref[2 * k], cf_ref[2 * k + 1]], axis=0),
            preferred_element_type=jnp.float32,
        )
        fields[k] = e
        intensity = intensity + weight_ref[k] * (e * e)
    loads[1].wait()
    low_rows = lane_iota((rows, LANES)) < BLK
    for b in range(NBLK):
        inten = intensity[b * rows : (b + 1) * rows]
        inten = inten + pltpu.roll(inten, BLK, 1)
        t = target_ref[:, (b // 2) * LANES : (b // 2 + 1) * LANES].astype(jnp.float32)
        other = pltpu.roll(t, BLK, 1)
        goal = jnp.where(low_rows, t, other) if b % 2 == 0 else jnp.where(low_rows, other, t)
        resist = jax.nn.sigmoid(steepness * (inten - threshold))
        resid = resist - goal
        slope[b * rows : (b + 1) * rows, :] = 2.0 * (resid * steepness * resist * (1.0 - resist))
        if b % 2 == 0:
            resid_ref[:, (b // 2) * LANES : (b // 2 + 1) * LANES] = resid
        else:
            resid_ref[:, (b // 2) * LANES + BLK : (b // 2 + 1) * LANES] = resid[:, BLK:]

    nothing = jnp.zeros((16, LANES), jnp.float32)
    for k in range(MODES):
        weight = weight_ref[k]
        for i in range(0, rows, 16):
            r31, r95 = [nothing], [nothing]
            for b in range(NBLK):
                at = slice(b * rows + i, b * rows + i + 16)
                g = weight * slope[at, :] * fields[k, at, :]
                r31.append(pltpu.roll(g, HALF, 1))
                r95.append(pltpu.roll(g, HALF + BLK, 1))
            r31.append(nothing)
            r95.append(nothing)
            for b in range(NBLK):
                at = slice(b * rows + i, b * rows + i + 16)
                re = jnp.where(before, r95[b], jnp.where(until, r31[b + 1], r95[b + 2]))
                im = jnp.where(before, r31[b], jnp.where(until, r95[b + 1], r31[b + 2]))
                gw[k % 2, at, :LANES] = re.astype(jnp.bfloat16)
                gw[k % 2, at, LANES:] = im.astype(jnp.bfloat16)
        for t in range(TERMS):
            gy = jnp.dot(
                gw[k % 2], ca_ref[k * TERMS + t], preferred_element_type=jnp.float32
            ).astype(jnp.bfloat16)
            at = (k * TERMS + t) * rows
            for b in range(NBLK):
                gys[at : at + rows, b * LANES : (b + 1) * LANES] = gy[b * rows : (b + 1) * rows]

    total = jnp.zeros((2 * EXT, NBLK * LANES), jnp.float32)
    for k in range(MODES):
        total = total + jnp.dot(
            jnp.concatenate([rt_ref[2 * k], rt_ref[2 * k + 1]], axis=1),
            gys[2 * k * LANES : 2 * (k + 1) * LANES, :],
            preferred_element_type=jnp.float32,
        )
    whole = []
    for h in range(2):
        v0 = total[:EXT, 2 * h * LANES : (2 * h + 1) * LANES]
        v1 = total[:EXT, (2 * h + 1) * LANES : (2 * h + 2) * LANES]
        u0 = total[EXT:, 2 * h * LANES : (2 * h + 1) * LANES]
        u1 = total[EXT:, (2 * h + 1) * LANES : (2 * h + 2) * LANES]
        whole.append(
            jnp.where(low, v0 + pltpu.roll(u0, BLK, 1), pltpu.roll(v1, BLK, 1) + u1)
        )
    zeros = jnp.zeros((PAD, LANES), jnp.float32)
    for k, grad in enumerate(grads):
        ahead = [pltpu.roll(side, MS * k, 1) if k else side for side in whole]
        for h in range(3):
            here = ahead[h] if h < 2 else 0.0
            behind = ahead[h - 1] if h else 0.0
            base = h * GROWS
            grad[base : base + PAD, :] = zeros
            grad[base + PAD : base + PAD + EXT, :] = jnp.where(lanes_ext >= MS * k, here, behind)
            grad[base + PAD + EXT : base + GROWS, :] = zeros

    def gather(j, u):
        for n, acc in enumerate(sums):
            m, at, shift, back = [ids[j, 8 * n + line, u] for line in (1, 4, 5, 6)]
            ahead = lanes8 - shift
            here = ahead >= 0
            nth = ahead & 127
            patch = None
            for k, grad in enumerate(grads):
                both = jnp.where(
                    here,
                    grad[pl.ds(at + k, 8, stride=4), :],
                    grad[pl.ds(at + k + GROWS, 8, stride=4), :],
                )
                patch = jnp.where(nth >= MS * k, both, patch) if k else both
            acc[m] += pltpu.roll(patch, back, 1)

    @pl.loop(0, places // STEP)
    def _(j):
        for u in range(STEP):
            gather(j, u)

    grads_ref[...] = (sums[0][...] + sums[1][...] + sums[2][...]).reshape(grads_ref.shape)


def main_step(weights, gathered, target, bands):
    devices, slabs = gathered.shape[:2]
    count = slabs - 1
    vmem = pl.BlockSpec(memory_space=pltpu.VMEM)
    return pl.pallas_call(
        functools.partial(main_kernel, devices),
        out_shape=(
            jax.ShapeDtypeStruct(target.shape, jnp.float32),
            pltpu.VMEM((devices, count, 8, LANES), jnp.float32),
        ),
        in_specs=[vmem] * 4 + [pl.BlockSpec(memory_space=pl.ANY)] * 2,
        out_specs=[vmem] * 2,
        scratch_shapes=[
            *[pltpu.VMEM((3 * CROWS, LANES), jnp.float32)] * 12,
            *[pltpu.VMEM((3 * GROWS, LANES), jnp.float32)] * 4,
            *[pltpu.VMEM((devices * count, 8, LANES), jnp.float32)] * 3,
            pltpu.VMEM((EXT, NBLK * LANES), jnp.bfloat16),
            pltpu.VMEM((2, NBLK * BLK, CH * LANES), jnp.bfloat16),
            pltpu.VMEM((MODES, NBLK * BLK, LANES), jnp.float32),
            pltpu.VMEM((NBLK * BLK, LANES), jnp.float32),
            pltpu.VMEM((2, NBLK * BLK, 2 * LANES), jnp.bfloat16),
            pltpu.VMEM((MODES * TERMS * BLK, NBLK * LANES), jnp.bfloat16),
            pltpu.VMEM((LANES // STEP, 24, STEP), jnp.int32),
            pltpu.SMEM((LANES // STEP, 24, STEP), jnp.int32),
            pltpu.SemaphoreType.DMA,
            pltpu.SMEM(weights.shape, jnp.float32),
            pltpu.VMEM(target.shape, jnp.bfloat16),
            pltpu.VMEM((MODES * CH * BLK, LANES), jnp.bfloat16),
            pltpu.VMEM((2 * MODES, 2 * EXT, LANES), jnp.bfloat16),
            pltpu.SemaphoreType.DMA((2,)),
        ],
        compiler_params=pltpu.CompilerParams(vmem_limit_bytes=28 << 20),
        name="imaging",
    )(
        in_vmem(gathered.reshape(devices * slabs, 8, LANES)),
        *[in_vmem(x) for x in bands],
        in_hbm(weights),
        in_hbm(target),
    )


def pack_kernel(masters_ref, owner_ref, local_ref, row_ref, col_ref, out_ref, spread):
    count = masters_ref.shape[0]
    for s in range(8):
        spread[pl.ds(s, count, stride=8), :] = masters_ref[:, s * LANES : (s + 1) * LANES]
    spread[8 * count :, :] = jnp.zeros((8, LANES), jnp.float32)
    for n, ref in enumerate((owner_ref, local_ref, row_ref, col_ref)):
        spread[8 * count + n : 8 * count + n + 1, :] = ref[...].astype(jnp.float32)
    out_ref[...] = spread[...].reshape(out_ref.shape).astype(jnp.bfloat16)


def pack(masters, *places):
    count = masters.shape[0]
    vmem = pl.BlockSpec(memory_space=pltpu.VMEM)
    return pl.pallas_call(
        pack_kernel,
        out_shape=pltpu.VMEM((1, count + 1, 8, LANES), jnp.bfloat16),
        in_specs=[vmem] * 5,
        out_specs=vmem,
        scratch_shapes=[pltpu.VMEM((8 * count + 8, LANES), jnp.float32)],
        compiler_params=pltpu.CompilerParams(vmem_limit_bytes=4 << 20),
        name="pack",
    )(in_hbm(masters), *[in_hbm(p.reshape(1, LANES)) for p in places])


def update_kernel(kept_ref, sent_ref, velocity_ref, masters_ref, velocity_out, masters_out, sums):
    count = velocity_ref.shape[0]
    sums[...] = (kept_ref[0] + sent_ref[0]).reshape(count * 8, LANES)
    for s in range(8):
        at = slice(s * LANES, (s + 1) * LANES)
        gradient = sums[pl.ds(s, count, stride=8), :]
        velocity = momentum * velocity_ref[:, at] + gradient
        velocity_out[:, at] = velocity
        masters_out[:, at] = masters_ref[:, at] - step_size * velocity


def update(kept, sent, velocity, masters):
    vmem = pl.BlockSpec(memory_space=pltpu.VMEM)
    return pl.pallas_call(
        update_kernel,
        out_shape=(jax.ShapeDtypeStruct(velocity.shape, jnp.float32),) * 2,
        in_specs=[vmem] * 4,
        out_specs=[vmem] * 2,
        scratch_shapes=[pltpu.VMEM((8 * velocity.shape[0], LANES), jnp.float32)],
        compiler_params=pltpu.CompilerParams(vmem_limit_bytes=4 << 20),
        name="update",
    )(kept, sent, velocity, masters)


def swap(value, bit, devices):
    return lax.ppermute(value, "tx", [(i, i ^ bit) for i in range(devices)])


def on_device(
    masters,
    velocity,
    place_owner,
    place_local,
    place_row,
    place_col,
    row_taps,
    col_taps,
    mode_weights,
    target,
):
    devices = lax.axis_size("tx")
    bits = devices.bit_length() - 1
    held = pack(masters, place_owner, place_local, place_row, place_col)
    stages = []
    for b in range(bits):
        held = jnp.concatenate([held, swap(held, 1 << b, devices)], axis=0)
        stages.append(held)
    bands = build_bands(row_taps, col_taps, (stages[0], stages[-2]))
    resid, grads = main_step(mode_weights, held, target, bands)
    for b in range(bits):
        half = grads.shape[0] // 2
        sent = swap(grads[half:], 1 << b, devices)
        if b < bits - 1:
            grads = grads[:half] + sent
    velocity_new, masters_new = update(grads, sent, velocity, masters)
    return resid, velocity_new, masters_new


def solution(mesh):
    return jax.shard_map(
        on_device,
        mesh=mesh,
        in_specs=(
            P(("groups", "tx"), None),
            P(("groups", "tx"), None),
            P(("groups", "tx"), None),
            P(("groups", "tx")),
            P(("groups", "tx")),
            P(("groups", "tx")),
            P(),
            P(),
            P(),
            P(("groups", "tx"), None),
        ),
        out_specs=(P(("groups", "tx"), None), P(("groups", "tx"), None), P(("groups", "tx"), None)),
        check_vma=False,
    )
```

```python
import functools
import jax
import jax.numpy as jnp
from jax import lax
from jax.experimental import pallas as pl
from jax.experimental.pallas import tpu as pltpu
from jax.sharding import PartitionSpec as P

W = 256
MS = 32
TAPS = 63
HALF = 31
TERMS = 4
MODES = 12
CH = 2 * TERMS
LANES = 128
BLK = 64
EXT = 128
STEP = 32
NBLK = W // BLK
CROWS = 320

steepness = 0.5
threshold = 8.0
momentum = 0.9
step_size = 0.05


def in_vmem(x):
    return pltpu.with_memory_space_constraint(x, pltpu.VMEM)


def in_hbm(x):
    return pltpu.with_memory_space_constraint(x, pltpu.HBM)


def lane_iota(shape):
    return lax.broadcasted_iota(jnp.int32, shape, len(shape) - 1)


def skew(row, shift):
    return pltpu.roll(
        jnp.broadcast_to(row, (BLK, LANES)), shift, 1, stride=1, stride_axis=0
    )


def pair(first, second):
    return (skew(first, 0), skew(first, BLK), skew(second, 0), skew(second, BLK))


def half_band(x):
    return x.astype(jnp.bfloat16)


def low_lanes():
    return lane_iota((BLK, LANES)) < BLK


def taps_kernel(row_ref, col_ref, taps):
    count = MODES * CH
    taps[...] = jnp.zeros_like(taps)
    for k in range(MODES):
        for t in range(TERMS):
            at = k * CH + 2 * t
            taps[at : at + 2, :TAPS] = row_ref[k, t].astype(jnp.float32)
            taps[count + at : count + at + 2, :TAPS] = col_ref[k, t].astype(jnp.float32)
    source = lax.broadcasted_iota(jnp.int32, (LANES, LANES), 0)
    mirror = (source + lane_iota((LANES, LANES))) % LANES == 0
    taps[2 * count :, :] = jnp.dot(
        taps[: 2 * count, :].astype(jnp.bfloat16),
        mirror.astype(jnp.bfloat16),
        preferred_element_type=jnp.float32,
    )
    taps[count : 2 * count, :] = pltpu.roll(taps[count : 2 * count, :], LANES - (TAPS - 1), 1)


def column_bands_kernel(taps, _, cf_ref):
    count = MODES * CH
    low = low_lanes()

    def step(n, carry):
        first = 3 * count + 4 * n
        for t in range(2):
            at = t * 2 * EXT
            a, a_far, b, b_far = pair(
                taps[pl.ds(first + 2 * t, 1), :], taps[pl.ds(first + 2 * t + 1, 1), :]
            )
            cf_ref[n, at : at + BLK, :] = half_band(jnp.where(low, a, b_far))
            cf_ref[n, at + BLK : at + EXT, :] = half_band(jnp.where(low, a_far, b))
            cf_ref[n, at + EXT : at + EXT + BLK, :] = half_band(jnp.where(low, -b, a_far))
            cf_ref[n, at + EXT + BLK : at + 2 * EXT, :] = half_band(jnp.where(low, -b_far, a))
        return carry

    lax.fori_loop(0, 2 * MODES, step, 0, unroll=3)


def column_adjoint_kernel(taps, _, ca_ref):
    count = MODES * CH
    low = low_lanes()

    def step(n, carry):
        first = count + 4 * n
        for t in range(2):
            a, a_far, b, b_far = pair(
                taps[pl.ds(first + 2 * t, 1), :], taps[pl.ds(first + 2 * t + 1, 1), :]
            )
            ca_ref[n * 2 + t, :BLK, :] = half_band(jnp.where(low, a, -b_far))
            ca_ref[n * 2 + t, BLK:EXT, :] = half_band(jnp.where(low, a_far, -b))
            ca_ref[n * 2 + t, EXT : EXT + BLK, :] = half_band(jnp.where(low, b, a_far))
            ca_ref[n * 2 + t, EXT + BLK :, :] = half_band(jnp.where(low, b_far, a))
        return carry

    lax.fori_loop(0, 2 * MODES, step, 0, unroll=3)


def build_bands(row_taps, col_taps, stages):
    vmem = pl.BlockSpec(memory_space=pltpu.VMEM)
    small = pltpu.CompilerParams(vmem_limit_bytes=4 << 20)
    taps = in_vmem(
        pl.pallas_call(
            taps_kernel,
            out_shape=pltpu.VMEM((4 * MODES * CH, LANES), jnp.float32),
            in_specs=[vmem] * 2,
            out_specs=vmem,
            compiler_params=small,
            name="taps",
        )(in_hbm(row_taps), in_hbm(col_taps))
    )
    built = [
        pl.pallas_call(
            kernel,
            out_shape=pltpu.VMEM(shape, jnp.bfloat16),
            in_specs=[vmem, pl.BlockSpec(memory_space=pl.ANY)],
            out_specs=vmem,
            compiler_params=small,
            name=name,
        )(taps, stage)
        for stage, (kernel, shape, name) in zip(
            stages,
            (
                (column_bands_kernel, (2 * MODES, CH * EXT // 2, LANES), "column_bands"),
                (column_adjoint_kernel, (4 * MODES, 2 * EXT, LANES), "column_adjoint"),
            ),
        )
    ]
    return [taps, *built]


def reversed_bits(value, bits):
    return sum(((value >> b) & 1) << (bits - 1 - b) for b in range(bits))


def main_kernel(
    devices,
    gathered_ref,
    taps,
    cf_ref,
    ca_ref,
    weight_hbm,
    target_hbm,
    resid_ref,
    grads_ref,
    *scratch,
):
    canvases, grads, sums = scratch[0:3], scratch[3:6], scratch[6:9]
    window, lhs, fields, slope, gw, gys, table, ids, sem = scratch[9:18]
    weight_ref, target_ref, r_ref, rt_ref, load_sems = scratch[18:]
    loads = [
        pltpu.make_async_copy(source, target, load_sems.at[n])
        for n, (source, target) in enumerate(
            (
                (weight_hbm, weight_ref),
                (target_hbm, target_ref),
            )
        )
    ]
    slabs = gathered_ref.shape[0] // devices
    count = slabs - 1
    places = LANES
    rows = BLK
    me = lax.axis_index("tx")
    bits = devices.bit_length() - 1
    bases = (HALF, HALF - rows, HALF + rows)
    for n, (other, missing) in enumerate(
        ((me, 0), (jnp.maximum(me - 1, 0), 0), (jnp.minimum(me + 1, devices - 1), BLK - MS))
    ):
        slab = gathered_ref[(other ^ me) * slabs + count].astype(jnp.float32).astype(jnp.int32)
        owner, local, row, col = slab[0:1] ^ me, slab[1:2], slab[2:3], slab[3:4]
        if n:
            row = jnp.where(other == me, missing, row)
        first_lane = (row + bases[n]) & 127
        lines = jnp.concatenate(
            [
                owner * slabs + local,
                reversed_bits(owner, bits) * count + local,
                col + HALF,
                first_lane,
                col,
                (LANES - first_lane) & 127,
                row,
                row,
            ],
            axis=0,
        )
        for j in range(places // STEP):
            table[j, 8 * n : 8 * n + 8, :] = (
                pltpu.roll(lines, LANES - STEP * j, 1) if j else lines
            )[:, :STEP]
    to_scalar = pltpu.make_async_copy(table, ids, sem)
    to_scalar.start()
    for load in loads:
        load.start()
    for canvas in canvases:
        canvas[...] = jnp.zeros_like(canvas)
    for acc in sums:
        acc[...] = jnp.zeros_like(acc)
    lanes8 = lane_iota((8, LANES))
    to_scalar.wait()

    def place(j, u):
        for n, canvas in enumerate(canvases):
            at, shift = ids[j, 8 * n + 2, u], ids[j, 8 * n + 3, u]
            moved = pltpu.roll(gathered_ref[ids[j, 8 * n, u]].astype(jnp.float32), shift, 1)
            nth = ((lanes8 - shift) & 127) >> 5
            spots = [pl.ds(at + k * CROWS + k, 8, stride=4) for k in range(4)]
            old = [canvas[spot, :] for spot in spots]
            for k, spot in enumerate(spots):
                canvas[spot, :] = old[k] + jnp.where(nth == k, moved, 0.0)

    @pl.loop(0, places // STEP)
    def _(j):
        for u in range(STEP):
            place(j, u)


    def of_above(k, lanes):
        return ((lanes - MS * k) & 127) < HALF

    def of_below(k, lanes):
        return ((lanes - MS * k) & 127) >= HALF + BLK

    used = slice(24, 288)
    wide = lane_iota((used.stop - used.start, LANES))
    columns = 0.0
    for k in range(4):
        lines = slice(k * CROWS + used.start, k * CROWS + used.stop)
        own, above, below = [canvas[lines, :] for canvas in canvases]
        joined = (
            own
            + jnp.where(of_above(k, wide), above, 0.0)
            + jnp.where(of_below(k, wide), below, 0.0)
        )
        columns = columns + (pltpu.roll(joined, LANES - MS * k, 1) if k else joined)
    columns = jnp.concatenate(
        [
            jnp.zeros((used.start, LANES), jnp.float32),
            columns,
            jnp.zeros((CROWS - used.stop, LANES), jnp.float32),
        ],
        axis=0,
    )
    for b in range(NBLK):
        window[:, b * LANES : (b + 1) * LANES] = jnp.transpose(
            columns[b * BLK : b * BLK + LANES]
        ).astype(jnp.bfloat16)
    low = lane_iota((EXT, LANES)) < BLK

    lanes16 = lane_iota((16, LANES))
    before = lanes16 < HALF
    until = lanes16 < HALF + BLK
    low64 = low_lanes()

    def row_bands(k):
        for c in range(CH):
            at = k * CH + c
            r_ref[at * BLK : (at + 1) * BLK, :] = half_band(skew(taps[at : at + 1, :], 0))

    def row_adjoint_bands(k):
        for n in (2 * k, 2 * k + 1):
            tap = 2 * MODES * CH + 4 * n
            for par in range(2):
                one, two = tap + par, tap + 2 + par
                a, a_far, b, b_far = pair(taps[one : one + 1, :], taps[two : two + 1, :])
                at = par * EXT
                rt_ref[n, at : at + BLK, :] = half_band(jnp.where(low64, a, b_far))
                rt_ref[n, at + BLK : at + EXT, :] = half_band(jnp.where(low64, a_far, b))

    loads[0].wait()
    row_bands(0)
    intensity = jnp.zeros((NBLK * rows, LANES), jnp.float32)
    for k in range(MODES):
        if k + 1 < MODES:
            row_bands(k + 1)
        row_adjoint_bands(k)
        field_y = jnp.dot(
            r_ref[k * CH * rows : (k + 1) * CH * rows, :],
            window[...],
            preferred_element_type=jnp.float32,
        ).astype(jnp.bfloat16)
        for c in range(CH):
            for b in range(NBLK):
                lhs[k % 2, b * rows : (b + 1) * rows, c * LANES : (c + 1) * LANES] = field_y[
                    c * rows : (c + 1) * rows, b * LANES : (b + 1) * LANES
                ]
        e = jnp.dot(
            lhs[k % 2],
            jnp.concatenate([cf_ref[2 * k], cf_ref[2 * k + 1]], axis=0),
            preferred_element_type=jnp.float32,
        )
        fields[k] = e
        intensity = intensity + weight_ref[k] * (e * e)
    loads[1].wait()
    low_rows = lane_iota((rows, LANES)) < BLK
    for b in range(NBLK):
        inten = intensity[b * rows : (b + 1) * rows]
        inten = inten + pltpu.roll(inten, BLK, 1)
        t = target_ref[:, (b // 2) * LANES : (b // 2 + 1) * LANES].astype(jnp.float32)
        other = pltpu.roll(t, BLK, 1)
        goal = jnp.where(low_rows, t, other) if b % 2 == 0 else jnp.where(low_rows, other, t)
        resist = jax.nn.sigmoid(steepness * (inten - threshold))
        resid = resist - goal
        slope[b * rows : (b + 1) * rows, :] = 2.0 * (resid * steepness * resist * (1.0 - resist))
        if b % 2 == 0:
            resid_ref[:, (b // 2) * LANES : (b // 2 + 1) * LANES] = resid
        else:
            resid_ref[:, (b // 2) * LANES + BLK : (b // 2 + 1) * LANES] = resid[:, BLK:]

    nothing = jnp.zeros((16, LANES), jnp.float32)
    for k in range(MODES):
        weight = weight_ref[k]
        for i in range(0, rows, 16):
            r31, r95 = [nothing], [nothing]
            for b in range(NBLK):
                at = slice(b * rows + i, b * rows + i + 16)
                g = weight * slope[at, :] * fields[k, at, :]
                r31.append(pltpu.roll(g, HALF, 1))
                r95.append(pltpu.roll(g, HALF + BLK, 1))
            r31.append(nothing)
            r95.append(nothing)
            for b in range(NBLK):
                at = slice(b * rows + i, b * rows + i + 16)
                re = jnp.where(before, r95[b], jnp.where(until, r31[b + 1], r95[b + 2]))
                im = jnp.where(before, r31[b], jnp.where(until, r95[b + 1], r31[b + 2]))
                gw[k % 2, at, :LANES] = re.astype(jnp.bfloat16)
                gw[k % 2, at, LANES:] = im.astype(jnp.bfloat16)
        for t in range(TERMS):
            gy = jnp.dot(
                gw[k % 2], ca_ref[k * TERMS + t], preferred_element_type=jnp.float32
            ).astype(jnp.bfloat16)
            at = (k * TERMS + t) * rows
            for b in range(NBLK):
                gys[at : at + rows, b * LANES : (b + 1) * LANES] = gy[b * rows : (b + 1) * rows]

    total = jnp.zeros((2 * EXT, NBLK * LANES), jnp.float32)
    for k in range(MODES):
        total = total + jnp.dot(
            jnp.concatenate([rt_ref[2 * k], rt_ref[2 * k + 1]], axis=1),
            gys[2 * k * LANES : 2 * (k + 1) * LANES, :],
            preferred_element_type=jnp.float32,
        )
    whole = []
    for h in range(2):
        v0 = total[:EXT, 2 * h * LANES : (2 * h + 1) * LANES]
        v1 = total[:EXT, (2 * h + 1) * LANES : (2 * h + 2) * LANES]
        u0 = total[EXT:, 2 * h * LANES : (2 * h + 1) * LANES]
        u1 = total[EXT:, (2 * h + 1) * LANES : (2 * h + 2) * LANES]
        whole.append(
            jnp.where(low, v0 + pltpu.roll(u0, BLK, 1), pltpu.roll(v1, BLK, 1) + u1)
        )
    columns = jnp.concatenate([jnp.transpose(side) for side in whole], axis=0)
    wide = lane_iota((W, LANES))
    for k in range(4):
        turned = pltpu.roll(columns, MS * k, 1) if k else columns
        lines = slice(k * W, (k + 1) * W)
        grads[0][lines, :] = turned
        grads[1][lines, :] = jnp.where(of_above(k, wide), turned, 0.0)
        grads[2][lines, :] = jnp.where(of_below(k, wide), turned, 0.0)

    def gather(j, u):
        for n, acc in enumerate(sums):
            m, shift, at, back = [ids[j, 8 * n + line, u] for line in (1, 3, 4, 5)]
            nth = (lanes8 - shift) & 127
            patch = None
            for k in range(4):
                rows_k = grads[n][pl.ds(at + k * W + k, 8, stride=4), :]
                patch = jnp.where(nth >= MS * k, rows_k, patch) if k else rows_k
            acc[m] += pltpu.roll(patch, back, 1)

    @pl.loop(0, places // STEP)
    def _(j):
        for u in range(STEP):
            gather(j, u)

    grads_ref[...] = (sums[0][...] + sums[1][...] + sums[2][...]).reshape(grads_ref.shape)


def main_step(weights, gathered, target, bands):
    devices, slabs = gathered.shape[:2]
    count = slabs - 1
    vmem = pl.BlockSpec(memory_space=pltpu.VMEM)
    return pl.pallas_call(
        functools.partial(main_kernel, devices),
        out_shape=(
            jax.ShapeDtypeStruct(target.shape, jnp.float32),
            pltpu.VMEM((devices, count, 8, LANES), jnp.float32),
        ),
        in_specs=[vmem] * 4 + [pl.BlockSpec(memory_space=pl.ANY)] * 2,
        out_specs=[vmem] * 2,
        scratch_shapes=[
            *[pltpu.VMEM((4 * CROWS, LANES), jnp.float32)] * 3,
            *[pltpu.VMEM((4 * W, LANES), jnp.float32)] * 3,
            *[pltpu.VMEM((devices * count, 8, LANES), jnp.float32)] * 3,
            pltpu.VMEM((EXT, NBLK * LANES), jnp.bfloat16),
            pltpu.VMEM((2, NBLK * BLK, CH * LANES), jnp.bfloat16),
            pltpu.VMEM((MODES, NBLK * BLK, LANES), jnp.float32),
            pltpu.VMEM((NBLK * BLK, LANES), jnp.float32),
            pltpu.VMEM((2, NBLK * BLK, 2 * LANES), jnp.bfloat16),
            pltpu.VMEM((MODES * TERMS * BLK, NBLK * LANES), jnp.bfloat16),
            pltpu.VMEM((LANES // STEP, 24, STEP), jnp.int32),
            pltpu.SMEM((LANES // STEP, 24, STEP), jnp.int32),
            pltpu.SemaphoreType.DMA,
            pltpu.SMEM(weights.shape, jnp.float32),
            pltpu.VMEM(target.shape, jnp.bfloat16),
            pltpu.VMEM((MODES * CH * BLK, LANES), jnp.bfloat16),
            pltpu.VMEM((2 * MODES, 2 * EXT, LANES), jnp.bfloat16),
            pltpu.SemaphoreType.DMA((2,)),
        ],
        compiler_params=pltpu.CompilerParams(vmem_limit_bytes=28 << 20),
        name="imaging",
    )(
        in_vmem(gathered.reshape(devices * slabs, 8, LANES)),
        *[in_vmem(x) for x in bands],
        in_hbm(weights),
        in_hbm(target),
    )


def flip_pixels(slabs, cells):
    lanes = lane_iota((8, LANES))

    def chosen(parts):
        out = parts[0]
        for n, part in enumerate(parts):
            if n:
                out = jnp.where(lanes >= MS * n, part, out)
        return out

    def turned(x, blocks):
        return pltpu.roll(x, (MS * blocks) % LANES, 1) if blocks else x

    cells[MS:, :] = jnp.zeros((LANES - MS, LANES), jnp.float32)
    for k in range(4):
        cells[pl.ds(k, 8, stride=4), :] = chosen([turned(x, m - k) for m, x in enumerate(slabs)])
    cells[...] = jnp.transpose(cells[...])
    return [
        chosen([turned(cells[pl.ds(MS * m + k, 8, stride=4), :], k) for k in range(4)])
        for m in range(len(slabs))
    ]


def pack_kernel(masters_ref, owner_ref, local_ref, row_ref, col_ref, out_ref, spread, cells):
    count = masters_ref.shape[0]
    for s in range(8):
        spread[pl.ds(s, count, stride=8), :] = masters_ref[:, s * LANES : (s + 1) * LANES]
    flipped = flip_pixels([spread[8 * m : 8 * m + 8, :] for m in range(count)], cells)
    for m, slab in enumerate(flipped):
        spread[8 * m : 8 * m + 8, :] = slab
    spread[8 * count :, :] = jnp.zeros((8, LANES), jnp.float32)
    for n, ref in enumerate((owner_ref, local_ref, row_ref, col_ref)):
        spread[8 * count + n : 8 * count + n + 1, :] = ref[...].astype(jnp.float32)
    out_ref[...] = spread[...].reshape(out_ref.shape).astype(jnp.bfloat16)


def pack(masters, *places):
    count = masters.shape[0]
    vmem = pl.BlockSpec(memory_space=pltpu.VMEM)
    return pl.pallas_call(
        pack_kernel,
        out_shape=pltpu.VMEM((1, count + 1, 8, LANES), jnp.bfloat16),
        in_specs=[vmem] * 5,
        out_specs=vmem,
        scratch_shapes=[
            pltpu.VMEM((8 * count + 8, LANES), jnp.float32),
            pltpu.VMEM((LANES, LANES), jnp.float32),
        ],
        compiler_params=pltpu.CompilerParams(vmem_limit_bytes=4 << 20),
        name="pack",
    )(in_hbm(masters), *[in_hbm(p.reshape(1, LANES)) for p in places])


def update_kernel(
    kept_ref, sent_ref, velocity_ref, masters_ref, velocity_out, masters_out, sums, cells
):
    count = velocity_ref.shape[0]
    flipped = flip_pixels([kept_ref[0, m] + sent_ref[0, m] for m in range(count)], cells)
    for m, slab in enumerate(flipped):
        sums[8 * m : 8 * m + 8, :] = slab
    for s in range(8):
        at = slice(s * LANES, (s + 1) * LANES)
        gradient = sums[pl.ds(s, count, stride=8), :]
        velocity = momentum * velocity_ref[:, at] + gradient
        velocity_out[:, at] = velocity
        masters_out[:, at] = masters_ref[:, at] - step_size * velocity


def update(kept, sent, velocity, masters):
    vmem = pl.BlockSpec(memory_space=pltpu.VMEM)
    return pl.pallas_call(
        update_kernel,
        out_shape=(jax.ShapeDtypeStruct(velocity.shape, jnp.float32),) * 2,
        in_specs=[vmem] * 4,
        out_specs=[vmem] * 2,
        scratch_shapes=[
            pltpu.VMEM((8 * velocity.shape[0], LANES), jnp.float32),
            pltpu.VMEM((LANES, LANES), jnp.float32),
        ],
        compiler_params=pltpu.CompilerParams(vmem_limit_bytes=4 << 20),
        name="update",
    )(kept, sent, velocity, masters)


def swap(value, bit, devices):
    return lax.ppermute(value, "tx", [(i, i ^ bit) for i in range(devices)])


def on_device(
    masters,
    velocity,
    place_owner,
    place_local,
    place_row,
    place_col,
    row_taps,
    col_taps,
    mode_weights,
    target,
):
    devices = lax.axis_size("tx")
    bits = devices.bit_length() - 1
    held = pack(masters, place_owner, place_local, place_row, place_col)
    stages = []
    for b in range(bits):
        held = jnp.concatenate([held, swap(held, 1 << b, devices)], axis=0)
        stages.append(held)
    bands = build_bands(row_taps, col_taps, (stages[0], stages[-2]))
    resid, grads = main_step(mode_weights, held, target, bands)
    for b in range(bits):
        half = grads.shape[0] // 2
        sent = swap(grads[half:], 1 << b, devices)
        if b < bits - 1:
            grads = grads[:half] + sent
    velocity_new, masters_new = update(grads, sent, velocity, masters)
    return resid, velocity_new, masters_new


def solution(mesh):
    return jax.shard_map(
        on_device,
        mesh=mesh,
        in_specs=(
            P(("groups", "tx"), None),
            P(("groups", "tx"), None),
            P(("groups", "tx"), None),
            P(("groups", "tx")),
            P(("groups", "tx")),
            P(("groups", "tx")),
            P(),
            P(),
            P(),
            P(("groups", "tx"), None),
        ),
        out_specs=(P(("groups", "tx"), None), P(("groups", "tx"), None), P(("groups", "tx"), None)),
        check_vma=False,
    )
```

```python
import functools
import jax
import jax.numpy as jnp
from jax import lax
from jax.experimental import pallas as pl
from jax.experimental.pallas import tpu as pltpu
from jax.sharding import PartitionSpec as P

W = 256
MS = 32
TAPS = 63
HALF = 31
TERMS = 4
MODES = 12
CH = 2 * TERMS
LANES = 128
BLK = 64
EXT = 128
STEP = 32
NBLK = W // BLK
CROWS = 320

steepness = 0.5
threshold = 8.0
momentum = 0.9
step_size = 0.05


def in_vmem(x):
    return pltpu.with_memory_space_constraint(x, pltpu.VMEM)


def in_hbm(x):
    return pltpu.with_memory_space_constraint(x, pltpu.HBM)


def lane_iota(shape):
    return lax.broadcasted_iota(jnp.int32, shape, len(shape) - 1)


def skew(row, shift):
    return pltpu.roll(
        jnp.broadcast_to(row, (BLK, LANES)), shift, 1, stride=1, stride_axis=0
    )


def pair(first, second):
    return (skew(first, 0), skew(first, BLK), skew(second, 0), skew(second, BLK))


def half_band(x):
    return x.astype(jnp.bfloat16)


def low_lanes():
    return lane_iota((BLK, LANES)) < BLK


def taps_kernel(row_ref, col_ref, taps):
    count = MODES * CH
    taps[...] = jnp.zeros_like(taps)
    for k in range(MODES):
        for t in range(TERMS):
            at = k * CH + 2 * t
            taps[at : at + 2, :TAPS] = row_ref[k, t].astype(jnp.float32)
            taps[count + at : count + at + 2, :TAPS] = col_ref[k, t].astype(jnp.float32)
    source = lax.broadcasted_iota(jnp.int32, (LANES, LANES), 0)
    mirror = (source + lane_iota((LANES, LANES))) % LANES == 0
    taps[2 * count :, :] = jnp.dot(
        taps[: 2 * count, :].astype(jnp.bfloat16),
        mirror.astype(jnp.bfloat16),
        preferred_element_type=jnp.float32,
    )
    taps[count : 2 * count, :] = pltpu.roll(taps[count : 2 * count, :], LANES - (TAPS - 1), 1)


def column_bands_kernel(taps, _, cf_ref):
    count = MODES * CH
    low = low_lanes()

    def step(n, carry):
        first = 3 * count + 4 * n
        for t in range(2):
            at = t * 2 * EXT
            a, a_far, b, b_far = pair(
                taps[pl.ds(first + 2 * t, 1), :], taps[pl.ds(first + 2 * t + 1, 1), :]
            )
            cf_ref[n, at : at + BLK, :] = half_band(jnp.where(low, a, b_far))
            cf_ref[n, at + BLK : at + EXT, :] = half_band(jnp.where(low, a_far, b))
            cf_ref[n, at + EXT : at + EXT + BLK, :] = half_band(jnp.where(low, -b, a_far))
            cf_ref[n, at + EXT + BLK : at + 2 * EXT, :] = half_band(jnp.where(low, -b_far, a))
        return carry

    lax.fori_loop(0, 2 * MODES, step, 0, unroll=3)


def row_adjoint_kernel(taps, _, rt_ref):
    low = low_lanes()

    def step(n, carry):
        first = 2 * MODES * CH + 4 * n
        for par in range(2):
            a, a_far, b, b_far = pair(
                taps[pl.ds(first + par, 1), :], taps[pl.ds(first + 2 + par, 1), :]
            )
            rt_ref[n, par * EXT : par * EXT + BLK, :] = half_band(jnp.where(low, a, b_far))
            rt_ref[n, par * EXT + BLK : (par + 1) * EXT, :] = half_band(jnp.where(low, a_far, b))
        return carry

    lax.fori_loop(0, 2 * MODES, step, 0, unroll=3)


def column_adjoint_kernel(taps, _, ca_ref):
    count = MODES * CH
    low = low_lanes()

    def step(n, carry):
        first = count + 4 * n
        for t in range(2):
            a, a_far, b, b_far = pair(
                taps[pl.ds(first + 2 * t, 1), :], taps[pl.ds(first + 2 * t + 1, 1), :]
            )
            ca_ref[n * 2 + t, :BLK, :] = half_band(jnp.where(low, a, -b_far))
            ca_ref[n * 2 + t, BLK:EXT, :] = half_band(jnp.where(low, a_far, -b))
            ca_ref[n * 2 + t, EXT : EXT + BLK, :] = half_band(jnp.where(low, b, a_far))
            ca_ref[n * 2 + t, EXT + BLK :, :] = half_band(jnp.where(low, b_far, a))
        return carry

    lax.fori_loop(0, 2 * MODES, step, 0, unroll=3)


def build_bands(row_taps, col_taps, stages):
    vmem = pl.BlockSpec(memory_space=pltpu.VMEM)
    small = pltpu.CompilerParams(vmem_limit_bytes=4 << 20)
    taps = in_vmem(
        pl.pallas_call(
            taps_kernel,
            out_shape=pltpu.VMEM((4 * MODES * CH, LANES), jnp.float32),
            in_specs=[vmem] * 2,
            out_specs=vmem,
            compiler_params=small,
            name="taps",
        )(in_hbm(row_taps), in_hbm(col_taps))
    )
    built = [
        pl.pallas_call(
            kernel,
            out_shape=pltpu.VMEM(shape, jnp.bfloat16),
            in_specs=[vmem, pl.BlockSpec(memory_space=pl.ANY)],
            out_specs=vmem,
            compiler_params=small,
            name=name,
        )(taps, stage)
        for stage, (kernel, shape, name) in zip(
            stages,
            (
                (column_bands_kernel, (2 * MODES, CH * EXT // 2, LANES), "column_bands"),
                (row_adjoint_kernel, (2 * MODES, 2 * EXT, LANES), "row_adjoint"),
                (column_adjoint_kernel, (4 * MODES, 2 * EXT, LANES), "column_adjoint"),
            ),
        )
    ]
    return [taps, *built]


def reversed_bits(value, bits):
    return sum(((value >> b) & 1) << (bits - 1 - b) for b in range(bits))


def main_kernel(
    devices,
    gathered_ref,
    taps,
    cf_ref,
    rt_ref,
    ca_ref,
    weight_hbm,
    target_hbm,
    resid_hbm,
    grads_ref,
    *scratch,
):
    canvases, grads, sums = scratch[0:3], scratch[3:6], scratch[6:9]
    window, lhs, fields, slope, gw, gys, table, ids, sem = scratch[9:18]
    weight_ref, target_ref, resid_ref, r_ref, load_sems = scratch[18:]
    loads = [
        pltpu.make_async_copy(source, target, load_sems.at[n])
        for n, (source, target) in enumerate(
            (
                (weight_hbm, weight_ref),
                (target_hbm, target_ref),
                (resid_ref, resid_hbm),
            )
        )
    ]
    slabs = gathered_ref.shape[0] // devices
    count = slabs - 1
    places = LANES
    rows = BLK
    me = lax.axis_index("tx")
    bits = devices.bit_length() - 1
    bases = (HALF, HALF - rows, HALF + rows)
    for n, (other, missing) in enumerate(
        ((me, 0), (jnp.maximum(me - 1, 0), 0), (jnp.minimum(me + 1, devices - 1), BLK - MS))
    ):
        slab = gathered_ref[(other ^ me) * slabs + count].astype(jnp.float32).astype(jnp.int32)
        owner, local, row, col = slab[0:1] ^ me, slab[1:2], slab[2:3], slab[3:4]
        if n:
            row = jnp.where(other == me, missing, row)
        first_lane = (row + bases[n]) & 127
        lines = jnp.concatenate(
            [
                owner * slabs + local,
                reversed_bits(owner, bits) * count + local,
                col + HALF,
                first_lane,
                col,
                (LANES - first_lane) & 127,
                row,
                row,
            ],
            axis=0,
        )
        for j in range(places // STEP):
            table[j, 8 * n : 8 * n + 8, :] = (
                pltpu.roll(lines, LANES - STEP * j, 1) if j else lines
            )[:, :STEP]
    to_scalar = pltpu.make_async_copy(table, ids, sem)
    to_scalar.start()
    for load in loads[:2]:
        load.start()
    for canvas in canvases:
        canvas[...] = jnp.zeros_like(canvas)
    for acc in sums:
        acc[...] = jnp.zeros_like(acc)
    lanes8 = lane_iota((8, LANES))
    to_scalar.wait()

    def place(j, u):
        for n, canvas in enumerate(canvases):
            at, shift = ids[j, 8 * n + 2, u], ids[j, 8 * n + 3, u]
            moved = pltpu.roll(gathered_ref[ids[j, 8 * n, u]].astype(jnp.float32), shift, 1)
            nth = ((lanes8 - shift) & 127) >> 5
            spots = [pl.ds(at + k * CROWS + k, 8, stride=4) for k in range(4)]
            old = [canvas[spot, :] for spot in spots]
            for k, spot in enumerate(spots):
                canvas[spot, :] = old[k] + jnp.where(nth == k, moved, 0.0)

    @pl.loop(0, places // STEP)
    def _(j):
        for u in range(STEP):
            place(j, u)


    def of_above(k, lanes):
        return ((lanes - MS * k) & 127) < HALF

    def of_below(k, lanes):
        return ((lanes - MS * k) & 127) >= HALF + BLK

    used = slice(24, 288)
    wide = lane_iota((used.stop - used.start, LANES))
    columns = 0.0
    for k in range(4):
        lines = slice(k * CROWS + used.start, k * CROWS + used.stop)
        own, above, below = [canvas[lines, :] for canvas in canvases]
        joined = (
            own
            + jnp.where(of_above(k, wide), above, 0.0)
            + jnp.where(of_below(k, wide), below, 0.0)
        )
        columns = columns + (pltpu.roll(joined, LANES - MS * k, 1) if k else joined)
    columns = jnp.concatenate(
        [
            jnp.zeros((used.start, LANES), jnp.float32),
            columns,
            jnp.zeros((CROWS - used.stop, LANES), jnp.float32),
        ],
        axis=0,
    )
    for b in range(NBLK):
        window[:, b * LANES : (b + 1) * LANES] = jnp.transpose(
            columns[b * BLK : b * BLK + LANES]
        ).astype(jnp.bfloat16)
    low = lane_iota((EXT, LANES)) < BLK

    lanes16 = lane_iota((16, LANES))
    before = lanes16 < HALF
    until = lanes16 < HALF + BLK
    def row_bands(k):
        for c in range(CH):
            at = k * CH + c
            r_ref[at * BLK : (at + 1) * BLK, :] = half_band(skew(taps[at : at + 1, :], 0))

    loads[0].wait()
    row_bands(0)
    intensity = jnp.zeros((NBLK * rows, LANES), jnp.float32)
    for k in range(MODES):
        if k + 1 < MODES:
            row_bands(k + 1)
        field_y = jnp.dot(
            r_ref[k * CH * rows : (k + 1) * CH * rows, :],
            window[...],
            preferred_element_type=jnp.float32,
        ).astype(jnp.bfloat16)
        for c in range(CH):
            for b in range(NBLK):
                lhs[k % 2, b * rows : (b + 1) * rows, c * LANES : (c + 1) * LANES] = field_y[
                    c * rows : (c + 1) * rows, b * LANES : (b + 1) * LANES
                ]
        e = jnp.dot(
            lhs[k % 2],
            jnp.concatenate([cf_ref[2 * k], cf_ref[2 * k + 1]], axis=0),
            preferred_element_type=jnp.float32,
        )
        fields[k] = e
        intensity = intensity + weight_ref[k] * (e * e)
    loads[1].wait()
    low_rows = lane_iota((rows, LANES)) < BLK

    def halves(x, first):
        turned = pltpu.roll(x, BLK, 1)
        return (jnp.where(low_rows, x, turned), jnp.where(low_rows, turned, x))[first]

    for h in range(2):
        one = intensity[2 * h * rows : (2 * h + 1) * rows]
        two = intensity[(2 * h + 1) * rows : (2 * h + 2) * rows]
        inten = jnp.where(
            low_rows, one + pltpu.roll(one, BLK, 1), two + pltpu.roll(two, BLK, 1)
        )
        at = slice(h * LANES, (h + 1) * LANES)
        resist = jax.nn.sigmoid(steepness * (inten - threshold))
        resid = resist - target_ref[:, at].astype(jnp.float32)
        resid_ref[:, at] = resid
        change = 2.0 * (resid * steepness * resist * (1.0 - resist))
        for n in range(2):
            slope[(2 * h + n) * rows : (2 * h + n + 1) * rows, :] = halves(change, n)

    loads[2].start()
    nothing = jnp.zeros((16, LANES), jnp.float32)
    for k in range(MODES):
        weight = weight_ref[k]
        for i in range(0, rows, 16):
            r31, r95 = [nothing], [nothing]
            for b in range(NBLK):
                at = slice(b * rows + i, b * rows + i + 16)
                g = weight * slope[at, :] * fields[k, at, :]
                r31.append(pltpu.roll(g, HALF, 1))
                r95.append(pltpu.roll(g, HALF + BLK, 1))
            r31.append(nothing)
            r95.append(nothing)
            for b in range(NBLK):
                at = slice(b * rows + i, b * rows + i + 16)
                re = jnp.where(before, r95[b], jnp.where(until, r31[b + 1], r95[b + 2]))
                im = jnp.where(before, r31[b], jnp.where(until, r95[b + 1], r31[b + 2]))
                gw[k % 2, at, :LANES] = re.astype(jnp.bfloat16)
                gw[k % 2, at, LANES:] = im.astype(jnp.bfloat16)
        for t in range(TERMS):
            gy = jnp.dot(
                gw[k % 2], ca_ref[k * TERMS + t], preferred_element_type=jnp.float32
            ).astype(jnp.bfloat16)
            at = (k * TERMS + t) * rows
            for b in range(NBLK):
                gys[at : at + rows, b * LANES : (b + 1) * LANES] = gy[b * rows : (b + 1) * rows]

    total = jnp.zeros((2 * EXT, NBLK * LANES), jnp.float32)
    for k in range(MODES):
        total = total + jnp.dot(
            jnp.concatenate([rt_ref[2 * k], rt_ref[2 * k + 1]], axis=1),
            gys[2 * k * LANES : 2 * (k + 1) * LANES, :],
            preferred_element_type=jnp.float32,
        )
    whole = []
    for h in range(2):
        v0 = total[:EXT, 2 * h * LANES : (2 * h + 1) * LANES]
        v1 = total[:EXT, (2 * h + 1) * LANES : (2 * h + 2) * LANES]
        u0 = total[EXT:, 2 * h * LANES : (2 * h + 1) * LANES]
        u1 = total[EXT:, (2 * h + 1) * LANES : (2 * h + 2) * LANES]
        whole.append(
            jnp.where(low, v0 + pltpu.roll(u0, BLK, 1), pltpu.roll(v1, BLK, 1) + u1)
        )
    columns = jnp.concatenate([jnp.transpose(side) for side in whole], axis=0)
    wide = lane_iota((W, LANES))
    for k in range(4):
        turned = pltpu.roll(columns, MS * k, 1) if k else columns
        lines = slice(k * W, (k + 1) * W)
        grads[0][lines, :] = turned
        grads[1][lines, :] = jnp.where(of_above(k, wide), turned, 0.0)
        grads[2][lines, :] = jnp.where(of_below(k, wide), turned, 0.0)

    def gather(j, u):
        for n, acc in enumerate(sums):
            m, shift, at, back = [ids[j, 8 * n + line, u] for line in (1, 3, 4, 5)]
            nth = (lanes8 - shift) & 127
            patch = None
            for k in range(4):
                rows_k = grads[n][pl.ds(at + k * W + k, 8, stride=4), :]
                patch = jnp.where(nth >= MS * k, rows_k, patch) if k else rows_k
            acc[m] += pltpu.roll(patch, back, 1)

    @pl.loop(0, places // STEP)
    def _(j):
        for u in range(STEP):
            gather(j, u)

    grads_ref[...] = (sums[0][...] + sums[1][...] + sums[2][...]).reshape(grads_ref.shape)
    loads[2].wait()


def main_step(weights, gathered, target, bands):
    devices, slabs = gathered.shape[:2]
    count = slabs - 1
    vmem = pl.BlockSpec(memory_space=pltpu.VMEM)
    return pl.pallas_call(
        functools.partial(main_kernel, devices),
        out_shape=(
            pltpu.HBM(target.shape, jnp.float32),
            pltpu.VMEM((devices, count, 8, LANES), jnp.float32),
        ),
        in_specs=[vmem] * 5 + [pl.BlockSpec(memory_space=pl.ANY)] * 2,
        out_specs=[pl.BlockSpec(memory_space=pl.ANY), vmem],
        scratch_shapes=[
            *[pltpu.VMEM((4 * CROWS, LANES), jnp.float32)] * 3,
            *[pltpu.VMEM((4 * W, LANES), jnp.float32)] * 3,
            *[pltpu.VMEM((devices * count, 8, LANES), jnp.float32)] * 3,
            pltpu.VMEM((EXT, NBLK * LANES), jnp.bfloat16),
            pltpu.VMEM((2, NBLK * BLK, CH * LANES), jnp.bfloat16),
            pltpu.VMEM((MODES, NBLK * BLK, LANES), jnp.float32),
            pltpu.VMEM((NBLK * BLK, LANES), jnp.float32),
            pltpu.VMEM((2, NBLK * BLK, 2 * LANES), jnp.bfloat16),
            pltpu.VMEM((MODES * TERMS * BLK, NBLK * LANES), jnp.bfloat16),
            pltpu.VMEM((LANES // STEP, 24, STEP), jnp.int32),
            pltpu.SMEM((LANES // STEP, 24, STEP), jnp.int32),
            pltpu.SemaphoreType.DMA,
            pltpu.SMEM(weights.shape, jnp.float32),
            pltpu.VMEM(target.shape, jnp.bfloat16),
            pltpu.VMEM(target.shape, jnp.float32),
            pltpu.VMEM((MODES * CH * BLK, LANES), jnp.bfloat16),
            pltpu.SemaphoreType.DMA((3,)),
        ],
        compiler_params=pltpu.CompilerParams(vmem_limit_bytes=28 << 20),
        name="imaging",
    )(
        in_vmem(gathered.reshape(devices * slabs, 8, LANES)),
        *[in_vmem(x) for x in bands],
        in_hbm(weights),
        in_hbm(target),
    )


def flip_pixels(slabs, cells):
    lanes = lane_iota((8, LANES))

    def chosen(parts):
        out = parts[0]
        for n, part in enumerate(parts):
            if n:
                out = jnp.where(lanes >= MS * n, part, out)
        return out

    def turned(x, blocks):
        return pltpu.roll(x, (MS * blocks) % LANES, 1) if blocks else x

    cells[MS:, :] = jnp.zeros((LANES - MS, LANES), jnp.float32)
    for k in range(4):
        cells[pl.ds(k, 8, stride=4), :] = chosen([turned(x, m - k) for m, x in enumerate(slabs)])
    cells[...] = jnp.transpose(cells[...])
    return [
        chosen([turned(cells[pl.ds(MS * m + k, 8, stride=4), :], k) for k in range(4)])
        for m in range(len(slabs))
    ]


def pack_kernel(masters_ref, owner_ref, local_ref, row_ref, col_ref, out_ref, spread, cells):
    count = masters_ref.shape[0]
    for s in range(8):
        spread[pl.ds(s, count, stride=8), :] = masters_ref[:, s * LANES : (s + 1) * LANES]
    flipped = flip_pixels([spread[8 * m : 8 * m + 8, :] for m in range(count)], cells)
    for m, slab in enumerate(flipped):
        spread[8 * m : 8 * m + 8, :] = slab
    spread[8 * count :, :] = jnp.zeros((8, LANES), jnp.float32)
    for n, ref in enumerate((owner_ref, local_ref, row_ref, col_ref)):
        spread[8 * count + n : 8 * count + n + 1, :] = ref[...].astype(jnp.float32)
    out_ref[...] = spread[...].reshape(out_ref.shape).astype(jnp.bfloat16)


def pack(masters, *places):
    count = masters.shape[0]
    vmem = pl.BlockSpec(memory_space=pltpu.VMEM)
    return pl.pallas_call(
        pack_kernel,
        out_shape=pltpu.VMEM((1, count + 1, 8, LANES), jnp.bfloat16),
        in_specs=[vmem] * 5,
        out_specs=vmem,
        scratch_shapes=[
            pltpu.VMEM((8 * count + 8, LANES), jnp.float32),
            pltpu.VMEM((LANES, LANES), jnp.float32),
        ],
        compiler_params=pltpu.CompilerParams(vmem_limit_bytes=4 << 20),
        name="pack",
    )(in_hbm(masters), *[in_hbm(p.reshape(1, LANES)) for p in places])


def update_kernel(
    kept_ref, sent_ref, velocity_ref, masters_ref, velocity_out, masters_out, sums, cells
):
    count = velocity_ref.shape[0]
    flipped = flip_pixels([kept_ref[0, m] + sent_ref[0, m] for m in range(count)], cells)
    for m, slab in enumerate(flipped):
        sums[8 * m : 8 * m + 8, :] = slab
    for s in range(8):
        at = slice(s * LANES, (s + 1) * LANES)
        gradient = sums[pl.ds(s, count, stride=8), :]
        velocity = momentum * velocity_ref[:, at] + gradient
        velocity_out[:, at] = velocity
        masters_out[:, at] = masters_ref[:, at] - step_size * velocity


def update(kept, sent, velocity, masters):
    vmem = pl.BlockSpec(memory_space=pltpu.VMEM)
    return pl.pallas_call(
        update_kernel,
        out_shape=(jax.ShapeDtypeStruct(velocity.shape, jnp.float32),) * 2,
        in_specs=[vmem] * 4,
        out_specs=[vmem] * 2,
        scratch_shapes=[
            pltpu.VMEM((8 * velocity.shape[0], LANES), jnp.float32),
            pltpu.VMEM((LANES, LANES), jnp.float32),
        ],
        compiler_params=pltpu.CompilerParams(vmem_limit_bytes=4 << 20),
        name="update",
    )(kept, sent, velocity, masters)


def swap(value, bit, devices):
    return lax.ppermute(value, "tx", [(i, i ^ bit) for i in range(devices)])


def on_device(
    masters,
    velocity,
    place_owner,
    place_local,
    place_row,
    place_col,
    row_taps,
    col_taps,
    mode_weights,
    target,
):
    devices = lax.axis_size("tx")
    bits = devices.bit_length() - 1
    held = pack(masters, place_owner, place_local, place_row, place_col)
    stages = []
    for b in range(bits):
        held = jnp.concatenate([held, swap(held, 1 << b, devices)], axis=0)
        stages.append(held)
    bands = build_bands(row_taps, col_taps, stages[-4:-1])
    resid, grads = main_step(mode_weights, held, target, bands)
    for b in range(bits):
        half = grads.shape[0] // 2
        sent = swap(grads[half:], 1 << b, devices)
        if b < bits - 1:
            grads = grads[:half] + sent
    velocity_new, masters_new = update(grads, sent, velocity, masters)
    return resid, velocity_new, masters_new


def solution(mesh):
    return jax.shard_map(
        on_device,
        mesh=mesh,
        in_specs=(
            P(("groups", "tx"), None),
            P(("groups", "tx"), None),
            P(("groups", "tx"), None),
            P(("groups", "tx")),
            P(("groups", "tx")),
            P(("groups", "tx")),
            P(),
            P(),
            P(),
            P(("groups", "tx"), None),
        ),
        out_specs=(P(("groups", "tx"), None), P(("groups", "tx"), None), P(("groups", "tx"), None)),
        check_vma=False,
    )
```

```python
import functools
import jax
import jax.numpy as jnp
from jax import lax
from jax.experimental import pallas as pl
from jax.experimental.pallas import tpu as pltpu
from jax.sharding import PartitionSpec as P

W = 256
MS = 32
TAPS = 63
HALF = 31
TERMS = 4
MODES = 12
CH = 2 * TERMS
LANES = 128
BLK = 64
EXT = 128
STEP = 32
NBLK = W // BLK
CROWS = 320

steepness = 0.5
threshold = 8.0
momentum = 0.9
step_size = 0.05


def in_vmem(x):
    return pltpu.with_memory_space_constraint(x, pltpu.VMEM)


def in_hbm(x):
    return pltpu.with_memory_space_constraint(x, pltpu.HBM)


def lane_iota(shape):
    return lax.broadcasted_iota(jnp.int32, shape, len(shape) - 1)


def skew(row, shift):
    return pltpu.roll(
        jnp.broadcast_to(row, (BLK, LANES)), shift, 1, stride=1, stride_axis=0
    )


def pair(first, second):
    return (skew(first, 0), skew(first, BLK), skew(second, 0), skew(second, BLK))


def half_band(x):
    return x.astype(jnp.bfloat16)


def low_lanes():
    return lane_iota((BLK, LANES)) < BLK


def taps_kernel(row_ref, col_ref, taps):
    count = MODES * CH
    taps[...] = jnp.zeros_like(taps)
    for k in range(MODES):
        for t in range(TERMS):
            at = k * CH + 2 * t
            taps[at : at + 2, :TAPS] = row_ref[k, t].astype(jnp.float32)
            taps[count + at : count + at + 2, :TAPS] = col_ref[k, t].astype(jnp.float32)
    source = lax.broadcasted_iota(jnp.int32, (LANES, LANES), 0)
    mirror = (source + lane_iota((LANES, LANES))) % LANES == 0
    taps[2 * count :, :] = jnp.dot(
        taps[: 2 * count, :].astype(jnp.bfloat16),
        mirror.astype(jnp.bfloat16),
        preferred_element_type=jnp.float32,
    )
    taps[count : 2 * count, :] = pltpu.roll(taps[count : 2 * count, :], LANES - (TAPS - 1), 1)


def column_bands_kernel(taps, _, cf_ref):
    count = MODES * CH
    low = low_lanes()

    def step(n, carry):
        first = 3 * count + 4 * n
        for t in range(2):
            at = t * 2 * EXT
            a, a_far, b, b_far = pair(
                taps[pl.ds(first + 2 * t, 1), :], taps[pl.ds(first + 2 * t + 1, 1), :]
            )
            cf_ref[n, at : at + BLK, :] = half_band(jnp.where(low, a, b_far))
            cf_ref[n, at + BLK : at + EXT, :] = half_band(jnp.where(low, a_far, b))
            cf_ref[n, at + EXT : at + EXT + BLK, :] = half_band(jnp.where(low, -b, a_far))
            cf_ref[n, at + EXT + BLK : at + 2 * EXT, :] = half_band(jnp.where(low, -b_far, a))
        return carry

    lax.fori_loop(0, 2 * MODES, step, 0, unroll=3)


def column_adjoint_kernel(taps, _, ca_ref):
    count = MODES * CH
    low = low_lanes()

    def step(n, carry):
        first = count + 4 * n
        for t in range(2):
            a, a_far, b, b_far = pair(
                taps[pl.ds(first + 2 * t, 1), :], taps[pl.ds(first + 2 * t + 1, 1), :]
            )
            ca_ref[n * 2 + t, :BLK, :] = half_band(jnp.where(low, a, -b_far))
            ca_ref[n * 2 + t, BLK:EXT, :] = half_band(jnp.where(low, a_far, -b))
            ca_ref[n * 2 + t, EXT : EXT + BLK, :] = half_band(jnp.where(low, b, a_far))
            ca_ref[n * 2 + t, EXT + BLK :, :] = half_band(jnp.where(low, b_far, a))
        return carry

    lax.fori_loop(0, 2 * MODES, step, 0, unroll=3)


def build_bands(row_taps, col_taps, stages):
    vmem = pl.BlockSpec(memory_space=pltpu.VMEM)
    small = pltpu.CompilerParams(vmem_limit_bytes=4 << 20)
    taps = in_vmem(
        pl.pallas_call(
            taps_kernel,
            out_shape=pltpu.VMEM((4 * MODES * CH, LANES), jnp.float32),
            in_specs=[vmem] * 2,
            out_specs=vmem,
            compiler_params=small,
            name="taps",
        )(in_hbm(row_taps), in_hbm(col_taps))
    )
    built = [
        pl.pallas_call(
            kernel,
            out_shape=pltpu.VMEM(shape, jnp.bfloat16),
            in_specs=[vmem, pl.BlockSpec(memory_space=pl.ANY)],
            out_specs=vmem,
            compiler_params=small,
            name=name,
        )(taps, stage)
        for stage, (kernel, shape, name) in zip(
            stages,
            (
                (column_bands_kernel, (2 * MODES, CH * EXT // 2, LANES), "column_bands"),
                (column_adjoint_kernel, (4 * MODES, 2 * EXT, LANES), "column_adjoint"),
            ),
        )
    ]
    return [taps, *built]


def reversed_bits(value, bits):
    return sum(((value >> b) & 1) << (bits - 1 - b) for b in range(bits))


def main_kernel(
    devices,
    gathered_ref,
    taps,
    cf_ref,
    ca_ref,
    weight_hbm,
    target_hbm,
    resid_hbm,
    grads_ref,
    *scratch,
):
    canvases, grads, sums = scratch[0:3], scratch[3:6], scratch[6:9]
    window, lhs, fields, slope, gw, gys, table, ids, sem = scratch[9:18]
    weight_ref, target_ref, resid_ref, r_ref, rt_ref, load_sems = scratch[18:]
    loads = [
        pltpu.make_async_copy(source, target, load_sems.at[n])
        for n, (source, target) in enumerate(
            (
                (weight_hbm, weight_ref),
                (target_hbm, target_ref),
                (resid_ref, resid_hbm),
            )
        )
    ]
    slabs = gathered_ref.shape[0] // devices
    count = slabs - 1
    places = LANES
    rows = BLK
    me = lax.axis_index("tx")
    bits = devices.bit_length() - 1
    bases = (HALF, HALF - rows, HALF + rows)
    for n, (other, missing) in enumerate(
        ((me, 0), (jnp.maximum(me - 1, 0), 0), (jnp.minimum(me + 1, devices - 1), BLK - MS))
    ):
        slab = gathered_ref[reversed_bits(other ^ me, bits) * slabs + count].astype(jnp.float32).astype(jnp.int32)
        owner, local, row, col = reversed_bits(slab[0:1] ^ me, bits), slab[1:2], slab[2:3], slab[3:4]
        if n:
            row = jnp.where(other == me, missing, row)
        first_lane = (row + bases[n]) & 127
        lines = jnp.concatenate(
            [
                owner * slabs + local,
                owner * count + local,
                col + HALF,
                first_lane,
                col,
                (LANES - first_lane) & 127,
                row,
                row,
            ],
            axis=0,
        )
        for j in range(places // STEP):
            table[j, 8 * n : 8 * n + 8, :] = (
                pltpu.roll(lines, LANES - STEP * j, 1) if j else lines
            )[:, :STEP]
    to_scalar = pltpu.make_async_copy(table, ids, sem)
    to_scalar.start()
    for load in loads[:2]:
        load.start()
    for canvas in canvases:
        canvas[...] = jnp.zeros_like(canvas)
    for acc in sums:
        acc[...] = jnp.zeros_like(acc)
    lanes8 = lane_iota((8, LANES))
    to_scalar.wait()

    def place(j, u):
        for n, canvas in enumerate(canvases):
            at, shift = ids[j, 8 * n + 2, u], ids[j, 8 * n + 3, u]
            moved = pltpu.roll(gathered_ref[ids[j, 8 * n, u]].astype(jnp.float32), shift, 1)
            nth = ((lanes8 - shift) & 127) >> 5
            spots = [pl.ds(at + k * CROWS + k, 8, stride=4) for k in range(4)]
            old = [canvas[spot, :] for spot in spots]
            for k, spot in enumerate(spots):
                canvas[spot, :] = old[k] + jnp.where(nth == k, moved, 0.0)

    @pl.loop(0, places // STEP)
    def _(j):
        for u in range(STEP):
            place(j, u)


    def of_above(k, lanes):
        return ((lanes - MS * k) & 127) < HALF

    def of_below(k, lanes):
        return ((lanes - MS * k) & 127) >= HALF + BLK

    used = slice(24, 288)
    wide = lane_iota((used.stop - used.start, LANES))
    columns = 0.0
    for k in range(4):
        lines = slice(k * CROWS + used.start, k * CROWS + used.stop)
        own, above, below = [canvas[lines, :] for canvas in canvases]
        joined = (
            own
            + jnp.where(of_above(k, wide), above, 0.0)
            + jnp.where(of_below(k, wide), below, 0.0)
        )
        columns = columns + (pltpu.roll(joined, LANES - MS * k, 1) if k else joined)
    columns = jnp.concatenate(
        [
            jnp.zeros((used.start, LANES), jnp.float32),
            columns,
            jnp.zeros((CROWS - used.stop, LANES), jnp.float32),
        ],
        axis=0,
    )
    for b in range(NBLK):
        window[:, b * LANES : (b + 1) * LANES] = jnp.transpose(
            columns[b * BLK : b * BLK + LANES]
        ).astype(jnp.bfloat16)
    low = lane_iota((EXT, LANES)) < BLK

    lanes16 = lane_iota((16, LANES))
    before = lanes16 < HALF
    until = lanes16 < HALF + BLK
    def row_bands(k):
        for c in range(CH):
            at = k * CH + c
            r_ref[at * BLK : (at + 1) * BLK, :] = half_band(skew(taps[at : at + 1, :], 0))

    low64 = low_lanes()

    def row_adjoint_bands(k):
        for n in (2 * k, 2 * k + 1):
            tap = 2 * MODES * CH + 4 * n
            for par in range(2):
                one, two = tap + par, tap + 2 + par
                a, a_far, b, b_far = pair(taps[one : one + 1, :], taps[two : two + 1, :])
                at = par * EXT
                rt_ref[n, at : at + BLK, :] = half_band(jnp.where(low64, a, b_far))
                rt_ref[n, at + BLK : at + EXT, :] = half_band(jnp.where(low64, a_far, b))

    loads[0].wait()
    row_bands(0)
    intensity = jnp.zeros((NBLK * rows, LANES), jnp.float32)
    for k in range(MODES):
        if k + 1 < MODES:
            row_bands(k + 1)
        row_adjoint_bands(k)
        field_y = jnp.dot(
            r_ref[k * CH * rows : (k + 1) * CH * rows, :],
            window[...],
            preferred_element_type=jnp.float32,
        ).astype(jnp.bfloat16)
        for c in range(CH):
            for b in range(NBLK):
                lhs[k % 2, b * rows : (b + 1) * rows, c * LANES : (c + 1) * LANES] = field_y[
                    c * rows : (c + 1) * rows, b * LANES : (b + 1) * LANES
                ]
        e = jnp.dot(
            lhs[k % 2],
            jnp.concatenate([cf_ref[2 * k], cf_ref[2 * k + 1]], axis=0),
            preferred_element_type=jnp.float32,
        )
        fields[k] = e
        intensity = intensity + weight_ref[k] * (e * e)
    loads[1].wait()
    low_rows = lane_iota((rows, LANES)) < BLK

    def halves(x, first):
        turned = pltpu.roll(x, BLK, 1)
        return (jnp.where(low_rows, x, turned), jnp.where(low_rows, turned, x))[first]

    for h in range(2):
        one = intensity[2 * h * rows : (2 * h + 1) * rows]
        two = intensity[(2 * h + 1) * rows : (2 * h + 2) * rows]
        inten = jnp.where(
            low_rows, one + pltpu.roll(one, BLK, 1), two + pltpu.roll(two, BLK, 1)
        )
        at = slice(h * LANES, (h + 1) * LANES)
        resist = jax.nn.sigmoid(steepness * (inten - threshold))
        resid = resist - target_ref[:, at].astype(jnp.float32)
        resid_ref[:, at] = resid
        change = 2.0 * (resid * steepness * resist * (1.0 - resist))
        for n in range(2):
            slope[(2 * h + n) * rows : (2 * h + n + 1) * rows, :] = halves(change, n)

    loads[2].start()
    nothing = jnp.zeros((16, LANES), jnp.float32)
    for k in range(MODES):
        weight = weight_ref[k]
        for i in range(0, rows, 16):
            r31, r95 = [nothing], [nothing]
            for b in range(NBLK):
                at = slice(b * rows + i, b * rows + i + 16)
                g = weight * slope[at, :] * fields[k, at, :]
                r31.append(pltpu.roll(g, HALF, 1))
                r95.append(pltpu.roll(g, HALF + BLK, 1))
            r31.append(nothing)
            r95.append(nothing)
            for b in range(NBLK):
                at = slice(b * rows + i, b * rows + i + 16)
                re = jnp.where(before, r95[b], jnp.where(until, r31[b + 1], r95[b + 2]))
                im = jnp.where(before, r31[b], jnp.where(until, r95[b + 1], r31[b + 2]))
                gw[k % 2, at, :LANES] = re.astype(jnp.bfloat16)
                gw[k % 2, at, LANES:] = im.astype(jnp.bfloat16)
        for t in range(TERMS):
            gy = jnp.dot(
                gw[k % 2], ca_ref[k * TERMS + t], preferred_element_type=jnp.float32
            ).astype(jnp.bfloat16)
            at = (k * TERMS + t) * rows
            for b in range(NBLK):
                gys[at : at + rows, b * LANES : (b + 1) * LANES] = gy[b * rows : (b + 1) * rows]

    total = jnp.zeros((2 * EXT, NBLK * LANES), jnp.float32)
    for k in range(MODES):
        total = total + jnp.dot(
            jnp.concatenate([rt_ref[2 * k], rt_ref[2 * k + 1]], axis=1),
            gys[2 * k * LANES : 2 * (k + 1) * LANES, :],
            preferred_element_type=jnp.float32,
        )
    whole = []
    for h in range(2):
        v0 = total[:EXT, 2 * h * LANES : (2 * h + 1) * LANES]
        v1 = total[:EXT, (2 * h + 1) * LANES : (2 * h + 2) * LANES]
        u0 = total[EXT:, 2 * h * LANES : (2 * h + 1) * LANES]
        u1 = total[EXT:, (2 * h + 1) * LANES : (2 * h + 2) * LANES]
        whole.append(
            jnp.where(low, v0 + pltpu.roll(u0, BLK, 1), pltpu.roll(v1, BLK, 1) + u1)
        )
    columns = jnp.concatenate([jnp.transpose(side) for side in whole], axis=0)
    wide = lane_iota((W, LANES))
    for k in range(4):
        turned = pltpu.roll(columns, MS * k, 1) if k else columns
        lines = slice(k * W, (k + 1) * W)
        grads[0][lines, :] = turned
        grads[1][lines, :] = jnp.where(of_above(k, wide), turned, 0.0)
        grads[2][lines, :] = jnp.where(of_below(k, wide), turned, 0.0)

    def gather(j, u):
        for n, acc in enumerate(sums):
            m, shift, at, back = [ids[j, 8 * n + line, u] for line in (1, 3, 4, 5)]
            nth = (lanes8 - shift) & 127
            patch = None
            for k in range(4):
                rows_k = grads[n][pl.ds(at + k * W + k, 8, stride=4), :]
                patch = jnp.where(nth >= MS * k, rows_k, patch) if k else rows_k
            acc[m] += pltpu.roll(patch, back, 1)

    @pl.loop(0, places // STEP)
    def _(j):
        for u in range(STEP):
            gather(j, u)

    grads_ref[...] = (sums[0][...] + sums[1][...] + sums[2][...]).reshape(grads_ref.shape)
    loads[2].wait()


def main_step(weights, gathered, target, bands):
    devices, slabs = gathered.shape[:2]
    count = slabs - 1
    vmem = pl.BlockSpec(memory_space=pltpu.VMEM)
    return pl.pallas_call(
        functools.partial(main_kernel, devices),
        out_shape=(
            pltpu.HBM(target.shape, jnp.float32),
            pltpu.VMEM((devices, count, 8, LANES), jnp.float32),
        ),
        in_specs=[vmem] * 4 + [pl.BlockSpec(memory_space=pl.ANY)] * 2,
        out_specs=[pl.BlockSpec(memory_space=pl.ANY), vmem],
        scratch_shapes=[
            *[pltpu.VMEM((4 * CROWS, LANES), jnp.float32)] * 3,
            *[pltpu.VMEM((4 * W, LANES), jnp.float32)] * 3,
            *[pltpu.VMEM((devices * count, 8, LANES), jnp.float32)] * 3,
            pltpu.VMEM((EXT, NBLK * LANES), jnp.bfloat16),
            pltpu.VMEM((2, NBLK * BLK, CH * LANES), jnp.bfloat16),
            pltpu.VMEM((MODES, NBLK * BLK, LANES), jnp.float32),
            pltpu.VMEM((NBLK * BLK, LANES), jnp.float32),
            pltpu.VMEM((2, NBLK * BLK, 2 * LANES), jnp.bfloat16),
            pltpu.VMEM((MODES * TERMS * BLK, NBLK * LANES), jnp.bfloat16),
            pltpu.VMEM((LANES // STEP, 24, STEP), jnp.int32),
            pltpu.SMEM((LANES // STEP, 24, STEP), jnp.int32),
            pltpu.SemaphoreType.DMA,
            pltpu.SMEM(weights.shape, jnp.float32),
            pltpu.VMEM(target.shape, jnp.bfloat16),
            pltpu.VMEM(target.shape, jnp.float32),
            pltpu.VMEM((MODES * CH * BLK, LANES), jnp.bfloat16),
            pltpu.VMEM((2 * MODES, 2 * EXT, LANES), jnp.bfloat16),
            pltpu.SemaphoreType.DMA((3,)),
        ],
        compiler_params=pltpu.CompilerParams(vmem_limit_bytes=28 << 20),
        name="imaging",
    )(
        in_vmem(gathered.reshape(devices * slabs, 8, LANES)),
        *[in_vmem(x) for x in bands],
        in_hbm(weights),
        in_hbm(target),
    )


def flip_pixels(slabs, cells):
    lanes = lane_iota((8, LANES))

    def chosen(parts):
        out = parts[0]
        for n, part in enumerate(parts):
            if n:
                out = jnp.where(lanes >= MS * n, part, out)
        return out

    def turned(x, blocks):
        return pltpu.roll(x, (MS * blocks) % LANES, 1) if blocks else x

    cells[MS:, :] = jnp.zeros((LANES - MS, LANES), jnp.float32)
    for k in range(4):
        cells[pl.ds(k, 8, stride=4), :] = chosen([turned(x, m - k) for m, x in enumerate(slabs)])
    cells[...] = jnp.transpose(cells[...])
    return [
        chosen([turned(cells[pl.ds(MS * m + k, 8, stride=4), :], k) for k in range(4)])
        for m in range(len(slabs))
    ]


def pack_kernel(masters_ref, owner_ref, local_ref, row_ref, col_ref, out_ref, spread, cells):
    count = masters_ref.shape[0]
    for s in range(8):
        spread[pl.ds(s, count, stride=8), :] = masters_ref[:, s * LANES : (s + 1) * LANES]
    flipped = flip_pixels([spread[8 * m : 8 * m + 8, :] for m in range(count)], cells)
    for m, slab in enumerate(flipped):
        spread[8 * m : 8 * m + 8, :] = slab
    spread[8 * count :, :] = jnp.zeros((8, LANES), jnp.float32)
    for n, ref in enumerate((owner_ref, local_ref, row_ref, col_ref)):
        spread[8 * count + n : 8 * count + n + 1, :] = ref[...].astype(jnp.float32)
    out_ref[...] = spread[...].reshape(out_ref.shape).astype(jnp.bfloat16)


def pack(masters, *places):
    count = masters.shape[0]
    vmem = pl.BlockSpec(memory_space=pltpu.VMEM)
    return pl.pallas_call(
        pack_kernel,
        out_shape=pltpu.VMEM((1, count + 1, 8, LANES), jnp.bfloat16),
        in_specs=[vmem] * 5,
        out_specs=vmem,
        scratch_shapes=[
            pltpu.VMEM((8 * count + 8, LANES), jnp.float32),
            pltpu.VMEM((LANES, LANES), jnp.float32),
        ],
        compiler_params=pltpu.CompilerParams(vmem_limit_bytes=4 << 20),
        name="pack",
    )(in_hbm(masters), *[in_hbm(p.reshape(1, LANES)) for p in places])


def update_kernel(
    kept_ref, sent_ref, velocity_ref, masters_ref, velocity_out, masters_out, sums, cells
):
    count = velocity_ref.shape[0]
    flipped = flip_pixels([kept_ref[0, m] + sent_ref[0, m] for m in range(count)], cells)
    for m, slab in enumerate(flipped):
        sums[8 * m : 8 * m + 8, :] = slab
    for s in range(8):
        at = slice(s * LANES, (s + 1) * LANES)
        gradient = sums[pl.ds(s, count, stride=8), :]
        velocity = momentum * velocity_ref[:, at] + gradient
        velocity_out[:, at] = velocity
        masters_out[:, at] = masters_ref[:, at] - step_size * velocity


def update(kept, sent, velocity, masters):
    vmem = pl.BlockSpec(memory_space=pltpu.VMEM)
    return pl.pallas_call(
        update_kernel,
        out_shape=(jax.ShapeDtypeStruct(velocity.shape, jnp.float32),) * 2,
        in_specs=[vmem] * 4,
        out_specs=[vmem] * 2,
        scratch_shapes=[
            pltpu.VMEM((8 * velocity.shape[0], LANES), jnp.float32),
            pltpu.VMEM((LANES, LANES), jnp.float32),
        ],
        compiler_params=pltpu.CompilerParams(vmem_limit_bytes=4 << 20),
        name="update",
    )(kept, sent, velocity, masters)


def swap(value, bit, devices):
    return lax.ppermute(value, "tx", [(i, i ^ bit) for i in range(devices)])


def on_device(
    masters,
    velocity,
    place_owner,
    place_local,
    place_row,
    place_col,
    row_taps,
    col_taps,
    mode_weights,
    target,
):
    devices = lax.axis_size("tx")
    bits = devices.bit_length() - 1
    held = pack(masters, place_owner, place_local, place_row, place_col)
    stages = []
    for b in reversed(range(bits)):
        held = jnp.concatenate([held, swap(held, 1 << b, devices)], axis=0)
        stages.append(held)
    bands = build_bands(row_taps, col_taps, stages[-4:-2])
    resid, grads = main_step(mode_weights, held, target, bands)
    for b in range(bits):
        half = grads.shape[0] // 2
        sent = swap(grads[half:], 1 << b, devices)
        if b < bits - 1:
            grads = grads[:half] + sent
    velocity_new, masters_new = update(grads, sent, velocity, masters)
    return resid, velocity_new, masters_new


def solution(mesh):
    return jax.shard_map(
        on_device,
        mesh=mesh,
        in_specs=(
            P(("groups", "tx"), None),
            P(("groups", "tx"), None),
            P(("groups", "tx"), None),
            P(("groups", "tx")),
            P(("groups", "tx")),
            P(("groups", "tx")),
            P(),
            P(),
            P(),
            P(("groups", "tx"), None),
        ),
        out_specs=(P(("groups", "tx"), None), P(("groups", "tx"), None), P(("groups", "tx"), None)),
        check_vma=False,
    )
```

```python
import functools
import jax
import jax.numpy as jnp
from jax import lax
from jax.experimental import pallas as pl
from jax.experimental.pallas import tpu as pltpu
from jax.sharding import PartitionSpec as P

W = 256
MS = 32
TAPS = 63
HALF = 31
TERMS = 4
MODES = 12
CH = 2 * TERMS
LANES = 128
BLK = 64
EXT = 128
STEP = 32
NBLK = W // BLK
CROWS = 320

steepness = 0.5
threshold = 8.0
momentum = 0.9
step_size = 0.05


def in_vmem(x):
    return pltpu.with_memory_space_constraint(x, pltpu.VMEM)


def in_hbm(x):
    return pltpu.with_memory_space_constraint(x, pltpu.HBM)


def lane_iota(shape):
    return lax.broadcasted_iota(jnp.int32, shape, len(shape) - 1)


def skew(row, shift):
    return pltpu.roll(
        jnp.broadcast_to(row, (BLK, LANES)), shift, 1, stride=1, stride_axis=0
    )


def pair(first, second):
    return (skew(first, 0), skew(first, BLK), skew(second, 0), skew(second, BLK))


def half_band(x):
    return x.astype(jnp.bfloat16)


def low_lanes():
    return lane_iota((BLK, LANES)) < BLK


def taps_kernel(row_ref, col_ref, taps):
    count = MODES * CH
    taps[...] = jnp.zeros_like(taps)
    for k in range(MODES):
        for t in range(TERMS):
            at = k * CH + 2 * t
            taps[at : at + 2, :TAPS] = row_ref[k, t].astype(jnp.float32)
            taps[count + at : count + at + 2, :TAPS] = col_ref[k, t].astype(jnp.float32)
    source = lax.broadcasted_iota(jnp.int32, (LANES, LANES), 0)
    mirror = (source + lane_iota((LANES, LANES))) % LANES == 0
    taps[2 * count :, :] = jnp.dot(
        taps[: 2 * count, :].astype(jnp.bfloat16),
        mirror.astype(jnp.bfloat16),
        preferred_element_type=jnp.float32,
    )
    taps[count : 2 * count, :] = pltpu.roll(taps[count : 2 * count, :], LANES - (TAPS - 1), 1)


def column_bands_kernel(taps, _, cf_ref):
    count = MODES * CH
    low = low_lanes()

    def step(n, carry):
        first = 3 * count + 4 * n
        for t in range(2):
            at = t * 2 * EXT
            a, a_far, b, b_far = pair(
                taps[pl.ds(first + 2 * t, 1), :], taps[pl.ds(first + 2 * t + 1, 1), :]
            )
            cf_ref[n, at : at + BLK, :] = half_band(jnp.where(low, a, b_far))
            cf_ref[n, at + BLK : at + EXT, :] = half_band(jnp.where(low, a_far, b))
            cf_ref[n, at + EXT : at + EXT + BLK, :] = half_band(jnp.where(low, -b, a_far))
            cf_ref[n, at + EXT + BLK : at + 2 * EXT, :] = half_band(jnp.where(low, -b_far, a))
        return carry

    lax.fori_loop(0, 2 * MODES, step, 0, unroll=3)


def column_adjoint_kernel(taps, _, ca_ref):
    count = MODES * CH
    low = low_lanes()

    def step(n, carry):
        first = count + 4 * n
        for t in range(2):
            a, a_far, b, b_far = pair(
                taps[pl.ds(first + 2 * t, 1), :], taps[pl.ds(first + 2 * t + 1, 1), :]
            )
            ca_ref[n * 2 + t, :BLK, :] = half_band(jnp.where(low, a, -b_far))
            ca_ref[n * 2 + t, BLK:EXT, :] = half_band(jnp.where(low, a_far, -b))
            ca_ref[n * 2 + t, EXT : EXT + BLK, :] = half_band(jnp.where(low, b, a_far))
            ca_ref[n * 2 + t, EXT + BLK :, :] = half_band(jnp.where(low, b_far, a))
        return carry

    lax.fori_loop(0, 2 * MODES, step, 0, unroll=3)


def build_bands(row_taps, col_taps, stages):
    vmem = pl.BlockSpec(memory_space=pltpu.VMEM)
    small = pltpu.CompilerParams(vmem_limit_bytes=4 << 20)
    taps = in_vmem(
        pl.pallas_call(
            taps_kernel,
            out_shape=pltpu.VMEM((4 * MODES * CH, LANES), jnp.float32),
            in_specs=[vmem] * 2,
            out_specs=vmem,
            compiler_params=small,
            name="taps",
        )(in_hbm(row_taps), in_hbm(col_taps))
    )
    built = [
        pl.pallas_call(
            kernel,
            out_shape=pltpu.VMEM(shape, jnp.bfloat16),
            in_specs=[vmem, pl.BlockSpec(memory_space=pl.ANY)],
            out_specs=vmem,
            compiler_params=small,
            name=name,
        )(taps, stage)
        for stage, (kernel, shape, name) in zip(
            stages,
            (
                (column_bands_kernel, (2 * MODES, CH * EXT // 2, LANES), "column_bands"),
                (column_adjoint_kernel, (4 * MODES, 2 * EXT, LANES), "column_adjoint"),
            ),
        )
    ]
    return [taps, *built]


def reversed_bits(value, bits):
    return sum(((value >> b) & 1) << (bits - 1 - b) for b in range(bits))


def main_kernel(
    devices,
    gathered_ref,
    taps,
    cf_ref,
    ca_ref,
    weight_hbm,
    target_hbm,
    resid_hbm,
    grads_ref,
    *scratch,
):
    canvases, grads, sums = scratch[0:3], scratch[3:6], scratch[6:9]
    window, lhs, fields, slope, gw, gys, table, ids, sem = scratch[9:18]
    weight_ref, target_ref, resid_ref, r_ref, rt_ref, load_sems = scratch[18:]
    loads = [
        pltpu.make_async_copy(source, target, load_sems.at[n])
        for n, (source, target) in enumerate(
            (
                (weight_hbm, weight_ref),
                (target_hbm, target_ref),
                (resid_ref, resid_hbm),
            )
        )
    ]
    slabs = gathered_ref.shape[0] // devices
    count = slabs - 1
    places = LANES
    rows = BLK
    me = lax.axis_index("tx")
    bits = devices.bit_length() - 1
    bases = (HALF, HALF - rows, HALF + rows)
    for n, (other, missing) in enumerate(
        ((me, 0), (jnp.maximum(me - 1, 0), 0), (jnp.minimum(me + 1, devices - 1), BLK - MS))
    ):
        slab = gathered_ref[reversed_bits(other ^ me, bits) * slabs + count].astype(jnp.float32).astype(jnp.int32)
        owner, local, row, col = reversed_bits(slab[0:1] ^ me, bits), slab[1:2], slab[2:3], slab[3:4]
        if n:
            row = jnp.where(other == me, missing, row)
        first_lane = (row + bases[n]) & 127
        lines = jnp.concatenate(
            [
                owner * slabs + local,
                owner * count + local,
                col + HALF,
                first_lane,
                col,
                (LANES - first_lane) & 127,
                row,
                row,
            ],
            axis=0,
        )
        for j in range(places // STEP):
            table[j, 8 * n : 8 * n + 8, :] = (
                pltpu.roll(lines, LANES - STEP * j, 1) if j else lines
            )[:, :STEP]
    to_scalar = pltpu.make_async_copy(table, ids, sem)
    to_scalar.start()
    for load in loads[:2]:
        load.start()
    for canvas in canvases:
        canvas[...] = jnp.zeros_like(canvas)
    for acc in sums:
        acc[...] = jnp.zeros_like(acc)
    lanes8 = lane_iota((8, LANES))
    to_scalar.wait()

    def place(j, u):
        for n, canvas in enumerate(canvases):
            at, shift = ids[j, 8 * n + 2, u], ids[j, 8 * n + 3, u]
            moved = pltpu.roll(gathered_ref[ids[j, 8 * n, u]].astype(jnp.float32), shift, 1)
            nth = ((lanes8 - shift) & 127) >> 5
            spots = [pl.ds(at + k * CROWS + k, 8, stride=4) for k in range(4)]
            old = [canvas[spot, :] for spot in spots]
            for k, spot in enumerate(spots):
                canvas[spot, :] = old[k] + jnp.where(nth == k, moved, 0.0)

    @pl.loop(0, places // STEP)
    def _(j):
        for u in range(STEP):
            place(j, u)


    def of_above(k, lanes):
        return ((lanes - MS * k) & 127) < HALF

    def of_below(k, lanes):
        return ((lanes - MS * k) & 127) >= HALF + BLK

    used = slice(24, 288)
    wide = lane_iota((used.stop - used.start, LANES))
    columns = 0.0
    for k in range(4):
        lines = slice(k * CROWS + used.start, k * CROWS + used.stop)
        own, above, below = [canvas[lines, :] for canvas in canvases]
        joined = (
            own
            + jnp.where(of_above(k, wide), above, 0.0)
            + jnp.where(of_below(k, wide), below, 0.0)
        )
        columns = columns + (pltpu.roll(joined, LANES - MS * k, 1) if k else joined)
    columns = jnp.concatenate(
        [
            jnp.zeros((used.start, LANES), jnp.float32),
            columns,
            jnp.zeros((CROWS - used.stop, LANES), jnp.float32),
        ],
        axis=0,
    )
    for b in range(NBLK):
        window[:, b * LANES : (b + 1) * LANES] = jnp.transpose(
            columns[b * BLK : b * BLK + LANES]
        ).astype(jnp.bfloat16)
    low = lane_iota((EXT, LANES)) < BLK

    lanes16 = lane_iota((16, LANES))
    before = lanes16 < HALF
    until = lanes16 < HALF + BLK
    def row_bands(k):
        for c in range(CH):
            at = k * CH + c
            r_ref[at * BLK : (at + 1) * BLK, :] = half_band(skew(taps[at : at + 1, :], 0))

    low64 = low_lanes()

    def row_adjoint_bands(k):
        for n in (2 * k, 2 * k + 1):
            tap = 2 * MODES * CH + 4 * n
            for par in range(2):
                one, two = tap + par, tap + 2 + par
                a, a_far, b, b_far = pair(taps[one : one + 1, :], taps[two : two + 1, :])
                at = par * EXT
                rt_ref[n, at : at + BLK, :] = half_band(jnp.where(low64, a, b_far))
                rt_ref[n, at + BLK : at + EXT, :] = half_band(jnp.where(low64, a_far, b))

    loads[0].wait()
    row_bands(0)
    intensity = jnp.zeros((NBLK * rows, LANES), jnp.float32)
    for k in range(MODES):
        if k + 1 < MODES:
            row_bands(k + 1)
        row_adjoint_bands(k)
        field_y = jnp.dot(
            r_ref[k * CH * rows : (k + 1) * CH * rows, :],
            window[...],
            preferred_element_type=jnp.float32,
        ).astype(jnp.bfloat16)
        for c in range(CH):
            for b in range(NBLK):
                lhs[k % 2, b * rows : (b + 1) * rows, c * LANES : (c + 1) * LANES] = field_y[
                    c * rows : (c + 1) * rows, b * LANES : (b + 1) * LANES
                ]
        e = jnp.dot(
            lhs[k % 2],
            jnp.concatenate([cf_ref[2 * k], cf_ref[2 * k + 1]], axis=0),
            preferred_element_type=jnp.float32,
        )
        fields[k] = e
        intensity = intensity + weight_ref[k] * (e * e)
    loads[1].wait()
    low_rows = lane_iota((rows, LANES)) < BLK

    def halves(x, first):
        turned = pltpu.roll(x, BLK, 1)
        return (jnp.where(low_rows, x, turned), jnp.where(low_rows, turned, x))[first]

    for h in range(2):
        one = intensity[2 * h * rows : (2 * h + 1) * rows]
        two = intensity[(2 * h + 1) * rows : (2 * h + 2) * rows]
        inten = jnp.where(
            low_rows, one + pltpu.roll(one, BLK, 1), two + pltpu.roll(two, BLK, 1)
        )
        at = slice(h * LANES, (h + 1) * LANES)
        resist = jax.nn.sigmoid(steepness * (inten - threshold))
        resid = resist - target_ref[:, at].astype(jnp.float32)
        resid_ref[:, at] = resid
        change = 2.0 * (resid * steepness * resist * (1.0 - resist))
        for n in range(2):
            slope[(2 * h + n) * rows : (2 * h + n + 1) * rows, :] = halves(change, n)

    loads[2].start()
    nothing = jnp.zeros((16, LANES), jnp.float32)
    for k in range(MODES):
        weight = weight_ref[k]
        for i in range(0, rows, 16):
            r31, r95 = [nothing], [nothing]
            for b in range(NBLK):
                at = slice(b * rows + i, b * rows + i + 16)
                g = weight * slope[at, :] * fields[k, at, :]
                r31.append(pltpu.roll(g, HALF, 1))
                r95.append(pltpu.roll(g, HALF + BLK, 1))
            r31.append(nothing)
            r95.append(nothing)
            for b in range(NBLK):
                at = slice(b * rows + i, b * rows + i + 16)
                re = jnp.where(before, r95[b], jnp.where(until, r31[b + 1], r95[b + 2]))
                im = jnp.where(before, r31[b], jnp.where(until, r95[b + 1], r31[b + 2]))
                gw[k % 2, at, :LANES] = re.astype(jnp.bfloat16)
                gw[k % 2, at, LANES:] = im.astype(jnp.bfloat16)
        for t in range(TERMS):
            gy = jnp.dot(
                gw[k % 2], ca_ref[k * TERMS + t], preferred_element_type=jnp.float32
            ).astype(jnp.bfloat16)
            at = (k * TERMS + t) * rows
            for b in range(NBLK):
                gys[at : at + rows, b * LANES : (b + 1) * LANES] = gy[b * rows : (b + 1) * rows]

    total = jnp.zeros((2 * EXT, NBLK * LANES), jnp.float32)
    for k in range(MODES):
        total = total + jnp.dot(
            jnp.concatenate([rt_ref[2 * k], rt_ref[2 * k + 1]], axis=1),
            gys[2 * k * LANES : 2 * (k + 1) * LANES, :],
            preferred_element_type=jnp.float32,
        )
    whole = []
    for h in range(2):
        v0 = total[:EXT, 2 * h * LANES : (2 * h + 1) * LANES]
        v1 = total[:EXT, (2 * h + 1) * LANES : (2 * h + 2) * LANES]
        u0 = total[EXT:, 2 * h * LANES : (2 * h + 1) * LANES]
        u1 = total[EXT:, (2 * h + 1) * LANES : (2 * h + 2) * LANES]
        whole.append(
            jnp.where(low, v0 + pltpu.roll(u0, BLK, 1), pltpu.roll(v1, BLK, 1) + u1)
        )
    columns = jnp.concatenate([jnp.transpose(side) for side in whole], axis=0)
    wide = lane_iota((W, LANES))
    for k in range(4):
        turned = pltpu.roll(columns, MS * k, 1) if k else columns
        lines = slice(k * W, (k + 1) * W)
        grads[0][lines, :] = turned
        grads[1][lines, :] = jnp.where(of_above(k, wide), turned, 0.0)
        grads[2][lines, :] = jnp.where(of_below(k, wide), turned, 0.0)

    def gather(j, u):
        for n, acc in enumerate(sums):
            m, shift, at, back = [ids[j, 8 * n + line, u] for line in (1, 3, 4, 5)]
            nth = (lanes8 - shift) & 127
            patch = None
            for k in range(4):
                rows_k = grads[n][pl.ds(at + k * W + k, 8, stride=4), :]
                patch = jnp.where(nth >= MS * k, rows_k, patch) if k else rows_k
            acc[m] += pltpu.roll(patch, back, 1)

    @pl.loop(0, places // STEP)
    def _(j):
        for u in range(STEP):
            gather(j, u)

    grads_ref[...] = (sums[0][...] + sums[1][...] + sums[2][...]).reshape(grads_ref.shape)
    loads[2].wait()


def main_step(weights, gathered, target, bands):
    devices, slabs = gathered.shape[:2]
    count = slabs - 1
    vmem = pl.BlockSpec(memory_space=pltpu.VMEM)
    return pl.pallas_call(
        functools.partial(main_kernel, devices),
        out_shape=(
            pltpu.HBM(target.shape, jnp.float32),
            pltpu.VMEM((devices, count, 8, LANES), jnp.float32),
        ),
        in_specs=[vmem] * 4 + [pl.BlockSpec(memory_space=pl.ANY)] * 2,
        out_specs=[pl.BlockSpec(memory_space=pl.ANY), vmem],
        scratch_shapes=[
            *[pltpu.VMEM((4 * CROWS, LANES), jnp.float32)] * 3,
            *[pltpu.VMEM((4 * W + 8, LANES), jnp.float32)] * 3,
            *[pltpu.VMEM((devices * count, 8, LANES), jnp.float32)] * 3,
            pltpu.VMEM((EXT, NBLK * LANES), jnp.bfloat16),
            pltpu.VMEM((2, NBLK * BLK, CH * LANES), jnp.bfloat16),
            pltpu.VMEM((MODES, NBLK * BLK, LANES), jnp.float32),
            pltpu.VMEM((NBLK * BLK, LANES), jnp.float32),
            pltpu.VMEM((2, NBLK * BLK, 2 * LANES), jnp.bfloat16),
            pltpu.VMEM((MODES * TERMS * BLK, NBLK * LANES), jnp.bfloat16),
            pltpu.VMEM((LANES // STEP, 24, STEP), jnp.int32),
            pltpu.SMEM((LANES // STEP, 24, STEP), jnp.int32),
            pltpu.SemaphoreType.DMA,
            pltpu.SMEM(weights.shape, jnp.float32),
            pltpu.VMEM(target.shape, jnp.bfloat16),
            pltpu.VMEM(target.shape, jnp.float32),
            pltpu.VMEM((MODES * CH * BLK, LANES), jnp.bfloat16),
            pltpu.VMEM((2 * MODES, 2 * EXT, LANES), jnp.bfloat16),
            pltpu.SemaphoreType.DMA((3,)),
        ],
        compiler_params=pltpu.CompilerParams(vmem_limit_bytes=28 << 20),
        name="imaging",
    )(
        in_vmem(gathered.reshape(devices * slabs, 8, LANES)),
        *[in_vmem(x) for x in bands],
        in_hbm(weights),
        in_hbm(target),
    )


def flip_pixels(slabs, cells):
    lanes = lane_iota((8, LANES))

    def chosen(parts):
        out = parts[0]
        for n, part in enumerate(parts):
            if n:
                out = jnp.where(lanes >= MS * n, part, out)
        return out

    def turned(x, blocks):
        return pltpu.roll(x, (MS * blocks) % LANES, 1) if blocks else x

    cells[MS:, :] = jnp.zeros((LANES + 8 - MS, LANES), jnp.float32)
    for k in range(4):
        cells[pl.ds(k, 8, stride=4), :] = chosen([turned(x, m - k) for m, x in enumerate(slabs)])
    cells[:LANES, :] = jnp.transpose(cells[:LANES, :])
    return [
        chosen([turned(cells[pl.ds(MS * m + k, 8, stride=4), :], k) for k in range(4)])
        for m in range(len(slabs))
    ]


def pack_kernel(masters_ref, owner_ref, local_ref, row_ref, col_ref, out_ref, spread, cells):
    count = masters_ref.shape[0]
    for s in range(8):
        spread[pl.ds(s, count, stride=8), :] = masters_ref[:, s * LANES : (s + 1) * LANES]
    flipped = flip_pixels([spread[8 * m : 8 * m + 8, :] for m in range(count)], cells)
    for m, slab in enumerate(flipped):
        spread[8 * m : 8 * m + 8, :] = slab
    spread[8 * count :, :] = jnp.zeros((8, LANES), jnp.float32)
    for n, ref in enumerate((owner_ref, local_ref, row_ref, col_ref)):
        spread[8 * count + n : 8 * count + n + 1, :] = ref[...].astype(jnp.float32)
    out_ref[...] = spread[...].reshape(out_ref.shape).astype(jnp.bfloat16)


def pack(masters, *places):
    count = masters.shape[0]
    vmem = pl.BlockSpec(memory_space=pltpu.VMEM)
    return pl.pallas_call(
        pack_kernel,
        out_shape=pltpu.VMEM((1, count + 1, 8, LANES), jnp.bfloat16),
        in_specs=[vmem] * 5,
        out_specs=vmem,
        scratch_shapes=[
            pltpu.VMEM((8 * count + 8, LANES), jnp.float32),
            pltpu.VMEM((LANES + 8, LANES), jnp.float32),
        ],
        compiler_params=pltpu.CompilerParams(vmem_limit_bytes=4 << 20),
        name="pack",
    )(in_hbm(masters), *[in_hbm(p.reshape(1, LANES)) for p in places])


def update_kernel(
    kept_ref, sent_ref, velocity_ref, masters_ref, velocity_out, masters_out, sums, cells
):
    count = velocity_ref.shape[0]
    flipped = flip_pixels([kept_ref[0, m] + sent_ref[0, m] for m in range(count)], cells)
    for m, slab in enumerate(flipped):
        sums[8 * m : 8 * m + 8, :] = slab
    for s in range(8):
        at = slice(s * LANES, (s + 1) * LANES)
        gradient = sums[pl.ds(s, count, stride=8), :]
        velocity = momentum * velocity_ref[:, at] + gradient
        velocity_out[:, at] = velocity
        masters_out[:, at] = masters_ref[:, at] - step_size * velocity


def update(kept, sent, velocity, masters):
    vmem = pl.BlockSpec(memory_space=pltpu.VMEM)
    return pl.pallas_call(
        update_kernel,
        out_shape=(jax.ShapeDtypeStruct(velocity.shape, jnp.float32),) * 2,
        in_specs=[vmem] * 4,
        out_specs=[vmem] * 2,
        scratch_shapes=[
            pltpu.VMEM((8 * velocity.shape[0] + 8, LANES), jnp.float32),
            pltpu.VMEM((LANES + 8, LANES), jnp.float32),
        ],
        compiler_params=pltpu.CompilerParams(vmem_limit_bytes=4 << 20),
        name="update",
    )(kept, sent, velocity, masters)


def swap(value, bit, devices):
    return lax.ppermute(value, "tx", [(i, i ^ bit) for i in range(devices)])


def on_device(
    masters,
    velocity,
    place_owner,
    place_local,
    place_row,
    place_col,
    row_taps,
    col_taps,
    mode_weights,
    target,
):
    devices = lax.axis_size("tx")
    bits = devices.bit_length() - 1
    held = pack(masters, place_owner, place_local, place_row, place_col)
    stages = []
    for b in reversed(range(bits)):
        held = jnp.concatenate([held, swap(held, 1 << b, devices)], axis=0)
        stages.append(held)
    bands = build_bands(row_taps, col_taps, stages[-4:-2])
    resid, grads = main_step(mode_weights, held, target, bands)
    for b in range(bits):
        half = grads.shape[0] // 2
        sent = swap(grads[half:], 1 << b, devices)
        if b < bits - 1:
            grads = grads[:half] + sent
    velocity_new, masters_new = update(grads, sent, velocity, masters)
    return resid, velocity_new, masters_new


def solution(mesh):
    return jax.shard_map(
        on_device,
        mesh=mesh,
        in_specs=(
            P(("groups", "tx"), None),
            P(("groups", "tx"), None),
            P(("groups", "tx"), None),
            P(("groups", "tx")),
            P(("groups", "tx")),
            P(("groups", "tx")),
            P(),
            P(),
            P(),
            P(("groups", "tx"), None),
        ),
        out_specs=(P(("groups", "tx"), None), P(("groups", "tx"), None), P(("groups", "tx"), None)),
        check_vma=False,
    )
```
